128 devices in a mesh: grp: 4 (over y), tile: 32 (over z, x, core).
Axes of the slice: x: 4, y: 4, z: 4, core: 2. Of those that a mesh axis runs over, the one named last changes fastest.
Arguments:
- screens: bfloat16 [3, 131072, 256], P(None, ('grp', 'tile')), may hold values from -4 to 4
- interp_weights: bfloat16 [3, 4, 256, 256], replicated, may hold values from -0.375 to 0.375
- footprint: int32 [32768, 3, 4], P(('grp', 'tile')), may hold values from 0 to 131071, as said below
- illumination: float32 [32768, 256], P(('grp', 'tile')), may hold values from 0.3 to 1
- cm_values: bfloat16 [896, 16, 16, 2, 128], P('tile', 'grp'), may hold values from -0.09375 to 0.09375
- cm_columns: int32 [896, 16], P('tile', 'grp'), may hold values from 0 to 255, as said below
- prev_commands: float32 [14336], P('tile'), may hold values from 0 to 5
- owner_map: int32 [14336], P('tile'), may hold values from 0 to 2, as said below
- dm_gain: float32 [3], replicated, may hold values from 0.2 to 1
Outputs:
- slopes: float32 [2, 32768], P(None, ('grp', 'tile'))
- commands: float32 [14336], P('tile')
The draws below stay inside these ranges and needn't reach their ends.
Inputs may be any that keep to these rules, and one draw needn't show every extreme that they name: `footprint`: the blocks of subaperture s lie among the 1024 blocks of the device holding s and the 256 blocks on either side of them, counted cyclically over all 131072 blocks; some subaperture reaches each end. `cm_columns`: nonzero block n names a column block from (n // 4) * 64 up to that plus 64 - 1. `owner_map`: every mirror owns some actuator.
All inputs are finite; a program needn't handle non-finite values.
Results may differ from the reference program's by a relative error of at most 0.0024.
Values may be sent and summed in bfloat16 or wider, within the bound.
No kernel may reach another device: no remote copies, remote signals or barrier semaphores. Data moves between devices by JAX's collectives and lax.ppermute only.
A program may use at most 64 MiB of HBM per device.

```python
import math
import jax
import jax.numpy as jnp
from jax import lax

SIDE = 16
P_SIZE = 256
LAYERS = 3
FOOT = 4
SUB_DEV = 256
BLK_DEV = 1024
REACH = 256
SUBS = 32768
SBLK = 131072
CBS = 128
NCB = 256
NCB_GRP = 64
RB = 16
ACT = 14336
ROWBLK = 896
NZB = 16
NZ_GRP = 4
NDM = 3


def draw_footprint(key, part):
    offsets = jax.random.randint(key, (SUBS, LAYERS, FOOT), -REACH, BLK_DEV + REACH)
    subap = jnp.arange(SUBS, dtype=jnp.int32)[:, None, None]
    owner = subap // SUB_DEV
    layer_ids = jnp.arange(LAYERS, dtype=jnp.int32)[None, :, None]
    slot_ids = jnp.arange(FOOT, dtype=jnp.int32)[None, None, :]
    forced = jnp.where(slot_ids == 0, -REACH, jnp.where(slot_ids == 1, BLK_DEV + REACH - 1, jnp.where(slot_ids == 2, -1, BLK_DEV)))
    first = (subap % SUB_DEV == 0) & (layer_ids == 0)
    offsets = jnp.where(first, forced, offsets)
    return ((owner * BLK_DEV + offsets) % SBLK).astype(jnp.int32)


def draw_cm_columns(key, part):
    picks = jax.random.randint(key, (ROWBLK, NZB), 0, NCB_GRP)
    group_ids = jnp.arange(NZB, dtype=jnp.int32)[None, :] // NZ_GRP
    columns = group_ids * NCB_GRP + picks
    rows = jnp.arange(ROWBLK, dtype=jnp.int32)[:, None]
    slots = jnp.arange(NZB, dtype=jnp.int32)[None, :]
    columns = jnp.where((rows == 0) & (slots == 0), 0, columns)
    columns = jnp.where((rows == 0) & (slots == NZB - 1), NCB - 1, columns)
    return columns.astype(jnp.int32)


def draw_owner_map(key, part):
    owners = jax.random.randint(key, (ACT,), 0, NDM)
    index = jnp.arange(ACT, dtype=jnp.int32)
    owners = jnp.where(index < NDM, index, owners)
    return owners.astype(jnp.int32)


def draw_prev_commands(key, part):
    ramp = 1.0 + 2.0 * jnp.arange(ACT, dtype=jnp.float32) / ACT
    values = jax.random.uniform(key, (ACT,), jnp.float32, 0.5, 1.5) * ramp
    return values.astype(jnp.float32)


def steps_of(own_key, dims, shards, smallest, largest):
    level, own = 1.0, jax.random.fold_in(own_key, 6)
    for position, blocks in shards:
        heights = jnp.exp(jax.random.uniform(jax.random.fold_in(own, position), (blocks,), jnp.float32, smallest / len(shards), largest / len(shards)))
        level = level * jnp.repeat(heights, dims[position] // blocks).reshape([-1 if axis == position else 1 for axis in range(len(dims))])
    return level


def gaussian(own_key, extent, deviation, bound, shards=(), kind=jnp.bfloat16):
    level = steps_of(own_key, extent, shards, -0.22, 0.18) if shards else 1.0
    result = jax.random.normal(own_key, extent, jnp.float32) * deviation * level
    return jnp.minimum(jnp.maximum(result, -bound), bound).astype(kind)


def setup_inputs(seed: int = 0) -> dict:
    seeds = jax.random.split(jax.random.key(seed), 10)
    screens = gaussian(seeds[0], (LAYERS, SBLK, P_SIZE), 0.5, 4.0, ((1, 128),))
    interp_weights = gaussian(seeds[1], (LAYERS, FOOT, P_SIZE, P_SIZE), P_SIZE ** -0.5, 0.375)
    footprint = draw_footprint(jax.random.fold_in(seeds[9], 71), 0)
    illumination = jnp.clip(jnp.exp(math.log(1.0) - 1.2039728 * jax.random.uniform(seeds[3], (SUBS, P_SIZE), jnp.float32) ** steps_of(seeds[3], (SUBS, P_SIZE), ((0, 128),), -0.2, 0.2)), 0.3, 1.0)
    cm_values = gaussian(seeds[4], (ROWBLK, NZB, RB, 2, CBS), (NZB * 2 * CBS) ** -0.5, 0.09375, ((0, 32), (1, 4)))
    cm_columns = draw_cm_columns(jax.random.fold_in(seeds[9], 71), 0)
    prev_commands = draw_prev_commands(jax.random.fold_in(seeds[9], 71), 0)
    owner_map = draw_owner_map(jax.random.fold_in(seeds[9], 71), 0)
    dm_gain = jnp.clip(jnp.exp(jax.random.uniform(seeds[8], (NDM,), jnp.float32, math.log(0.2), math.log(1.0))), 0.2, 1.0)
    return {"screens": screens, "interp_weights": interp_weights, "footprint": footprint, "illumination": illumination, "cm_values": cm_values, "cm_columns": cm_columns, "prev_commands": prev_commands, "owner_map": owner_map, "dm_gain": dm_gain}


def spectrum_tables(side):
    pixels = side * side
    index = jnp.arange(pixels, dtype=jnp.int32)
    row_ids = index // side
    col_ids = index % side
    turns = (row_ids[:, None] * row_ids[None, :] + col_ids[:, None] * col_ids[None, :]) % side
    angle = turns.astype(jnp.float32) * (2.0 * math.pi / side)
    cosine = jnp.cos(angle)
    sine = jnp.sin(angle)
    table = jnp.concatenate([jnp.concatenate([cosine, -sine], 1), jnp.concatenate([sine, cosine], 1)], 0)
    half = side // 2
    centre_v = (col_ids - side * (col_ids >= half).astype(jnp.int32)).astype(jnp.float32)
    centre_u = (row_ids - side * (row_ids >= half).astype(jnp.int32)).astype(jnp.float32)
    return table.astype(jnp.bfloat16), centre_v, centre_u


def spot_slopes(phase, illum, table, centre_v, centre_u):
    pixels = phase.shape[1]
    field = jnp.concatenate([illum * jnp.cos(phase), illum * jnp.sin(phase)], 1).astype(jnp.bfloat16)
    spectrum = jnp.dot(field, table, preferred_element_type=jnp.float32)
    real_part = spectrum[:, :pixels]
    imag_part = spectrum[:, pixels:]
    intensity = real_part * real_part + imag_part * imag_part
    total = jnp.sum(intensity, axis=1)
    slope_x = jnp.sum(intensity * centre_v[None, :], axis=1) / total
    slope_y = jnp.sum(intensity * centre_u[None, :], axis=1) / total
    return jnp.stack([slope_x, slope_y], 0)


def settle(recon, prev_commands, owner_map, dm_gain):
    mirrors = dm_gain.shape[0]
    onehot = (owner_map[:, None] == jnp.arange(mirrors, dtype=jnp.int32)[None, :]).astype(jnp.float32)
    gains = jnp.sum(onehot * dm_gain[None, :], axis=1)
    updated = prev_commands - gains * recon
    sums = jnp.sum(onehot * updated[:, None], axis=0)
    counts = jnp.sum(onehot, axis=0)
    piston = sums / counts
    return updated - jnp.sum(onehot * piston[None, :], axis=1)


def reference(screens, interp_weights, footprint, illumination, cm_values, cm_columns, prev_commands, owner_map, dm_gain):
    table, centre_v, centre_u = spectrum_tables(SIDE)
    weights_flat = interp_weights.reshape(LAYERS * FOOT * P_SIZE, P_SIZE)
    groups = SUBS // SUB_DEV

    def sense(pair):
        foot_rows, illum_rows = pair
        picked = jnp.stack([jnp.take(screens[layer], foot_rows[:, layer, :], axis=0) for layer in range(LAYERS)], axis=1)
        picked = picked.reshape(foot_rows.shape[0], LAYERS * FOOT * P_SIZE)
        phase = jnp.dot(picked, weights_flat, preferred_element_type=jnp.float32)
        return spot_slopes(phase, illum_rows, table, centre_v, centre_u)

    parts = lax.map(sense, (footprint.reshape(groups, SUB_DEV, LAYERS, FOOT), illumination.reshape(groups, SUB_DEV, P_SIZE)))
    slopes = jnp.transpose(parts, (1, 0, 2)).reshape(2, SUBS)
    slope_words = slopes.astype(jnp.bfloat16)
    blocks = slope_words.reshape(2, NCB, CBS)
    picked_blocks = jnp.take(blocks, cm_columns, axis=1)
    recon = jnp.einsum("rjics,crjs->ri", cm_values.astype(jnp.float32), picked_blocks.astype(jnp.float32)).reshape(ACT)
    commands = settle(recon, prev_commands, owner_map, dm_gain)
    return slopes, commands
```

```python
import math

import jax
import jax.numpy as jnp
import numpy as np
from jax import lax
from jax.experimental import pallas as pl
from jax.experimental.pallas import tpu as pltpu
from jax.sharding import PartitionSpec as P

SIDE = 16
DEVICES = ("grp", "tile")
LANES = 128
TILE_ROWS = 256


def from_behind(block, axis, distance):
    devices = range(lax.axis_size(axis))
    route = [((i - distance) % len(devices), i) for i in devices]
    return lax.ppermute(block, axis, route)


def transform_table(side):
    index = np.arange(side * side)
    rows, cols = index // side, index % side
    turns = (rows[:, None] * rows[None, :] + cols[:, None] * cols[None, :]) % side
    angle = turns.astype(np.float32) * np.float32(2.0 * math.pi / side)
    cosine, sine = np.cos(angle), np.sin(angle)
    table = np.concatenate(
        [np.concatenate([cosine, -sine], 1), np.concatenate([sine, cosine], 1)], 0
    )
    return jnp.asarray(table.T.astype(jnp.bfloat16))


def pick(offsets, block, blocks):
    rows = offsets.shape[0]
    lane = lax.broadcasted_iota(jnp.int32, (rows, TILE_ROWS), 1).astype(jnp.float32)
    hit = jnp.where(lane == offsets - float(block * TILE_ROWS), 1.0, 0.0).astype(jnp.bfloat16)
    return jnp.dot(hit, blocks, preferred_element_type=jnp.float32)


def offsets_of(foot_rows, start, total):
    away = foot_rows - start
    away = jnp.where(away < -(total // 2), away + total, away)
    away = jnp.where(away >= total // 2, away - total, away)
    away = away.astype(jnp.float32)
    foot, subs = away.shape
    filled = jnp.concatenate([away, jnp.zeros((8 - foot, subs), jnp.float32)], 0)
    return filled.T


def sense_own(start_ref, foot_ref, screens_ref, weights_ref, phase_ref, *, total):
    offsets = offsets_of(foot_ref[0], start_ref[0], total)
    foot = foot_ref.shape[1]
    blocks = screens_ref.shape[1] // TILE_ROWS
    phase = jnp.zeros(phase_ref.shape, jnp.float32)
    for k in range(foot):
        column = jnp.broadcast_to(offsets[:, k : k + 1], (offsets.shape[0], TILE_ROWS))
        picked = None
        for b in range(blocks):
            part = pick(column, b, screens_ref[0, b * TILE_ROWS : (b + 1) * TILE_ROWS, :])
            picked = part if picked is None else picked + part
        phase = phase + jnp.dot(
            picked.astype(jnp.bfloat16), weights_ref[0, k], preferred_element_type=jnp.float32
        )

    @pl.when(pl.program_id(0) == 0)
    def _():
        phase_ref[...] = phase

    @pl.when(pl.program_id(0) != 0)
    def _():
        phase_ref[...] = phase_ref[...] + phase


def sense_rest(
    start_ref, foot_ref, before_ref, after_ref, weights_ref, phase_ref, illum_ref, table_ref,
    slopes_ref, words_ref, *, total, own
):
    layers, foot, subs = foot_ref.shape
    phase = phase_ref[...]
    for layer in range(layers):
        offsets = offsets_of(foot_ref[layer], start_ref[0], total)
        for k in range(foot):
            column = jnp.broadcast_to(offsets[:, k : k + 1], (subs, TILE_ROWS))
            picked = pick(column, -1, before_ref[layer]) + pick(column, own, after_ref[layer])
            phase = phase + jnp.dot(
                picked.astype(jnp.bfloat16),
                weights_ref[layer, k],
                preferred_element_type=jnp.float32,
            )
    pixels = phase.shape[1]
    phase = phase.T
    illum = illum_ref[...].T
    field = jnp.concatenate([illum * jnp.cos(phase), illum * jnp.sin(phase)], 0)
    spectrum = jnp.dot(
        table_ref[...], field.astype(jnp.bfloat16), preferred_element_type=jnp.float32
    )
    real_part = spectrum[:pixels]
    imag_part = spectrum[pixels:]
    intensity = real_part * real_part + imag_part * imag_part
    row = lax.broadcasted_iota(jnp.int32, intensity.shape, 0)
    cv = row % SIDE
    cu = row // SIDE
    cv = (cv - SIDE * (cv >= SIDE // 2).astype(jnp.int32)).astype(jnp.float32)
    cu = (cu - SIDE * (cu >= SIDE // 2).astype(jnp.int32)).astype(jnp.float32)
    count = jnp.sum(intensity, axis=0, keepdims=True)
    slope_x = jnp.sum(intensity * cv, axis=0, keepdims=True) / count
    slope_y = jnp.sum(intensity * cu, axis=0, keepdims=True) / count
    slopes = jnp.concatenate([slope_x, slope_y], 0)
    slopes_ref[...] = slopes
    words = slopes.astype(jnp.bfloat16).astype(jnp.float32)
    rows = [words[:, h * LANES : (h + 1) * LANES] for h in range(subs // LANES)]
    words_ref[...] = jnp.broadcast_to(jnp.concatenate(rows, 0)[None], words_ref.shape)


def reconstruct(words_ref, cm_ref, rows_ref, owner_ref, prev_ref, gain_ref, sent_ref, *, share):
    words = words_ref[...].astype(jnp.bfloat16)
    positions = cm_ref.shape[0]
    width = cm_ref.shape[1]
    row = lax.broadcasted_iota(jnp.int32, (words.shape[0], width), 0)
    total = jnp.zeros((words.shape[0], width), jnp.float32)
    for n in range(positions):
        for c in range(2):
            product = lax.dot_general(
                words,
                cm_ref[n, :, c * LANES : (c + 1) * LANES],
                (((1,), (1,)), ((), ())),
                preferred_element_type=jnp.float32,
            )
            total = total + jnp.where(row == rows_ref[n : n + 1, :] * 2 + c, product, 0.0)
    recon = jnp.sum(total, axis=0, keepdims=True)
    owner = owner_ref[...]
    lane = lax.broadcasted_iota(jnp.int32, (1, width), 1)
    mirrors = gain_ref.shape[0]
    line = recon
    for m in range(mirrors):
        mine = owner == m
        part = jnp.where(mine, prev_ref[...] * share - gain_ref[m] * recon, 0.0)
        line = jnp.where(lane == width - 2 * mirrors + m, jnp.sum(part, axis=1, keepdims=True), line)
        held = jnp.where(mine, share, 0.0)
        line = jnp.where(lane == width - mirrors + m, jnp.sum(held, axis=1, keepdims=True), line)
    rows = [line[:, i * LANES : (i + 1) * LANES] for i in range(width // LANES)]
    sent_ref[...] = jnp.broadcast_to(jnp.concatenate(rows, 0)[None], sent_ref.shape)


def settle(tile_ref, got_ref, owner_ref, prev_ref, gain_ref, commands_ref, *, groups):
    tiles = got_ref.shape[0] // groups
    recon = got_ref[tile_ref[0]]
    for g in range(1, groups):
        recon = recon + got_ref[g * tiles + tile_ref[0]]
    sums = jnp.sum(got_ref[...], axis=0)
    last = sums[sums.shape[0] - 1 :, :]
    lane = lax.broadcasted_iota(jnp.int32, last.shape, 1)
    owner = owner_ref[...]
    mirrors = gain_ref.shape[0]
    gains = jnp.zeros(owner.shape, jnp.float32)
    piston = jnp.zeros(owner.shape, jnp.float32)
    for m in range(mirrors):
        mine = owner == m
        total = jnp.sum(jnp.where(lane == LANES - 2 * mirrors + m, last, 0.0), axis=1, keepdims=True)
        count = jnp.sum(jnp.where(lane == LANES - mirrors + m, last, 0.0), axis=1, keepdims=True)
        gains = jnp.where(mine, gain_ref[m], gains)
        piston = jnp.where(mine, total / count, piston)
    commands_ref[...] = prev_ref[...] - gains * recon - piston


def on_device(
    screens,
    interp_weights,
    footprint,
    illumination,
    cm_values,
    cm_columns,
    prev_commands,
    owner_map,
    dm_gain,
):
    layers, blk_dev, pixels = screens.shape
    subs, _, foot = footprint.shape
    groups, tiles = lax.axis_size("grp"), lax.axis_size("tile")
    total = blk_dev * groups * tiles
    here = lax.axis_index(DEVICES)
    reach = TILE_ROWS
    smem = pl.BlockSpec(memory_space=pltpu.SMEM)
    limit = pltpu.CompilerParams(vmem_limit_bytes=24 * 2**20)

    before = from_behind(screens[:, blk_dev - reach :], DEVICES, 1)
    after = from_behind(screens[:, :reach], DEVICES, -1)

    start = (here * blk_dev).astype(jnp.int32).reshape(1)
    foot_rows = jnp.transpose(footprint, (1, 2, 0))
    phase = pl.pallas_call(
        lambda *refs: sense_own(*refs, total=total),
        grid=(layers,),
        in_specs=[
            smem,
            pl.BlockSpec((1, foot, subs), lambda i: (i, 0, 0)),
            pl.BlockSpec((1, blk_dev, pixels), lambda i: (i, 0, 0)),
            pl.BlockSpec((1, foot, pixels, pixels), lambda i: (i, 0, 0, 0)),
        ],
        out_specs=pl.BlockSpec((subs, pixels), lambda i: (0, 0)),
        out_shape=jax.ShapeDtypeStruct((subs, pixels), jnp.float32),
        compiler_params=limit,
        name="sense_own",
    )(start, foot_rows, screens, interp_weights)

    slopes, words = pl.pallas_call(
        lambda *refs: sense_rest(*refs, total=total, own=blk_dev // TILE_ROWS),
        in_specs=[smem] + [pl.BlockSpec(memory_space=pltpu.VMEM)] * 7,
        out_shape=(
            jax.ShapeDtypeStruct((2, subs), jnp.float32),
            jax.ShapeDtypeStruct((tiles, 2 * subs // LANES, LANES), jnp.float32),
        ),
        compiler_params=limit,
        name="sense_rest",
    )(start, foot_rows, before, after, interp_weights, phase, illumination, transform_table(SIDE))

    rowblk, positions, rb, comps, cbs = cm_values.shape
    acts = rowblk * rb
    mirrors = dm_gain.shape[0]
    width = -(-(acts + 2 * mirrors) // LANES) * LANES
    pad = width - acts
    cm = jnp.transpose(cm_values, (1, 0, 2, 3, 4)).reshape(positions, acts, comps * cbs)
    cm = jnp.pad(cm, ((0, 0), (0, pad), (0, 0)))
    column_base = lax.axis_index("grp") * (tiles * subs // cbs)
    rows = jnp.repeat((cm_columns - column_base).T, rb, axis=1)
    rows = jnp.pad(rows, ((0, 0), (0, pad)), constant_values=-1)
    owner = jnp.pad(owner_map, (0, pad), constant_values=-1)
    prev = jnp.pad(prev_commands, (0, pad))

    gathered = lax.all_to_all(words, "tile", 0, 0).reshape(-1, LANES)
    lines = width // LANES
    sent = pl.pallas_call(
        lambda *refs: reconstruct(*refs, share=1.0 / groups),
        in_specs=[pl.BlockSpec(memory_space=pltpu.VMEM)] * 5 + [smem],
        out_shape=jax.ShapeDtypeStruct((groups * tiles, lines, LANES), jnp.float32),
        compiler_params=limit,
        name="reconstruct",
    )(gathered, cm, rows, owner.reshape(1, width), prev.reshape(1, width), dm_gain)
    got = lax.all_to_all(sent, DEVICES, 0, 0)
    tile = lax.axis_index("tile").astype(jnp.int32).reshape(1)
    commands = pl.pallas_call(
        lambda *refs: settle(*refs, groups=groups),
        in_specs=[smem] + [pl.BlockSpec(memory_space=pltpu.VMEM)] * 3 + [smem],
        out_shape=jax.ShapeDtypeStruct((lines, LANES), jnp.float32),
        compiler_params=limit,
        name="settle",
    )(tile, got, owner.reshape(lines, LANES), prev.reshape(lines, LANES), dm_gain)
    return (slopes, commands.reshape(width)[:acts])


def solution(mesh):
    in_specs = (
        P(None, ("grp", "tile"), None),
        P(),
        P(("grp", "tile"), None, None),
        P(("grp", "tile"), None),
        P("tile", "grp", None, None, None),
        P("tile", "grp"),
        P("tile"),
        P("tile"),
        P(),
    )
    out_specs = (P(None, ("grp", "tile")), P("tile"))
    return jax.shard_map(
        on_device, mesh=mesh, in_specs=in_specs, out_specs=out_specs, check_vma=False
    )
```

```python
import math

import jax
import jax.numpy as jnp
import numpy as np
from jax import lax
from jax.experimental import pallas as pl
from jax.experimental.pallas import tpu as pltpu
from jax.sharding import PartitionSpec as P

SIDE = 16
DEVICES = ("grp", "tile")
LANES = 128
EDGE = 256


def from_behind(block, axis, distance):
    devices = range(lax.axis_size(axis))
    route = [((i - distance) % len(devices), i) for i in devices]
    return lax.ppermute(block, axis, route)


def transform_table(side):
    index = np.arange(side * side)
    rows, cols = index // side, index % side
    turns = (rows[:, None] * rows[None, :] + cols[:, None] * cols[None, :]) % side
    angle = turns.astype(np.float32) * np.float32(2.0 * math.pi / side)
    cosine, sine = np.cos(angle), np.sin(angle)
    table = np.concatenate(
        [np.concatenate([cosine, -sine], 1), np.concatenate([sine, cosine], 1)], 0
    )
    return jnp.asarray(table.T.astype(jnp.bfloat16))


def sine_cosine(angle):
    turns = jnp.floor(angle * np.float32(2.0 / math.pi) + 0.5)
    rest = angle - turns * np.float32(1.5703125)
    rest = rest - turns * np.float32(4.837512969970703125e-4)
    rest = rest - turns * np.float32(7.54978995489188216e-8)
    sq = rest * rest
    sine = (np.float32(-1.9515295891e-4) * sq + np.float32(8.3321608736e-3)) * sq
    sine = (sine - np.float32(1.6666654611e-1)) * sq * rest + rest
    cosine = (np.float32(2.443315711809948e-5) * sq - np.float32(1.388731625493765e-3)) * sq
    cosine = (cosine + np.float32(4.166664568298827e-2)) * sq * sq - np.float32(0.5) * sq + 1.0
    quarter = turns.astype(jnp.int32)
    odd = (quarter & 1) == 1
    out_sine = jnp.where(odd, cosine, sine)
    out_cosine = jnp.where(odd, sine, cosine)
    out_sine = jnp.where((quarter & 2) == 2, -out_sine, out_sine)
    out_cosine = jnp.where(((quarter + 1) & 2) == 2, -out_cosine, out_cosine)
    return out_sine, out_cosine


def offsets_of(foot_rows, start, total):
    away = foot_rows - start
    away = jnp.where(away < -(total // 2), away + total, away)
    away = jnp.where(away >= total // 2, away - total, away)
    away = away.astype(jnp.float32)
    foot, subs = away.shape
    filled = jnp.concatenate([away, jnp.zeros((8 - foot, subs), jnp.float32)], 0)
    return filled.T.astype(jnp.int32)


def hits(column, first, count):
    column = jnp.broadcast_to(column, (column.shape[0], LANES)).astype(jnp.int16)
    lane = lax.broadcasted_iota(jnp.int16, column.shape, 1)
    one, zero = jnp.bfloat16(1), jnp.bfloat16(0)
    parts = [
        jnp.where(lane == column - jnp.int16(first + b), one, zero)
        for b in range(0, count, LANES)
    ]
    return jnp.concatenate(parts, 1)


def edges(screens_ref, tail_ref, head_ref, sems):
    layers, blocks, _ = screens_ref.shape
    copies = []
    for layer in range(layers):
        tail = screens_ref.at[layer, pl.ds(blocks - EDGE, EDGE)]
        head = screens_ref.at[layer, pl.ds(0, EDGE)]
        copies.append(pltpu.make_async_copy(tail, tail_ref.at[layer], sems.at[2 * layer]))
        copies.append(pltpu.make_async_copy(head, head_ref.at[layer], sems.at[2 * layer + 1]))
    for copy in copies:
        copy.start()
    for copy in copies:
        copy.wait()


def sense_own(
    start_ref, base_ref, gain_ref, foot_ref, cols_ref, owner_ref, prev_ref, screens_ref,
    weights_ref, phase_ref, spot_ref, state_ref, *, total
):
    layers, foot, _ = foot_ref.shape
    blocks, pixels = screens_ref.shape[1:]
    phase = None
    for layer in range(layers):
        offsets = offsets_of(foot_ref[layer], start_ref[0], total)
        picked = [
            jnp.dot(
                hits(offsets[:, k : k + 1], 0, blocks),
                screens_ref[layer],
                preferred_element_type=jnp.float32,
            ).astype(jnp.bfloat16)
            for k in range(foot)
        ]
        part = jnp.dot(
            jnp.concatenate(picked, 1),
            weights_ref[layer].reshape(foot * pixels, pixels),
            preferred_element_type=jnp.float32,
        )
        phase = part if phase is None else phase + part
    phase_ref[...] = phase

    positions, rowblk = cols_ref.shape
    acts = owner_ref.shape[1]
    rb = acts // rowblk
    cols = (cols_ref[...] - base_ref[0]).astype(jnp.float32)
    lane = lax.broadcasted_iota(jnp.int32, (positions, LANES), 1)
    place = lax.broadcasted_iota(jnp.int32, (positions, LANES), 0)
    spread = jnp.where(lane // (2 * rb) == place, 1.0, 0.0)
    cols = lax.dot_general(
        cols, spread, (((0,), (0,)), ((), ())), preferred_element_type=jnp.float32
    )
    comp = lax.broadcasted_iota(jnp.int32, cols.shape, 1) % 2
    spot = cols.astype(jnp.int32) * 2 + comp
    height = spot_ref.shape[0]
    spot_ref[...] = jnp.concatenate(
        [spot, jnp.full((height - rowblk, LANES), -1, jnp.int32)], 0
    )
    lines = height * rb // LANES
    owner = owner_ref[...]
    gain = jnp.zeros(owner.shape, jnp.float32)
    for m in range(gain_ref.shape[0]):
        gain = jnp.where(owner == m, gain_ref[m], gain)
    missing = lines * LANES - acts
    rows = []
    for values, fill in ((owner.astype(jnp.float32), -1.0), (prev_ref[...], 0.0), (gain, 0.0)):
        values = jnp.concatenate([values, jnp.full((1, missing), fill, jnp.float32)], 1)
        rows += [values[:, i * LANES : (i + 1) * LANES] for i in range(lines)]
    state_ref[...] = jnp.concatenate(rows, 0)


def sense_rest(
    start_ref, foot_ref, before_ref, after_ref, weights_ref, phase_ref, illum_ref, table_ref,
    slopes_ref, words_ref, *, total, own
):
    layers, foot, subs = foot_ref.shape
    pixels = phase_ref.shape[1]
    phase = phase_ref[...]
    for layer in range(layers):
        offsets = offsets_of(foot_ref[layer], start_ref[0], total)
        blocks = jnp.concatenate([before_ref[layer], after_ref[layer]], 0)
        picked = []
        for k in range(foot):
            column = offsets[:, k : k + 1]
            found = jnp.concatenate([hits(column, -EDGE, EDGE), hits(column, own, EDGE)], 1)
            rows = jnp.dot(found, blocks, preferred_element_type=jnp.float32)
            picked.append(rows.astype(jnp.bfloat16))
        phase = phase + jnp.dot(
            jnp.concatenate(picked, 1),
            weights_ref[layer].reshape(foot * pixels, pixels),
            preferred_element_type=jnp.float32,
        )
    phase = phase.T
    illum = illum_ref[...].T
    sine, cosine = sine_cosine(phase)
    field = jnp.concatenate([illum * cosine, illum * sine], 0).astype(jnp.bfloat16)
    spectrum = jnp.dot(table_ref[...], field, preferred_element_type=jnp.float32)
    real_part = spectrum[:pixels]
    imag_part = spectrum[pixels:]
    intensity = real_part * real_part + imag_part * imag_part
    row = lax.broadcasted_iota(jnp.int32, intensity.shape, 0)
    cv = row % SIDE
    cu = row // SIDE
    cv = (cv - SIDE * (cv >= SIDE // 2).astype(jnp.int32)).astype(jnp.float32)
    cu = (cu - SIDE * (cu >= SIDE // 2).astype(jnp.int32)).astype(jnp.float32)
    whole = jnp.sum(intensity, axis=0, keepdims=True)
    slope_x = jnp.sum(intensity * cv, axis=0, keepdims=True) / whole
    slope_y = jnp.sum(intensity * cu, axis=0, keepdims=True) / whole
    slopes = jnp.concatenate([slope_x, slope_y], 0)
    slopes_ref[...] = slopes
    words = slopes.astype(jnp.bfloat16).astype(jnp.float32)
    words = [words[:, h * LANES : (h + 1) * LANES] for h in range(subs // LANES)]
    words_ref[...] = jnp.broadcast_to(jnp.concatenate(words, 0)[None], words_ref.shape)


def reconstruct(words_ref, cm_ref, spot_ref, state_ref, sent_ref, *, rb, share, mirrors):
    words = words_ref[...].astype(jnp.bfloat16)
    rowblk = cm_ref.shape[0] // LANES
    row = lax.broadcasted_iota(jnp.int32, (words.shape[0], LANES), 0)
    parts = []
    for i in range(rowblk):
        product = lax.dot_general(
            words,
            cm_ref[i * LANES : (i + 1) * LANES, :],
            (((1,), (1,)), ((), ())),
            preferred_element_type=jnp.float32,
        )
        chosen = jnp.where(row == spot_ref[i : i + 1, :], product, 0.0)
        parts.append(jnp.sum(chosen, axis=0, keepdims=True))
    height = spot_ref.shape[0]
    if height > rowblk:
        parts.append(jnp.zeros((height - rowblk, LANES), jnp.float32))
    parts = jnp.concatenate(parts, 0)
    source = lax.broadcasted_iota(jnp.int32, (LANES, LANES), 0)
    lane = lax.broadcasted_iota(jnp.int32, (LANES, LANES), 1)
    fold = jnp.where((source % (2 * rb)) // 2 == lane % rb, 1.0, 0.0)
    spread = jnp.dot(
        parts, fold, preferred_element_type=jnp.float32, precision=lax.Precision.HIGHEST
    )
    per = LANES // rb
    block = lax.broadcasted_iota(jnp.int32, spread.shape, 0)
    lane = lax.broadcasted_iota(jnp.int32, spread.shape, 1)
    spread = jnp.where(lane // rb == block % per, spread, 0.0)
    lines = height // per
    recon = jnp.sum(spread.reshape(lines, per, LANES), axis=1)
    owner = state_ref[:lines]
    updated = state_ref[lines : 2 * lines] * share - state_ref[2 * lines :] * recon
    row = lax.broadcasted_iota(jnp.int32, recon.shape, 0)
    lane = lax.broadcasted_iota(jnp.int32, recon.shape, 1)
    last = row == lines - 1
    for m in range(mirrors):
        mine = owner == float(m)
        recon = jnp.where(
            last & (lane == LANES - 2 * mirrors + m),
            jnp.sum(jnp.where(mine, updated, 0.0), keepdims=True),
            recon,
        )
        recon = jnp.where(
            last & (lane == LANES - mirrors + m),
            jnp.sum(jnp.where(mine, share, 0.0), keepdims=True),
            recon,
        )
    sent_ref[...] = jnp.broadcast_to(recon[None], sent_ref.shape)


def settle(tile_ref, got_ref, state_ref, commands_ref, *, groups, mirrors):
    count, lines, _ = got_ref.shape
    tiles = count // groups
    recon = got_ref[tile_ref[0]]
    for g in range(1, groups):
        recon = recon + got_ref[g * tiles + tile_ref[0]]
    last = jnp.sum(got_ref[:, lines - 1, :], axis=0, keepdims=True)
    lane = lax.broadcasted_iota(jnp.int32, last.shape, 1)

    def entry(at):
        return jnp.sum(jnp.where(lane == at, last, 0.0), axis=1, keepdims=True)

    owner = state_ref[:lines]
    piston = jnp.zeros(owner.shape, jnp.float32)
    for m in range(mirrors):
        mean = entry(LANES - 2 * mirrors + m) / entry(LANES - mirrors + m)
        piston = jnp.where(owner == float(m), mean, piston)
    commands = state_ref[lines : 2 * lines] - state_ref[2 * lines :] * recon - piston
    acts = commands_ref.shape[0]
    for i in range(lines):
        some = min(LANES, acts - i * LANES)
        commands_ref[i * LANES : i * LANES + some] = commands[i, :some]


def on_device(
    screens,
    interp_weights,
    footprint,
    illumination,
    cm_values,
    cm_columns,
    prev_commands,
    owner_map,
    dm_gain,
):
    layers, blk_dev, pixels = screens.shape
    subs, _, foot = footprint.shape
    groups, tiles = lax.axis_size("grp"), lax.axis_size("tile")
    total = blk_dev * groups * tiles
    rowblk, positions, rb, comps, cbs = cm_values.shape
    acts = rowblk * rb
    mirrors = dm_gain.shape[0]
    height = -(-(acts + 2 * mirrors) // LANES) * LANES // rb
    lines = height * rb // LANES
    smem = pl.BlockSpec(memory_space=pltpu.SMEM)
    vmem = pl.BlockSpec(memory_space=pltpu.VMEM)
    limit = pltpu.CompilerParams(vmem_limit_bytes=24 * 2**20)
    f32 = jnp.float32

    edge = jax.ShapeDtypeStruct((layers, EDGE, pixels), screens.dtype)
    tail, head = pl.pallas_call(
        edges,
        in_specs=[pl.BlockSpec(memory_space=pltpu.HBM)],
        out_specs=[vmem, vmem],
        out_shape=[edge, edge],
        scratch_shapes=[pltpu.SemaphoreType.DMA((2 * layers,))],
        compiler_params=limit,
        name="edges",
    )(pltpu.with_memory_space_constraint(screens, pltpu.HBM))
    before = from_behind(tail, DEVICES, 1)
    after = from_behind(head, DEVICES, -1)

    start = (lax.axis_index(DEVICES) * blk_dev).astype(jnp.int32).reshape(1)
    base = (lax.axis_index("grp") * (tiles * subs // cbs)).astype(jnp.int32).reshape(1)
    foot_rows = jnp.transpose(footprint, (1, 2, 0))
    phase, spot, state = pl.pallas_call(
        lambda *refs: sense_own(*refs, total=total),
        in_specs=[smem] * 3 + [vmem] * 6,
        out_shape=(
            jax.ShapeDtypeStruct((subs, pixels), f32),
            jax.ShapeDtypeStruct((height, LANES), jnp.int32),
            jax.ShapeDtypeStruct((3 * lines, LANES), f32),
        ),
        compiler_params=limit,
        name="sense_own",
    )(
        start, base, dm_gain, foot_rows, cm_columns.T, owner_map.reshape(1, acts),
        prev_commands.reshape(1, acts), screens, interp_weights,
    )
    slopes, words = pl.pallas_call(
        lambda *refs: sense_rest(*refs, total=total, own=blk_dev),
        in_specs=[smem] + [vmem] * 7,
        out_shape=(
            jax.ShapeDtypeStruct((2, subs), f32),
            jax.ShapeDtypeStruct((tiles, 2 * subs // LANES, LANES), f32),
        ),
        compiler_params=limit,
        name="sense_rest",
    )(start, foot_rows, before, after, interp_weights, phase, illumination, transform_table(SIDE))

    cm = cm_values.reshape(rowblk * positions * rb * comps, cbs)
    gathered = lax.all_to_all(words, "tile", 0, 0).reshape(-1, LANES)
    sent = pl.pallas_call(
        lambda *refs: reconstruct(*refs, rb=rb, share=1.0 / groups, mirrors=mirrors),
        in_specs=[vmem] * 4,
        out_shape=jax.ShapeDtypeStruct((groups * tiles, lines, LANES), f32),
        compiler_params=limit,
        name="reconstruct",
    )(gathered, cm, spot, state)
    got = lax.all_to_all(sent, DEVICES, 0, 0)
    tile = lax.axis_index("tile").astype(jnp.int32).reshape(1)
    commands = pl.pallas_call(
        lambda *refs: settle(*refs, groups=groups, mirrors=mirrors),
        in_specs=[smem, vmem, vmem],
        out_shape=jax.ShapeDtypeStruct((acts,), f32),
        compiler_params=limit,
        name="settle",
    )(tile, got, state)
    return (slopes, commands)


def solution(mesh):
    in_specs = (
        P(None, ("grp", "tile"), None),
        P(),
        P(("grp", "tile"), None, None),
        P(("grp", "tile"), None),
        P("tile", "grp", None, None, None),
        P("tile", "grp"),
        P("tile"),
        P("tile"),
        P(),
    )
    out_specs = (P(None, ("grp", "tile")), P("tile"))
    return jax.shard_map(
        on_device, mesh=mesh, in_specs=in_specs, out_specs=out_specs, check_vma=False
    )
```

```python
import math

import jax
import jax.numpy as jnp
import numpy as np
from jax import lax
from jax.experimental import pallas as pl
from jax.experimental.pallas import tpu as pltpu
from jax.sharding import PartitionSpec as P

SIDE = 16
DEVICES = ("grp", "tile")
LANES = 128
EDGE = 256


def swap(block, step):
    count = lax.axis_size(DEVICES)
    route = [(i, (i + step if i % 2 else i - step) % count) for i in range(count)]
    return lax.ppermute(block, DEVICES, route)


def transform_table(side):
    index = np.arange(side * side)
    rows, cols = index // side, index % side
    turns = (rows[:, None] * rows[None, :] + cols[:, None] * cols[None, :]) % side
    angle = turns.astype(np.float32) * np.float32(2.0 * math.pi / side)
    cosine, sine = np.cos(angle), np.sin(angle)
    table = np.concatenate(
        [np.concatenate([cosine, -sine], 1), np.concatenate([sine, cosine], 1)], 0
    )
    return jnp.asarray(table.T.astype(jnp.bfloat16))


def sine_cosine(angle):
    turns = jnp.floor(angle * np.float32(2.0 / math.pi) + 0.5)
    rest = angle - turns * np.float32(1.5703125)
    rest = rest - turns * np.float32(4.837512969970703125e-4)
    rest = rest - turns * np.float32(7.54978995489188216e-8)
    sq = rest * rest
    sine = (np.float32(-1.9515295891e-4) * sq + np.float32(8.3321608736e-3)) * sq
    sine = (sine - np.float32(1.6666654611e-1)) * sq * rest + rest
    cosine = (np.float32(2.443315711809948e-5) * sq - np.float32(1.388731625493765e-3)) * sq
    cosine = (cosine + np.float32(4.166664568298827e-2)) * sq * sq - np.float32(0.5) * sq + 1.0
    quarter = turns.astype(jnp.int32)
    odd = (quarter & 1) == 1
    out_sine = jnp.where(odd, cosine, sine)
    out_cosine = jnp.where(odd, sine, cosine)
    out_sine = jnp.where((quarter & 2) == 2, -out_sine, out_sine)
    out_cosine = jnp.where(((quarter + 1) & 2) == 2, -out_cosine, out_cosine)
    return out_sine, out_cosine


def offsets_of(foot_rows, start, total):
    away = foot_rows - start
    away = jnp.where(away < -(total // 2), away + total, away)
    away = jnp.where(away >= total // 2, away - total, away)
    away = away.astype(jnp.float32)
    foot, subs = away.shape
    filled = jnp.concatenate([away, jnp.zeros((8 - foot, subs), jnp.float32)], 0)
    return filled.T.astype(jnp.int32)


def hits(column, first, count):
    column = jnp.broadcast_to(column, (column.shape[0], LANES)).astype(jnp.int16)
    lane = lax.broadcasted_iota(jnp.int16, column.shape, 1)
    one, zero = jnp.bfloat16(1), jnp.bfloat16(0)
    parts = [
        jnp.where(lane == column - jnp.int16(first + b), one, zero)
        for b in range(0, count, LANES)
    ]
    return jnp.concatenate(parts, 1)


def edges(odd_ref, screens_ref, outer_ref, inner_ref, sems):
    layers, blocks, _ = screens_ref.shape
    last = (blocks // EDGE - 1) * EDGE
    outer = pl.multiple_of(odd_ref[0] * last, EDGE)
    inner = pl.multiple_of((1 - odd_ref[0]) * last, EDGE)
    copies = []
    for layer in range(layers):
        for first, ref, sem in ((outer, outer_ref, 0), (inner, inner_ref, 1)):
            block = screens_ref.at[layer, pl.ds(first, EDGE)]
            copies.append(
                pltpu.make_async_copy(block, ref.at[layer], sems.at[2 * layer + sem])
            )
    for copy in copies:
        copy.start()
    for copy in copies:
        copy.wait()


def sense_own(
    start_ref, first_ref, base_ref, gain_ref, foot_ref, cols_ref, owner_ref, prev_ref,
    screens_ref, inner_ref, weights_ref, phase_ref, spot_ref, state_ref, *, total
):
    layers, foot, _ = foot_ref.shape
    blocks, pixels = screens_ref.shape[1:]
    phase = None
    for layer in range(layers):
        offsets = offsets_of(foot_ref[layer], start_ref[0], total)
        picked = []
        for k in range(foot):
            column = offsets[:, k : k + 1]
            rows = jnp.dot(
                hits(column, 0, blocks), screens_ref[layer], preferred_element_type=jnp.float32
            )
            rows = rows + jnp.dot(
                hits(column - first_ref[0], 0, EDGE),
                inner_ref[layer],
                preferred_element_type=jnp.float32,
            )
            picked.append(rows.astype(jnp.bfloat16))
        part = jnp.dot(
            jnp.concatenate(picked, 1),
            weights_ref[layer].reshape(foot * pixels, pixels),
            preferred_element_type=jnp.float32,
        )
        phase = part if phase is None else phase + part
    phase_ref[...] = phase

    positions, rowblk = cols_ref.shape
    acts = owner_ref.shape[1]
    rb = acts // rowblk
    cols = (cols_ref[...] - base_ref[0]).astype(jnp.float32)
    lane = lax.broadcasted_iota(jnp.int32, (positions, LANES), 1)
    place = lax.broadcasted_iota(jnp.int32, (positions, LANES), 0)
    spread = jnp.where(lane // (2 * rb) == place, 1.0, 0.0)
    cols = lax.dot_general(
        cols, spread, (((0,), (0,)), ((), ())), preferred_element_type=jnp.float32
    )
    comp = lax.broadcasted_iota(jnp.int32, cols.shape, 1) % 2
    spot = cols.astype(jnp.int32) * 2 + comp
    height = spot_ref.shape[0]
    spot_ref[...] = jnp.concatenate(
        [spot, jnp.full((height - rowblk, LANES), -1, jnp.int32)], 0
    )
    lines = height * rb // LANES
    owner = owner_ref[...]
    gain = jnp.zeros(owner.shape, jnp.float32)
    for m in range(gain_ref.shape[0]):
        gain = jnp.where(owner == m, gain_ref[m], gain)
    missing = lines * LANES - acts
    rows = []
    for values, fill in ((owner.astype(jnp.float32), -1.0), (prev_ref[...], 0.0), (gain, 0.0)):
        values = jnp.concatenate([values, jnp.full((1, missing), fill, jnp.float32)], 1)
        rows += [values[:, i * LANES : (i + 1) * LANES] for i in range(lines)]
    state_ref[...] = jnp.concatenate(rows, 0)


def sense_rest(
    start_ref, first_ref, foot_ref, outer_ref, weights_ref, phase_ref, illum_ref, table_ref,
    slopes_ref, words_ref, *, total
):
    layers, foot, subs = foot_ref.shape
    pixels = phase_ref.shape[1]
    phase = phase_ref[...]
    for layer in range(layers):
        offsets = offsets_of(foot_ref[layer], start_ref[0], total)
        picked = []
        for k in range(foot):
            found = hits(offsets[:, k : k + 1] - first_ref[0], 0, EDGE)
            rows = jnp.dot(found, outer_ref[layer], preferred_element_type=jnp.float32)
            picked.append(rows.astype(jnp.bfloat16))
        phase = phase + jnp.dot(
            jnp.concatenate(picked, 1),
            weights_ref[layer].reshape(foot * pixels, pixels),
            preferred_element_type=jnp.float32,
        )
    phase = phase.T
    illum = illum_ref[...].T
    sine, cosine = sine_cosine(phase)
    field = jnp.concatenate([illum * cosine, illum * sine], 0).astype(jnp.bfloat16)
    spectrum = jnp.dot(table_ref[...], field, preferred_element_type=jnp.float32)
    real_part = spectrum[:pixels]
    imag_part = spectrum[pixels:]
    intensity = real_part * real_part + imag_part * imag_part
    row = lax.broadcasted_iota(jnp.int32, intensity.shape, 0)
    cv = row % SIDE
    cu = row // SIDE
    cv = (cv - SIDE * (cv >= SIDE // 2).astype(jnp.int32)).astype(jnp.float32)
    cu = (cu - SIDE * (cu >= SIDE // 2).astype(jnp.int32)).astype(jnp.float32)
    whole = jnp.sum(intensity, axis=0, keepdims=True)
    slope_x = jnp.sum(intensity * cv, axis=0, keepdims=True) / whole
    slope_y = jnp.sum(intensity * cu, axis=0, keepdims=True) / whole
    slopes = jnp.concatenate([slope_x, slope_y], 0)
    slopes_ref[...] = slopes
    words = slopes.astype(jnp.bfloat16).astype(jnp.float32)
    words = [words[:, h * LANES : (h + 1) * LANES] for h in range(subs // LANES)]
    words_ref[...] = jnp.broadcast_to(jnp.concatenate(words, 0)[None], words_ref.shape)


def reconstruct(words_ref, cm_ref, spot_ref, state_ref, sent_ref, *, rb, share, mirrors):
    words = words_ref[...].astype(jnp.bfloat16)
    rowblk = cm_ref.shape[0] // LANES
    row = lax.broadcasted_iota(jnp.int32, (words.shape[0], LANES), 0)
    parts = []
    for i in range(rowblk):
        product = lax.dot_general(
            words,
            cm_ref[i * LANES : (i + 1) * LANES, :],
            (((1,), (1,)), ((), ())),
            preferred_element_type=jnp.float32,
        )
        chosen = jnp.where(row == spot_ref[i : i + 1, :], product, 0.0)
        parts.append(jnp.sum(chosen, axis=0, keepdims=True))
    height = spot_ref.shape[0]
    if height > rowblk:
        parts.append(jnp.zeros((height - rowblk, LANES), jnp.float32))
    parts = jnp.concatenate(parts, 0)
    source = lax.broadcasted_iota(jnp.int32, (LANES, LANES), 0)
    lane = lax.broadcasted_iota(jnp.int32, (LANES, LANES), 1)
    fold = jnp.where((source % (2 * rb)) // 2 == lane % rb, 1.0, 0.0)
    spread = jnp.dot(
        parts, fold, preferred_element_type=jnp.float32, precision=lax.Precision.HIGHEST
    )
    per = LANES // rb
    block = lax.broadcasted_iota(jnp.int32, spread.shape, 0)
    lane = lax.broadcasted_iota(jnp.int32, spread.shape, 1)
    spread = jnp.where(lane // rb == block % per, spread, 0.0)
    lines = height // per
    recon = jnp.sum(spread.reshape(lines, per, LANES), axis=1)
    owner = state_ref[:lines]
    updated = state_ref[lines : 2 * lines] * share - state_ref[2 * lines :] * recon
    row = lax.broadcasted_iota(jnp.int32, recon.shape, 0)
    lane = lax.broadcasted_iota(jnp.int32, recon.shape, 1)
    last = row == lines - 1
    for m in range(mirrors):
        mine = owner == float(m)
        recon = jnp.where(
            last & (lane == LANES - 2 * mirrors + m),
            jnp.sum(jnp.where(mine, updated, 0.0), keepdims=True),
            recon,
        )
        recon = jnp.where(
            last & (lane == LANES - mirrors + m),
            jnp.sum(jnp.where(mine, share, 0.0), keepdims=True),
            recon,
        )
    sent_ref[...] = jnp.broadcast_to(recon[None], sent_ref.shape)


def settle(tile_ref, got_ref, state_ref, commands_ref, *, groups, mirrors):
    count, lines, _ = got_ref.shape
    tiles = count // groups
    recon = got_ref[tile_ref[0]]
    for g in range(1, groups):
        recon = recon + got_ref[g * tiles + tile_ref[0]]
    last = jnp.sum(got_ref[:, lines - 1, :], axis=0, keepdims=True)
    lane = lax.broadcasted_iota(jnp.int32, last.shape, 1)

    def entry(at):
        return jnp.sum(jnp.where(lane == at, last, 0.0), axis=1, keepdims=True)

    owner = state_ref[:lines]
    piston = jnp.zeros(owner.shape, jnp.float32)
    for m in range(mirrors):
        mean = entry(LANES - 2 * mirrors + m) / entry(LANES - mirrors + m)
        piston = jnp.where(owner == float(m), mean, piston)
    commands = state_ref[lines : 2 * lines] - state_ref[2 * lines :] * recon - piston
    acts = commands_ref.shape[0]
    for i in range(lines):
        some = min(LANES, acts - i * LANES)
        commands_ref[i * LANES : i * LANES + some] = commands[i, :some]


def on_device(
    screens,
    interp_weights,
    footprint,
    illumination,
    cm_values,
    cm_columns,
    prev_commands,
    owner_map,
    dm_gain,
):
    layers, blk_dev, pixels = screens.shape
    subs, _, foot = footprint.shape
    groups, tiles = lax.axis_size("grp"), lax.axis_size("tile")
    total = blk_dev * groups * tiles
    rowblk, positions, rb, comps, cbs = cm_values.shape
    acts = rowblk * rb
    mirrors = dm_gain.shape[0]
    height = -(-(acts + 2 * mirrors) // LANES) * LANES // rb
    lines = height * rb // LANES
    smem = pl.BlockSpec(memory_space=pltpu.SMEM)
    vmem = pl.BlockSpec(memory_space=pltpu.VMEM)
    limit = pltpu.CompilerParams(vmem_limit_bytes=24 * 2**20)
    f32 = jnp.float32

    edge = jax.ShapeDtypeStruct((layers, EDGE, pixels), screens.dtype)
    odd = (lax.axis_index("tile") % 2).astype(jnp.int32).reshape(1)
    outer, inner = pl.pallas_call(
        edges,
        in_specs=[smem, pl.BlockSpec(memory_space=pltpu.HBM)],
        out_specs=[vmem, vmem],
        out_shape=[edge, edge],
        scratch_shapes=[pltpu.SemaphoreType.DMA((2 * layers,))],
        compiler_params=limit,
        name="edges",
    )(odd, pltpu.with_memory_space_constraint(screens, pltpu.HBM))
    outer = swap(outer, 1)
    inner = swap(inner, -1)
    outer_first = odd * (blk_dev + EDGE) - EDGE
    inner_first = (1 - odd) * (blk_dev + EDGE) - EDGE

    start = (lax.axis_index(DEVICES) * blk_dev).astype(jnp.int32).reshape(1)
    base = (lax.axis_index("grp") * (tiles * subs // cbs)).astype(jnp.int32).reshape(1)
    foot_rows = jnp.transpose(footprint, (1, 2, 0))
    phase, spot, state = pl.pallas_call(
        lambda *refs: sense_own(*refs, total=total),
        in_specs=[smem] * 4 + [vmem] * 7,
        out_shape=(
            jax.ShapeDtypeStruct((subs, pixels), f32),
            jax.ShapeDtypeStruct((height, LANES), jnp.int32),
            jax.ShapeDtypeStruct((3 * lines, LANES), f32),
        ),
        compiler_params=limit,
        name="sense_own",
    )(
        start, inner_first, base, dm_gain, foot_rows, cm_columns.T, owner_map.reshape(1, acts),
        prev_commands.reshape(1, acts), screens, inner, interp_weights,
    )
    slopes, words = pl.pallas_call(
        lambda *refs: sense_rest(*refs, total=total),
        in_specs=[smem] * 2 + [vmem] * 6,
        out_shape=(
            jax.ShapeDtypeStruct((2, subs), f32),
            jax.ShapeDtypeStruct((tiles, 2 * subs // LANES, LANES), f32),
        ),
        compiler_params=limit,
        name="sense_rest",
    )(
        start, outer_first, foot_rows, outer, interp_weights, phase, illumination,
        transform_table(SIDE),
    )

    cm = cm_values.reshape(rowblk * positions * rb * comps, cbs)
    gathered = lax.all_to_all(words, "tile", 0, 0).reshape(-1, LANES)
    sent = pl.pallas_call(
        lambda *refs: reconstruct(*refs, rb=rb, share=1.0 / groups, mirrors=mirrors),
        in_specs=[vmem] * 4,
        out_shape=jax.ShapeDtypeStruct((groups * tiles, lines, LANES), f32),
        compiler_params=limit,
        name="reconstruct",
    )(gathered, cm, spot, state)
    got = lax.all_to_all(sent, DEVICES, 0, 0)
    tile = lax.axis_index("tile").astype(jnp.int32).reshape(1)
    commands = pl.pallas_call(
        lambda *refs: settle(*refs, groups=groups, mirrors=mirrors),
        in_specs=[smem, vmem, vmem],
        out_shape=jax.ShapeDtypeStruct((acts,), f32),
        compiler_params=limit,
        name="settle",
    )(tile, got, state)
    return (slopes, commands)


def solution(mesh):
    in_specs = (
        P(None, ("grp", "tile"), None),
        P(),
        P(("grp", "tile"), None, None),
        P(("grp", "tile"), None),
        P("tile", "grp", None, None, None),
        P("tile", "grp"),
        P("tile"),
        P("tile"),
        P(),
    )
    out_specs = (P(None, ("grp", "tile")), P("tile"))
    return jax.shard_map(
        on_device, mesh=mesh, in_specs=in_specs, out_specs=out_specs, check_vma=False
    )
```

```python
import math

import jax
import jax.numpy as jnp
import numpy as np
from jax import lax
from jax.experimental import pallas as pl
from jax.experimental.pallas import tpu as pltpu
from jax.sharding import PartitionSpec as P

SIDE = 16
DEVICES = ("grp", "tile")
LANES = 128
EDGE = 256


def swap(block, step):
    count = lax.axis_size(DEVICES)
    route = [(i, (i + step if i % 2 else i - step) % count) for i in range(count)]
    return lax.ppermute(block, DEVICES, route)


def transform_table(side):
    index = np.arange(side * side)
    rows, cols = index // side, index % side
    turns = (rows[:, None] * rows[None, :] + cols[:, None] * cols[None, :]) % side
    angle = turns.astype(np.float32) * np.float32(2.0 * math.pi / side)
    cosine, sine = np.cos(angle), np.sin(angle)
    table = np.concatenate(
        [np.concatenate([cosine, -sine], 1), np.concatenate([sine, cosine], 1)], 0
    )
    return jnp.asarray(table.T.astype(jnp.bfloat16))


def sine_cosine(angle):
    turns = jnp.floor(angle * np.float32(2.0 / math.pi) + 0.5)
    rest = angle - turns * np.float32(1.5703125)
    rest = rest - turns * np.float32(4.837512969970703125e-4)
    rest = rest - turns * np.float32(7.54978995489188216e-8)
    sq = rest * rest
    sine = (np.float32(-1.9515295891e-4) * sq + np.float32(8.3321608736e-3)) * sq
    sine = (sine - np.float32(1.6666654611e-1)) * sq * rest + rest
    cosine = (np.float32(2.443315711809948e-5) * sq - np.float32(1.388731625493765e-3)) * sq
    cosine = (cosine + np.float32(4.166664568298827e-2)) * sq * sq - np.float32(0.5) * sq + 1.0
    quarter = turns.astype(jnp.int32)
    odd = (quarter & 1) == 1
    out_sine = jnp.where(odd, cosine, sine)
    out_cosine = jnp.where(odd, sine, cosine)
    out_sine = jnp.where((quarter & 2) == 2, -out_sine, out_sine)
    out_cosine = jnp.where(((quarter + 1) & 2) == 2, -out_cosine, out_cosine)
    return out_sine, out_cosine


def offsets_of(foot_rows, start, total):
    away = foot_rows - start
    away = jnp.where(away < -(total // 2), away + total, away)
    away = jnp.where(away >= total // 2, away - total, away)
    away = away.astype(jnp.float32)
    foot, subs = away.shape
    filled = jnp.concatenate([away, jnp.zeros((8 - foot, subs), jnp.float32)], 0)
    return filled.T.astype(jnp.int32)


def hits(column, first, count):
    column = jnp.broadcast_to(column, (column.shape[0], LANES)).astype(jnp.int16)
    lane = lax.broadcasted_iota(jnp.int16, column.shape, 1)
    one, zero = jnp.bfloat16(1), jnp.bfloat16(0)
    parts = [
        jnp.where(lane == column - jnp.int16(first + b), one, zero)
        for b in range(0, count, LANES)
    ]
    return jnp.concatenate(parts, 1)


def edges(odd_ref, screens_ref, outer_ref, inner_ref, sems):
    layers, blocks, _ = screens_ref.shape
    last = (blocks // EDGE - 1) * EDGE
    outer = pl.multiple_of(odd_ref[0] * last, EDGE)
    inner = pl.multiple_of((1 - odd_ref[0]) * last, EDGE)
    copies = []
    for layer in range(layers):
        for first, ref, sem in ((outer, outer_ref, 0), (inner, inner_ref, 1)):
            block = screens_ref.at[layer, pl.ds(first, EDGE)]
            copies.append(
                pltpu.make_async_copy(block, ref.at[layer], sems.at[2 * layer + sem])
            )
    for copy in copies:
        copy.start()
    for copy in copies:
        copy.wait()


def mirror_rows(
    base_ref, gain_ref, cols_ref, owner_ref, prev_ref, cm_ref, sent_ref, spot_ref, state_ref
):
    tiles, rows_sent, _ = sent_ref.shape
    mirrors = gain_ref.shape[0]
    positions, rowblk = cols_ref.shape
    acts = owner_ref.shape[1]
    rb = acts // rowblk
    cols = (cols_ref[...] - base_ref[0]).astype(jnp.float32)
    lane = lax.broadcasted_iota(jnp.int32, (positions, LANES), 1)
    place = lax.broadcasted_iota(jnp.int32, (positions, LANES), 0)
    spread = jnp.where(lane // (2 * rb) == place, 1.0, 0.0)
    cols = lax.dot_general(
        cols, spread, (((0,), (0,)), ((), ())), preferred_element_type=jnp.float32
    ).astype(jnp.int32)
    comp = lax.broadcasted_iota(jnp.int32, cols.shape, 1) % 2
    height = spot_ref.shape[0]
    spot_ref[...] = jnp.concatenate(
        [cols * 2 + comp, jnp.full((height - rowblk, LANES), -1, jnp.int32)], 0
    )
    owner = owner_ref[...]
    act = lax.broadcasted_iota(jnp.int32, (rowblk, acts), 1)
    block = lax.broadcasted_iota(jnp.int32, (rowblk, acts), 0)
    held = jnp.where(act // rb == block, owner, 0).astype(jnp.float32).astype(jnp.bfloat16)
    act = lax.broadcasted_iota(jnp.int32, (acts, LANES), 0)
    wide = lax.broadcasted_iota(jnp.int32, (acts, LANES), 1)
    spread = jnp.where(act % rb == (wide % (2 * rb)) // 2, 1.0, 0.0).astype(jnp.bfloat16)
    owners = jnp.dot(held, spread, preferred_element_type=jnp.float32)
    target = cols * (2 * mirrors) + comp * mirrors + owners.astype(jnp.int32)

    used = 4 * mirrors
    row = lax.broadcasted_iota(jnp.int16, (tiles * used, LANES), 0)
    one, zero = jnp.bfloat16(1), jnp.bfloat16(0)
    picks = [
        jnp.where(
            row == jnp.broadcast_to(target[i : i + 1, :], row.shape).astype(jnp.int16), one, zero
        )
        for i in range(rowblk)
    ]
    sums = jnp.dot(
        jnp.concatenate(picks, 1), cm_ref[...], preferred_element_type=jnp.float32
    )
    lane = lax.broadcasted_iota(jnp.int32, (1, LANES), 1)
    extra = jnp.zeros((1, LANES), jnp.float32)
    gain = jnp.zeros(owner.shape, jnp.float32)
    for m in range(mirrors):
        mine = owner == m
        gain = jnp.where(mine, gain_ref[m], gain)
        prev = jnp.sum(jnp.where(mine, prev_ref[...], 0.0), axis=1, keepdims=True)
        number = jnp.sum(jnp.where(mine, 1.0, 0.0), axis=1, keepdims=True)
        extra = jnp.where(lane == m, prev, jnp.where(lane == mirrors + m, number, extra))
    for t in range(tiles):
        sent_ref[t, 0:used, :] = sums[t * used : (t + 1) * used]
    sent_ref[:, used : used + 1, :] = jnp.broadcast_to(extra[None], (tiles, 1, LANES))
    left = rows_sent - used - 1
    sent_ref[:, used + 1 :, :] = jnp.zeros((tiles, left, LANES), jnp.float32)

    lines = height * rb // LANES
    missing = lines * LANES - acts
    rows = []
    for values, fill in ((owner.astype(jnp.float32), -1.0), (prev_ref[...], 0.0), (gain, 0.0)):
        values = jnp.concatenate([values, jnp.full((1, missing), fill, jnp.float32)], 1)
        rows += [values[:, i * LANES : (i + 1) * LANES] for i in range(lines)]
    state_ref[...] = jnp.concatenate(rows, 0)


def sense_own(
    start_ref, first_ref, foot_ref, screens_ref, inner_ref, weights_ref, phase_ref, *, total
):
    layers, foot, _ = foot_ref.shape
    blocks, pixels = screens_ref.shape[1:]
    phase = None
    for layer in range(layers):
        offsets = offsets_of(foot_ref[layer], start_ref[0], total)
        picked = []
        for k in range(foot):
            column = offsets[:, k : k + 1]
            rows = jnp.dot(
                hits(column, 0, blocks), screens_ref[layer], preferred_element_type=jnp.float32
            )
            rows = rows + jnp.dot(
                hits(column - first_ref[0], 0, EDGE),
                inner_ref[layer],
                preferred_element_type=jnp.float32,
            )
            picked.append(rows.astype(jnp.bfloat16))
        part = jnp.dot(
            jnp.concatenate(picked, 1),
            weights_ref[layer].reshape(foot * pixels, pixels),
            preferred_element_type=jnp.float32,
        )
        phase = part if phase is None else phase + part
    phase_ref[...] = phase


def sense_rest(
    start_ref, first_ref, foot_ref, outer_ref, weights_ref, phase_ref, illum_ref, table_ref,
    slopes_ref, words_ref, *, total
):
    layers, foot, subs = foot_ref.shape
    pixels = phase_ref.shape[1]
    phase = phase_ref[...]
    for layer in range(layers):
        offsets = offsets_of(foot_ref[layer], start_ref[0], total)
        picked = []
        for k in range(foot):
            found = hits(offsets[:, k : k + 1] - first_ref[0], 0, EDGE)
            rows = jnp.dot(found, outer_ref[layer], preferred_element_type=jnp.float32)
            picked.append(rows.astype(jnp.bfloat16))
        phase = phase + jnp.dot(
            jnp.concatenate(picked, 1),
            weights_ref[layer].reshape(foot * pixels, pixels),
            preferred_element_type=jnp.float32,
        )
    phase = phase.T
    illum = illum_ref[...].T
    sine, cosine = sine_cosine(phase)
    field = jnp.concatenate([illum * cosine, illum * sine], 0).astype(jnp.bfloat16)
    spectrum = jnp.dot(table_ref[...], field, preferred_element_type=jnp.float32)
    real_part = spectrum[:pixels]
    imag_part = spectrum[pixels:]
    intensity = real_part * real_part + imag_part * imag_part
    row = lax.broadcasted_iota(jnp.int32, intensity.shape, 0)
    cv = row % SIDE
    cu = row // SIDE
    cv = (cv - SIDE * (cv >= SIDE // 2).astype(jnp.int32)).astype(jnp.float32)
    cu = (cu - SIDE * (cu >= SIDE // 2).astype(jnp.int32)).astype(jnp.float32)
    whole = jnp.sum(intensity, axis=0, keepdims=True)
    slope_x = jnp.sum(intensity * cv, axis=0, keepdims=True) / whole
    slope_y = jnp.sum(intensity * cu, axis=0, keepdims=True) / whole
    slopes = jnp.concatenate([slope_x, slope_y], 0)
    slopes_ref[...] = slopes
    words = slopes.astype(jnp.bfloat16).astype(jnp.float32)
    words = [words[:, h * LANES : (h + 1) * LANES] for h in range(subs // LANES)]
    words_ref[...] = jnp.concatenate(words, 0)


def pack(words_ref, rows_ref, sent_ref, extra_ref, *, mirrors):
    words = words_ref[...]
    sums = jnp.sum(rows_ref[...], axis=0)
    lane = lax.broadcasted_iota(jnp.int32, (1, LANES), 1)
    line = jnp.zeros((1, LANES), jnp.float32)
    for m in range(mirrors):
        product = jnp.zeros((1, LANES), jnp.float32)
        for k in range(words.shape[0]):
            at = k * mirrors + m
            product = product + sums[at : at + 1] * words[k : k + 1]
        line = jnp.where(lane == m, jnp.sum(product, axis=1, keepdims=True), line)
    high = line.astype(jnp.bfloat16).astype(jnp.float32)
    middle = (line - high).astype(jnp.bfloat16).astype(jnp.float32)
    low = line - high - middle
    rows = jnp.concatenate([words, high, middle, low, jnp.zeros_like(low)], 0)
    sent_ref[...] = jnp.broadcast_to(rows.astype(jnp.bfloat16)[None], sent_ref.shape)
    used = words.shape[0] * mirrors
    extra_ref[...] = sums[used : used + 1]


def reconstruct(words_ref, cm_ref, spot_ref, sent_ref, *, rb):
    got = words_ref[...].astype(jnp.float32)
    words = got[:, :4, :].reshape(-1, LANES).astype(jnp.bfloat16)
    line = jnp.sum(got, axis=0)
    line = line[4:5] + line[5:6] + line[6:7]
    rowblk = cm_ref.shape[0] // LANES
    row = lax.broadcasted_iota(jnp.int32, (words.shape[0], LANES), 0)
    parts = []
    for i in range(rowblk):
        product = lax.dot_general(
            words,
            cm_ref[i * LANES : (i + 1) * LANES, :],
            (((1,), (1,)), ((), ())),
            preferred_element_type=jnp.float32,
        )
        chosen = jnp.where(row == spot_ref[i : i + 1, :], product, 0.0)
        parts.append(jnp.sum(chosen, axis=0, keepdims=True))
    height = spot_ref.shape[0]
    if height > rowblk:
        parts.append(jnp.zeros((height - rowblk, LANES), jnp.float32))
    parts = jnp.concatenate(parts, 0)
    source = lax.broadcasted_iota(jnp.int32, (LANES, LANES), 0)
    lane = lax.broadcasted_iota(jnp.int32, (LANES, LANES), 1)
    fold = jnp.where((source % (2 * rb)) // 2 == lane % rb, 1.0, 0.0)
    spread = jnp.dot(
        parts, fold, preferred_element_type=jnp.float32, precision=lax.Precision.HIGHEST
    )
    per = LANES // rb
    block = lax.broadcasted_iota(jnp.int32, spread.shape, 0)
    lane = lax.broadcasted_iota(jnp.int32, spread.shape, 1)
    spread = jnp.where(lane // rb == block % per, spread, 0.0)
    recon = jnp.sum(spread.reshape(height // per, per, LANES), axis=1)
    rest = sent_ref.shape[1] - recon.shape[0] - 1
    rows = jnp.concatenate([recon, line, jnp.zeros((rest, LANES), jnp.float32)], 0)
    sent_ref[...] = jnp.broadcast_to(rows[None], sent_ref.shape)


def settle(got_ref, extra_ref, state_ref, commands_ref, *, mirrors):
    lines = state_ref.shape[0] // 3
    sums = jnp.sum(got_ref[...], axis=0)
    line = sums[lines : lines + 1]
    extra = extra_ref[...]
    lane = lax.broadcasted_iota(jnp.int32, line.shape, 1)

    def entry(values, at):
        return jnp.sum(jnp.where(lane == at, values, 0.0), axis=1, keepdims=True)

    owner = state_ref[:lines]
    gain = state_ref[2 * lines :]
    piston = jnp.zeros(owner.shape, jnp.float32)
    for m in range(mirrors):
        total = entry(extra, m) - gain * entry(line, m)
        piston = jnp.where(owner == float(m), total / entry(extra, mirrors + m), piston)
    commands = state_ref[lines : 2 * lines] - gain * sums[:lines] - piston
    acts = commands_ref.shape[0]
    for i in range(lines):
        some = min(LANES, acts - i * LANES)
        commands_ref[i * LANES : i * LANES + some] = commands[i, :some]


def on_device(
    screens,
    interp_weights,
    footprint,
    illumination,
    cm_values,
    cm_columns,
    prev_commands,
    owner_map,
    dm_gain,
):
    layers, blk_dev, pixels = screens.shape
    subs, _, foot = footprint.shape
    groups, tiles = lax.axis_size("grp"), lax.axis_size("tile")
    total = blk_dev * groups * tiles
    rowblk, positions, rb, comps, cbs = cm_values.shape
    acts = rowblk * rb
    mirrors = dm_gain.shape[0]
    height = -(-acts // LANES) * LANES // rb
    lines = height * rb // LANES
    smem = pl.BlockSpec(memory_space=pltpu.SMEM)
    vmem = pl.BlockSpec(memory_space=pltpu.VMEM)
    limit = pltpu.CompilerParams(vmem_limit_bytes=24 * 2**20)
    f32 = jnp.float32

    edge = jax.ShapeDtypeStruct((layers, EDGE, pixels), screens.dtype)
    odd = (lax.axis_index("tile") % 2).astype(jnp.int32).reshape(1)
    outer, inner = pl.pallas_call(
        edges,
        in_specs=[smem, pl.BlockSpec(memory_space=pltpu.HBM)],
        out_specs=[vmem, vmem],
        out_shape=[edge, edge],
        scratch_shapes=[pltpu.SemaphoreType.DMA((2 * layers,))],
        compiler_params=limit,
        name="edges",
    )(odd, pltpu.with_memory_space_constraint(screens, pltpu.HBM))
    outer = swap(outer, 1)
    inner = swap(inner, -1)
    outer_first = odd * (blk_dev + EDGE) - EDGE
    inner_first = (1 - odd) * (blk_dev + EDGE) - EDGE

    base = (lax.axis_index("grp") * (tiles * subs // cbs)).astype(jnp.int32).reshape(1)
    cm = cm_values.reshape(rowblk * positions * rb * comps, cbs)
    rows, spot, state = pl.pallas_call(
        mirror_rows,
        in_specs=[smem] * 2 + [vmem] * 4,
        out_shape=(
            jax.ShapeDtypeStruct((tiles, 16, LANES), f32),
            jax.ShapeDtypeStruct((height, LANES), jnp.int32),
            jax.ShapeDtypeStruct((3 * lines, LANES), f32),
        ),
        compiler_params=limit,
        name="mirror_rows",
    )(
        base, dm_gain, cm_columns.T, owner_map.reshape(1, acts), prev_commands.reshape(1, acts), cm
    )
    start = (lax.axis_index(DEVICES) * blk_dev).astype(jnp.int32).reshape(1)
    foot_rows = jnp.transpose(footprint, (1, 2, 0))
    rows, foot_rows = lax.optimization_barrier((rows, foot_rows))
    rows = lax.all_to_all(rows, "tile", 0, 0)

    phase = pl.pallas_call(
        lambda *refs: sense_own(*refs, total=total),
        in_specs=[smem] * 2 + [vmem] * 4,
        out_shape=jax.ShapeDtypeStruct((subs, pixels), f32),
        compiler_params=limit,
        name="sense_own",
    )(start, inner_first, foot_rows, screens, inner, interp_weights)
    slopes, words = pl.pallas_call(
        lambda *refs: sense_rest(*refs, total=total),
        in_specs=[smem] * 2 + [vmem] * 6,
        out_shape=(
            jax.ShapeDtypeStruct((2, subs), f32),
            jax.ShapeDtypeStruct((2 * subs // LANES, LANES), f32),
        ),
        compiler_params=limit,
        name="sense_rest",
    )(
        start, outer_first, foot_rows, outer, interp_weights, phase, illumination,
        transform_table(SIDE),
    )
    packed, extra = pl.pallas_call(
        lambda *refs: pack(*refs, mirrors=mirrors),
        in_specs=[vmem] * 2,
        out_shape=(
            jax.ShapeDtypeStruct((tiles, 8, LANES), jnp.bfloat16),
            jax.ShapeDtypeStruct((1, LANES), f32),
        ),
        compiler_params=limit,
        name="pack",
    )(words, rows)

    gathered = lax.all_to_all(packed, "tile", 0, 0)
    sent = pl.pallas_call(
        lambda *refs: reconstruct(*refs, rb=rb),
        in_specs=[vmem] * 3,
        out_shape=jax.ShapeDtypeStruct((groups, 8, LANES), f32),
        compiler_params=limit,
        name="reconstruct",
    )(gathered, cm, spot)
    got = lax.all_to_all(sent, "grp", 0, 0)
    commands = pl.pallas_call(
        lambda *refs: settle(*refs, mirrors=mirrors),
        in_specs=[vmem] * 3,
        out_shape=jax.ShapeDtypeStruct((acts,), f32),
        compiler_params=limit,
        name="settle",
    )(got, extra, state)
    return (slopes, commands)


def solution(mesh):
    in_specs = (
        P(None, ("grp", "tile"), None),
        P(),
        P(("grp", "tile"), None, None),
        P(("grp", "tile"), None),
        P("tile", "grp", None, None, None),
        P("tile", "grp"),
        P("tile"),
        P("tile"),
        P(),
    )
    out_specs = (P(None, ("grp", "tile")), P("tile"))
    return jax.shard_map(
        on_device, mesh=mesh, in_specs=in_specs, out_specs=out_specs, check_vma=False
    )
```

```python
import math

import jax
import jax.numpy as jnp
import numpy as np
from jax import lax
from jax.experimental import pallas as pl
from jax.experimental.pallas import tpu as pltpu
from jax.sharding import PartitionSpec as P

SIDE = 16
DEVICES = ("grp", "tile")
LANES = 128
EDGE = 256


def swap(block, step):
    count = lax.axis_size(DEVICES)
    route = [(i, (i + step if i % 2 else i - step) % count) for i in range(count)]
    return lax.ppermute(block, DEVICES, route)


def transform_table(side):
    index = np.arange(side * side)
    rows, cols = index // side, index % side
    turns = (rows[:, None] * rows[None, :] + cols[:, None] * cols[None, :]) % side
    angle = turns.astype(np.float32) * np.float32(2.0 * math.pi / side)
    cosine, sine = np.cos(angle), np.sin(angle)
    table = np.concatenate(
        [np.concatenate([cosine, -sine], 1), np.concatenate([sine, cosine], 1)], 0
    )
    return jnp.asarray(table.T.astype(jnp.bfloat16))


def sine_cosine(angle):
    turns = jnp.floor(angle * np.float32(2.0 / math.pi) + 0.5)
    rest = angle - turns * np.float32(1.5703125)
    rest = rest - turns * np.float32(4.837512969970703125e-4)
    rest = rest - turns * np.float32(7.54978995489188216e-8)
    sq = rest * rest
    sine = (np.float32(-1.9515295891e-4) * sq + np.float32(8.3321608736e-3)) * sq
    sine = (sine - np.float32(1.6666654611e-1)) * sq * rest + rest
    cosine = (np.float32(2.443315711809948e-5) * sq - np.float32(1.388731625493765e-3)) * sq
    cosine = (cosine + np.float32(4.166664568298827e-2)) * sq * sq - np.float32(0.5) * sq + 1.0
    quarter = turns.astype(jnp.int32)
    odd = (quarter & 1) == 1
    out_sine = jnp.where(odd, cosine, sine)
    out_cosine = jnp.where(odd, sine, cosine)
    out_sine = jnp.where((quarter & 2) == 2, -out_sine, out_sine)
    out_cosine = jnp.where(((quarter + 1) & 2) == 2, -out_cosine, out_cosine)
    return out_sine, out_cosine


def offsets_of(foot_rows, start, total):
    away = foot_rows - start
    away = jnp.where(away < -(total // 2), away + total, away)
    away = jnp.where(away >= total // 2, away - total, away)
    away = away.astype(jnp.float32)
    foot, subs = away.shape
    filled = jnp.concatenate([away, jnp.zeros((8 - foot, subs), jnp.float32)], 0)
    return filled.T.astype(jnp.int32)


def hits(column, first, count):
    column = jnp.broadcast_to(column, (column.shape[0], LANES)).astype(jnp.int16)
    lane = lax.broadcasted_iota(jnp.int16, column.shape, 1)
    one, zero = jnp.bfloat16(1), jnp.bfloat16(0)
    parts = [
        jnp.where(lane == column - jnp.int16(first + b), one, zero)
        for b in range(0, count, LANES)
    ]
    return jnp.concatenate(parts, 1)


def edges(screens_ref, matrix_ref, outer_ref, inner_ref, cm_ref, sems):
    layers, blocks, _ = screens_ref.shape
    last = (blocks // EDGE - 1) * EDGE
    odd = lax.axis_index("tile") % 2
    outer = pl.multiple_of(odd * last, EDGE)
    inner = pl.multiple_of((1 - odd) * last, EDGE)
    copies = []
    for layer in range(layers):
        for first, ref, sem in ((outer, outer_ref, 0), (inner, inner_ref, 1)):
            block = screens_ref.at[layer, pl.ds(first, EDGE)]
            copies.append(
                pltpu.make_async_copy(block, ref.at[layer], sems.at[2 * layer + sem])
            )
    copies.append(pltpu.make_async_copy(matrix_ref, cm_ref, sems.at[2 * layers]))
    for copy in copies:
        copy.start()
    for copy in copies:
        copy.wait()


def mirror_rows(
    gain_ref, cols_ref, owner_ref, prev_ref, cm_ref, sent_ref, spot_ref, state_ref, *, columns
):
    tiles, rows_sent, _ = sent_ref.shape
    mirrors = gain_ref.shape[0]
    positions, rowblk = cols_ref.shape
    acts = owner_ref.shape[1]
    rb = acts // rowblk
    cols = (cols_ref[...] - lax.axis_index("grp") * columns).astype(jnp.float32)
    lane = lax.broadcasted_iota(jnp.int32, (positions, LANES), 1)
    place = lax.broadcasted_iota(jnp.int32, (positions, LANES), 0)
    spread = jnp.where(lane // (2 * rb) == place, 1.0, 0.0)
    cols = lax.dot_general(
        cols, spread, (((0,), (0,)), ((), ())), preferred_element_type=jnp.float32
    ).astype(jnp.int32)
    comp = lax.broadcasted_iota(jnp.int32, cols.shape, 1) % 2
    height = spot_ref.shape[0]
    spot_ref[...] = jnp.concatenate(
        [cols * 2 + comp, jnp.full((height - rowblk, LANES), -1, jnp.int32)], 0
    )
    owner = owner_ref[...]
    act = lax.broadcasted_iota(jnp.int32, (rowblk, acts), 1)
    block = lax.broadcasted_iota(jnp.int32, (rowblk, acts), 0)
    held = jnp.where(act // rb == block, owner, 0).astype(jnp.float32).astype(jnp.bfloat16)
    act = lax.broadcasted_iota(jnp.int32, (acts, LANES), 0)
    wide = lax.broadcasted_iota(jnp.int32, (acts, LANES), 1)
    spread = jnp.where(act % rb == (wide % (2 * rb)) // 2, 1.0, 0.0).astype(jnp.bfloat16)
    owners = jnp.dot(held, spread, preferred_element_type=jnp.float32)
    target = cols * (2 * mirrors) + comp * mirrors + owners.astype(jnp.int32)

    used = 4 * mirrors
    row = lax.broadcasted_iota(jnp.int16, (tiles * used, LANES), 0)
    one, zero = jnp.bfloat16(1), jnp.bfloat16(0)
    picks = [
        jnp.where(
            row == jnp.broadcast_to(target[i : i + 1, :], row.shape).astype(jnp.int16), one, zero
        )
        for i in range(rowblk)
    ]
    lane = lax.broadcasted_iota(jnp.int32, (1, LANES), 1)
    extra = jnp.zeros((1, LANES), jnp.float32)
    gain = jnp.zeros(owner.shape, jnp.float32)
    for m in range(mirrors):
        mine = owner == m
        gain = jnp.where(mine, gain_ref[m], gain)
        prev = jnp.sum(jnp.where(mine, prev_ref[...], 0.0), axis=1, keepdims=True)
        number = jnp.sum(jnp.where(mine, 1.0, 0.0), axis=1, keepdims=True)
        extra = jnp.where(lane == m, prev, jnp.where(lane == mirrors + m, number, extra))
    lines = height * rb // LANES
    missing = lines * LANES - acts
    rows = []
    for values, fill in ((owner.astype(jnp.float32), -1.0), (prev_ref[...], 0.0), (gain, 0.0)):
        values = jnp.concatenate([values, jnp.full((1, missing), fill, jnp.float32)], 1)
        rows += [values[:, i * LANES : (i + 1) * LANES] for i in range(lines)]
    state_ref[...] = jnp.concatenate(rows, 0)

    sums = jnp.dot(
        jnp.concatenate(picks, 1), cm_ref[...], preferred_element_type=jnp.float32
    )
    for t in range(tiles):
        sent_ref[t, 0:used, :] = sums[t * used : (t + 1) * used]
    sent_ref[:, used : used + 1, :] = jnp.broadcast_to(extra[None], (tiles, 1, LANES))
    left = rows_sent - used - 1
    sent_ref[:, used + 1 :, :] = jnp.zeros((tiles, left, LANES), jnp.float32)


def pick_own(foot_ref, screens_ref, inner_ref, picked_ref, *, total):
    layers, foot, _ = foot_ref.shape
    blocks, pixels = screens_ref.shape[1:]
    start = lax.axis_index(DEVICES) * blocks
    first = (1 - lax.axis_index("tile") % 2) * (blocks + EDGE) - EDGE
    for layer in range(layers):
        offsets = offsets_of(foot_ref[layer], start, total)
        for k in range(foot):
            column = offsets[:, k : k + 1]
            rows = jnp.dot(
                hits(column, 0, blocks), screens_ref[layer], preferred_element_type=jnp.float32
            )
            rows = rows + jnp.dot(
                hits(column - first, 0, EDGE),
                inner_ref[layer],
                preferred_element_type=jnp.float32,
            )
            picked_ref[layer, :, k * pixels : (k + 1) * pixels] = rows.astype(jnp.bfloat16)


def sense_rest(
    foot_ref, outer_ref, weights_ref, own_ref, illum_ref, table_ref, slopes_ref, words_ref, *,
    total, blocks
):
    layers, foot, subs = foot_ref.shape
    pixels = illum_ref.shape[1]
    start = lax.axis_index(DEVICES) * blocks
    first = (lax.axis_index("tile") % 2) * (blocks + EDGE) - EDGE
    phase = None
    for layer in range(layers):
        offsets = offsets_of(foot_ref[layer], start, total)
        picked = []
        for k in range(foot):
            found = hits(offsets[:, k : k + 1] - first, 0, EDGE)
            rows = jnp.dot(found, outer_ref[layer], preferred_element_type=jnp.float32)
            own = own_ref[layer, :, k * pixels : (k + 1) * pixels]
            picked.append(rows.astype(jnp.bfloat16) + own)
        part = jnp.dot(
            jnp.concatenate(picked, 1),
            weights_ref[layer].reshape(foot * pixels, pixels),
            preferred_element_type=jnp.float32,
        )
        phase = part if phase is None else phase + part
    phase = phase.T
    illum = illum_ref[...].T
    sine, cosine = sine_cosine(phase)
    field = jnp.concatenate([illum * cosine, illum * sine], 0).astype(jnp.bfloat16)
    spectrum = jnp.dot(table_ref[...], field, preferred_element_type=jnp.float32)
    real_part = spectrum[:pixels]
    imag_part = spectrum[pixels:]
    intensity = real_part * real_part + imag_part * imag_part
    row = lax.broadcasted_iota(jnp.int32, intensity.shape, 0)
    cv = row % SIDE
    cu = row // SIDE
    cv = (cv - SIDE * (cv >= SIDE // 2).astype(jnp.int32)).astype(jnp.float32)
    cu = (cu - SIDE * (cu >= SIDE // 2).astype(jnp.int32)).astype(jnp.float32)
    whole = jnp.sum(intensity, axis=0, keepdims=True)
    slope_x = jnp.sum(intensity * cv, axis=0, keepdims=True) / whole
    slope_y = jnp.sum(intensity * cu, axis=0, keepdims=True) / whole
    slopes = jnp.concatenate([slope_x, slope_y], 0)
    slopes_ref[...] = slopes
    words = slopes.astype(jnp.bfloat16).astype(jnp.float32)
    words = [words[:, h * LANES : (h + 1) * LANES] for h in range(subs // LANES)]
    words_ref[...] = jnp.concatenate(words, 0)


def pack(words_ref, rows_ref, sent_ref, extra_ref, *, mirrors):
    words = words_ref[...]
    sums = jnp.sum(rows_ref[...], axis=0)
    lane = lax.broadcasted_iota(jnp.int32, (1, LANES), 1)
    line = jnp.zeros((1, LANES), jnp.float32)
    for m in range(mirrors):
        product = jnp.zeros((1, LANES), jnp.float32)
        for k in range(words.shape[0]):
            at = k * mirrors + m
            product = product + sums[at : at + 1] * words[k : k + 1]
        line = jnp.where(lane == m, jnp.sum(product, axis=1, keepdims=True), line)
    high = line.astype(jnp.bfloat16).astype(jnp.float32)
    middle = (line - high).astype(jnp.bfloat16).astype(jnp.float32)
    low = line - high - middle
    rows = jnp.concatenate([words, high, middle, low, jnp.zeros_like(low)], 0)
    sent_ref[...] = jnp.broadcast_to(rows.astype(jnp.bfloat16)[None], sent_ref.shape)
    used = words.shape[0] * mirrors
    extra_ref[...] = sums[used : used + 1]


def reconstruct(words_ref, cm_ref, spot_ref, sent_ref, *, rb):
    got = words_ref[...].astype(jnp.float32)
    words = got[:, :4, :].reshape(-1, LANES).astype(jnp.bfloat16)
    line = jnp.sum(got, axis=0)
    line = line[4:5] + line[5:6] + line[6:7]
    rowblk = cm_ref.shape[0] // LANES
    row = lax.broadcasted_iota(jnp.int32, (words.shape[0], LANES), 0)
    parts = []
    for i in range(rowblk):
        product = lax.dot_general(
            words,
            cm_ref[i * LANES : (i + 1) * LANES, :],
            (((1,), (1,)), ((), ())),
            preferred_element_type=jnp.float32,
        )
        chosen = jnp.where(row == spot_ref[i : i + 1, :], product, 0.0)
        parts.append(jnp.sum(chosen, axis=0, keepdims=True))
    height = spot_ref.shape[0]
    if height > rowblk:
        parts.append(jnp.zeros((height - rowblk, LANES), jnp.float32))
    parts = jnp.concatenate(parts, 0)
    source = lax.broadcasted_iota(jnp.int32, (LANES, LANES), 0)
    lane = lax.broadcasted_iota(jnp.int32, (LANES, LANES), 1)
    fold = jnp.where((source % (2 * rb)) // 2 == lane % rb, 1.0, 0.0)
    spread = jnp.dot(
        parts, fold, preferred_element_type=jnp.float32, precision=lax.Precision.HIGHEST
    )
    per = LANES // rb
    block = lax.broadcasted_iota(jnp.int32, spread.shape, 0)
    lane = lax.broadcasted_iota(jnp.int32, spread.shape, 1)
    spread = jnp.where(lane // rb == block % per, spread, 0.0)
    recon = jnp.sum(spread.reshape(height // per, per, LANES), axis=1)
    rest = sent_ref.shape[1] - recon.shape[0] - 1
    rows = jnp.concatenate([recon, line, jnp.zeros((rest, LANES), jnp.float32)], 0)
    sent_ref[...] = jnp.broadcast_to(rows[None], sent_ref.shape)


def settle(got_ref, extra_ref, state_ref, commands_ref, *, mirrors):
    lines = state_ref.shape[0] // 3
    sums = jnp.sum(got_ref[...], axis=0)
    line = sums[lines : lines + 1]
    extra = extra_ref[...]
    lane = lax.broadcasted_iota(jnp.int32, line.shape, 1)

    def entry(values, at):
        return jnp.sum(jnp.where(lane == at, values, 0.0), axis=1, keepdims=True)

    owner = state_ref[:lines]
    gain = state_ref[2 * lines :]
    piston = jnp.zeros(owner.shape, jnp.float32)
    for m in range(mirrors):
        total = entry(extra, m) - gain * entry(line, m)
        piston = jnp.where(owner == float(m), total / entry(extra, mirrors + m), piston)
    commands = state_ref[lines : 2 * lines] - gain * sums[:lines] - piston
    acts = commands_ref.shape[0]
    for i in range(lines):
        some = min(LANES, acts - i * LANES)
        commands_ref[i * LANES : i * LANES + some] = commands[i, :some]


def on_device(
    screens,
    interp_weights,
    footprint,
    illumination,
    cm_values,
    cm_columns,
    prev_commands,
    owner_map,
    dm_gain,
):
    layers, blk_dev, pixels = screens.shape
    subs, _, foot = footprint.shape
    groups, tiles = lax.axis_size("grp"), lax.axis_size("tile")
    total = blk_dev * groups * tiles
    rowblk, positions, rb, comps, cbs = cm_values.shape
    acts = rowblk * rb
    mirrors = dm_gain.shape[0]
    height = -(-acts // LANES) * LANES // rb
    lines = height * rb // LANES
    smem = pl.BlockSpec(memory_space=pltpu.SMEM)
    vmem = pl.BlockSpec(memory_space=pltpu.VMEM)
    limit = pltpu.CompilerParams(vmem_limit_bytes=24 * 2**20)
    f32 = jnp.float32

    edge = jax.ShapeDtypeStruct((layers, EDGE, pixels), screens.dtype)
    hbm = pl.BlockSpec(memory_space=pltpu.HBM)
    cm = cm_values.reshape(rowblk * positions * rb * comps, cbs)
    outer, inner, loaded = pl.pallas_call(
        edges,
        in_specs=[hbm] * 2,
        out_specs=[vmem] * 3,
        out_shape=[edge, edge, jax.ShapeDtypeStruct(cm.shape, cm.dtype)],
        scratch_shapes=[pltpu.SemaphoreType.DMA((2 * layers + 1,))],
        compiler_params=limit,
        name="edges",
    )(
        pltpu.with_memory_space_constraint(screens, pltpu.HBM),
        pltpu.with_memory_space_constraint(cm, pltpu.HBM),
    )
    outer = swap(outer, 1)
    inner = swap(inner, -1)

    rows, spot, state = pl.pallas_call(
        lambda *refs: mirror_rows(*refs, columns=tiles * subs // cbs),
        in_specs=[smem] + [vmem] * 4,
        out_shape=(
            jax.ShapeDtypeStruct((tiles, 16, LANES), f32),
            jax.ShapeDtypeStruct((height, LANES), jnp.int32),
            jax.ShapeDtypeStruct((3 * lines, LANES), f32),
        ),
        compiler_params=limit,
        name="mirror_rows",
    )(
        dm_gain, cm_columns.T, owner_map.reshape(1, acts), prev_commands.reshape(1, acts), loaded
    )
    foot_rows = jnp.transpose(footprint, (1, 2, 0))
    rows, foot_rows = lax.optimization_barrier((rows, foot_rows))
    rows = lax.all_to_all(rows, "tile", 0, 0)

    picked = pl.pallas_call(
        lambda *refs: pick_own(*refs, total=total),
        in_specs=[vmem] * 3,
        out_shape=jax.ShapeDtypeStruct((layers, subs, foot * pixels), screens.dtype),
        compiler_params=limit,
        name="pick_own",
    )(foot_rows, screens, inner)
    slopes, words = pl.pallas_call(
        lambda *refs: sense_rest(*refs, total=total, blocks=blk_dev),
        in_specs=[vmem] * 6,
        out_shape=(
            jax.ShapeDtypeStruct((2, subs), f32),
            jax.ShapeDtypeStruct((2 * subs // LANES, LANES), f32),
        ),
        compiler_params=limit,
        name="sense_rest",
    )(
        foot_rows, outer, interp_weights, picked, illumination, transform_table(SIDE)
    )
    packed, extra = pl.pallas_call(
        lambda *refs: pack(*refs, mirrors=mirrors),
        in_specs=[vmem] * 2,
        out_shape=(
            jax.ShapeDtypeStruct((tiles, 8, LANES), jnp.bfloat16),
            jax.ShapeDtypeStruct((1, LANES), f32),
        ),
        compiler_params=limit,
        name="pack",
    )(words, rows)

    gathered = lax.all_to_all(packed, "tile", 0, 0)
    sent = pl.pallas_call(
        lambda *refs: reconstruct(*refs, rb=rb),
        in_specs=[vmem] * 3,
        out_shape=jax.ShapeDtypeStruct((groups, 8, LANES), f32),
        compiler_params=limit,
        name="reconstruct",
    )(gathered, cm, spot)
    got = lax.all_to_all(sent, "grp", 0, 0)
    commands = pl.pallas_call(
        lambda *refs: settle(*refs, mirrors=mirrors),
        in_specs=[vmem] * 3,
        out_shape=jax.ShapeDtypeStruct((acts,), f32),
        compiler_params=limit,
        name="settle",
    )(got, extra, state)
    return (slopes, commands)


def solution(mesh):
    in_specs = (
        P(None, ("grp", "tile"), None),
        P(),
        P(("grp", "tile"), None, None),
        P(("grp", "tile"), None),
        P("tile", "grp", None, None, None),
        P("tile", "grp"),
        P("tile"),
        P("tile"),
        P(),
    )
    out_specs = (P(None, ("grp", "tile")), P("tile"))
    return jax.shard_map(
        on_device, mesh=mesh, in_specs=in_specs, out_specs=out_specs, check_vma=False
    )
```

```python
import math

import jax
import jax.numpy as jnp
import numpy as np
from jax import lax
from jax.experimental import pallas as pl
from jax.experimental.pallas import tpu as pltpu
from jax.sharding import PartitionSpec as P


SIDE = 16
DEVICES = ("grp", "tile")
LANES = 128
EDGE = 256


def swap(block, step):
    count = lax.axis_size(DEVICES)
    route = [(i, (i + step if i % 2 else i - step) % count) for i in range(count)]
    return lax.ppermute(block, DEVICES, route)


def transform_table(side):
    index = np.arange(side * side)
    rows, cols = index // side, index % side
    turns = (rows[:, None] * rows[None, :] + cols[:, None] * cols[None, :]) % side
    angle = turns.astype(np.float32) * np.float32(2.0 * math.pi / side)
    cosine, sine = np.cos(angle), np.sin(angle)
    table = np.concatenate(
        [np.concatenate([cosine, -sine], 1), np.concatenate([sine, cosine], 1)], 0
    )
    return jnp.asarray(table.T.astype(jnp.bfloat16))


def sine_cosine(angle):
    turns = jnp.floor(angle * np.float32(2.0 / math.pi) + 0.5)
    rest = angle - turns * np.float32(1.5703125)
    rest = rest - turns * np.float32(4.837512969970703125e-4)
    rest = rest - turns * np.float32(7.54978995489188216e-8)
    sq = rest * rest
    sine = (np.float32(-1.9515295891e-4) * sq + np.float32(8.3321608736e-3)) * sq
    sine = (sine - np.float32(1.6666654611e-1)) * sq * rest + rest
    cosine = (np.float32(2.443315711809948e-5) * sq - np.float32(1.388731625493765e-3)) * sq
    cosine = (cosine + np.float32(4.166664568298827e-2)) * sq * sq - np.float32(0.5) * sq + 1.0
    quarter = turns.astype(jnp.int32)
    odd = (quarter & 1) == 1
    out_sine = jnp.where(odd, cosine, sine)
    out_cosine = jnp.where(odd, sine, cosine)
    out_sine = jnp.where((quarter & 2) == 2, -out_sine, out_sine)
    out_cosine = jnp.where(((quarter + 1) & 2) == 2, -out_cosine, out_cosine)
    return out_sine, out_cosine


def offsets_of(foot_rows, start, total):
    away = foot_rows - start
    away = jnp.where(away < -(total // 2), away + total, away)
    away = jnp.where(away >= total // 2, away - total, away)
    away = away.astype(jnp.float32)
    foot, subs = away.shape
    filled = jnp.concatenate([away, jnp.zeros((8 - foot, subs), jnp.float32)], 0)
    return filled.T.astype(jnp.int32)


def hits(column, first, count):
    column = jnp.broadcast_to(column, (column.shape[0], LANES)).astype(jnp.int16)
    lane = lax.broadcasted_iota(jnp.int16, column.shape, 1)
    one, zero = jnp.bfloat16(1), jnp.bfloat16(0)
    parts = [
        jnp.where(lane == column - jnp.int16(first + b), one, zero)
        for b in range(0, count, LANES)
    ]
    return jnp.concatenate(parts, 1)


def edges(
    screens_ref, matrix_ref, cols_hbm, owner_hbm, outer_ref, inner_ref, cm_ref, picks_ref, spot_ref,
    cols_ref, owner_ref, sems, *, columns, mirrors
):
    layers, blocks, _ = screens_ref.shape
    last = (blocks // EDGE - 1) * EDGE
    odd = lax.axis_index("tile") % 2
    outer = pl.multiple_of(odd * last, EDGE)
    inner = pl.multiple_of((1 - odd) * last, EDGE)
    copies = []
    for first, ref in ((outer, outer_ref), (inner, inner_ref)):
        for layer in range(layers):
            block = screens_ref.at[layer, pl.ds(first, EDGE)]
            copies.append(pltpu.make_async_copy(block, ref.at[layer], sems.at[len(copies)]))
    copies.append(pltpu.make_async_copy(matrix_ref, cm_ref, sems.at[len(copies)]))
    small = [
        pltpu.make_async_copy(cols_hbm, cols_ref, sems.at[len(copies)]),
        pltpu.make_async_copy(owner_hbm, owner_ref, sems.at[len(copies) + 1]),
    ]
    for copy in small + copies:
        copy.start()
    positions, rowblk = cols_ref.shape
    acts = owner_ref.shape[1]
    rb = acts // rowblk
    act = lax.broadcasted_iota(jnp.int32, (acts, LANES), 0)
    wide = lax.broadcasted_iota(jnp.int32, (acts, LANES), 1)
    over = jnp.where(act % rb == (wide % (2 * rb)) // 2, 1.0, 0.0).astype(jnp.bfloat16)
    for copy in small:
        copy.wait()
    cols = (cols_ref[...] - lax.axis_index("grp") * columns).astype(jnp.float32)
    lane = lax.broadcasted_iota(jnp.int32, (positions, LANES), 1)
    place = lax.broadcasted_iota(jnp.int32, (positions, LANES), 0)
    spread = jnp.where(lane // (2 * rb) == place, 1.0, 0.0)
    cols = lax.dot_general(
        cols, spread, (((0,), (0,)), ((), ())), preferred_element_type=jnp.float32
    ).astype(jnp.int32)
    comp = lax.broadcasted_iota(jnp.int32, cols.shape, 1) % 2
    height = spot_ref.shape[0]
    spot_ref[...] = jnp.concatenate(
        [cols * 2 + comp, jnp.full((height - rowblk, LANES), -1, jnp.int32)], 0
    )
    act = lax.broadcasted_iota(jnp.int32, (rowblk, acts), 1)
    block = lax.broadcasted_iota(jnp.int32, (rowblk, acts), 0)
    held = jnp.where(act // rb == block, owner_ref[...], 0)
    held = held.astype(jnp.float32).astype(jnp.bfloat16)
    owners = jnp.dot(held, over, preferred_element_type=jnp.float32)
    target = cols * (2 * mirrors) + comp * mirrors + owners.astype(jnp.int32)
    row = lax.broadcasted_iota(jnp.int16, (picks_ref.shape[0], LANES), 0)
    one, zero = jnp.bfloat16(1), jnp.bfloat16(0)
    for i in range(rowblk):
        named = jnp.broadcast_to(target[i : i + 1, :], row.shape).astype(jnp.int16)
        picks_ref[:, i * LANES : (i + 1) * LANES] = jnp.where(row == named, one, zero)
    for copy in copies:
        copy.wait()


def mirror_rows(
    gain_ref, owner_ref, prev_ref, picks_ref, cm_ref, sent_ref, state_ref, extra_ref, half_ref, sems
):
    tiles, threes, fours, _ = sent_ref.shape
    mirrors = gain_ref.shape[0]
    acts = owner_ref.shape[1]
    half = tiles // 2
    rows = half * threes * fours
    copies = []
    for part in range(2):
        sums = jnp.dot(
            picks_ref[part * rows : (part + 1) * rows, :],
            cm_ref[...],
            preferred_element_type=jnp.float32,
        )
        for t in range(half):
            for j in range(threes):
                at = (t * threes + j) * fours
                half_ref[part * half + t, j] = sums[at : at + fours]
        span = pl.ds(part * half, half)
        copies.append(
            pltpu.make_async_copy(half_ref.at[span], sent_ref.at[span], sems.at[part])
        )
        copies[part].start()
    owner = owner_ref[...]
    lane = lax.broadcasted_iota(jnp.int32, (1, LANES), 1)
    extra = jnp.zeros((1, LANES), jnp.float32)
    gain = jnp.zeros(owner.shape, jnp.float32)
    for m in range(mirrors):
        mine = owner == m
        gain = jnp.where(mine, gain_ref[m], gain)
        prev = jnp.sum(jnp.where(mine, prev_ref[...], 0.0), axis=1, keepdims=True)
        number = jnp.sum(jnp.where(mine, 1.0, 0.0), axis=1, keepdims=True)
        extra = jnp.where(lane == mirrors + m, prev, extra)
        extra = jnp.where(lane == 2 * mirrors + m, number, extra)
    extra_ref[...] = extra
    lines = state_ref.shape[0] // 3
    missing = lines * LANES - acts
    rows = []
    for values, fill in ((owner.astype(jnp.float32), -1.0), (prev_ref[...], 0.0), (gain, 0.0)):
        values = jnp.concatenate([values, jnp.full((1, missing), fill, jnp.float32)], 1)
        rows += [values[:, i * LANES : (i + 1) * LANES] for i in range(lines)]
    state_ref[...] = jnp.concatenate(rows, 0)
    for copy in copies:
        copy.wait()


def pick_own(foot_ref, screens_ref, inner_ref, picked_ref, *, total):
    layers, foot, _ = foot_ref.shape
    blocks, pixels = screens_ref.shape[1:]
    start = lax.axis_index(DEVICES) * blocks
    first = (1 - lax.axis_index("tile") % 2) * (blocks + EDGE) - EDGE
    for layer in range(layers):
        offsets = offsets_of(foot_ref[layer], start, total)
        for k in range(foot):
            column = offsets[:, k : k + 1]
            rows = jnp.dot(
                hits(column, 0, blocks), screens_ref[layer], preferred_element_type=jnp.float32
            )
            rows = rows + jnp.dot(
                hits(column - first, 0, EDGE),
                inner_ref[layer],
                preferred_element_type=jnp.float32,
            )
            picked_ref[layer, :, k * pixels : (k + 1) * pixels] = rows.astype(jnp.bfloat16)


def sense_rest(
    foot_ref, outer_ref, weights_ref, own_ref, illum_ref, table_ref, slopes_ref, words_ref, *,
    total, blocks
):
    layers, foot, subs = foot_ref.shape
    pixels = illum_ref.shape[1]
    start = lax.axis_index(DEVICES) * blocks
    first = (lax.axis_index("tile") % 2) * (blocks + EDGE) - EDGE
    phase = None
    for layer in range(layers):
        offsets = offsets_of(foot_ref[layer], start, total)
        picked = []
        for k in range(foot):
            found = hits(offsets[:, k : k + 1] - first, 0, EDGE)
            rows = jnp.dot(found, outer_ref[layer], preferred_element_type=jnp.float32)
            own = own_ref[layer, :, k * pixels : (k + 1) * pixels]
            picked.append(rows.astype(jnp.bfloat16) + own)
        part = jnp.dot(
            jnp.concatenate(picked, 1),
            weights_ref[layer].reshape(foot * pixels, pixels),
            preferred_element_type=jnp.float32,
        )
        phase = part if phase is None else phase + part
    phase = phase.T
    illum = illum_ref[...].T
    sine, cosine = sine_cosine(phase)
    field = jnp.concatenate([illum * cosine, illum * sine], 0).astype(jnp.bfloat16)
    spectrum = jnp.dot(table_ref[...], field, preferred_element_type=jnp.float32)
    real_part = spectrum[:pixels]
    imag_part = spectrum[pixels:]
    intensity = real_part * real_part + imag_part * imag_part
    row = lax.broadcasted_iota(jnp.int32, intensity.shape, 0)
    cv = row % SIDE
    cu = row // SIDE
    cv = (cv - SIDE * (cv >= SIDE // 2).astype(jnp.int32)).astype(jnp.float32)
    cu = (cu - SIDE * (cu >= SIDE // 2).astype(jnp.int32)).astype(jnp.float32)
    whole = jnp.sum(intensity, axis=0, keepdims=True)
    slope_x = jnp.sum(intensity * cv, axis=0, keepdims=True) / whole
    slope_y = jnp.sum(intensity * cu, axis=0, keepdims=True) / whole
    slopes = jnp.concatenate([slope_x, slope_y], 0)
    slopes_ref[...] = slopes
    words = slopes.astype(jnp.bfloat16).astype(jnp.float32)
    words = [words[:, h * LANES : (h + 1) * LANES] for h in range(subs // LANES)]
    words_ref[...] = jnp.concatenate(words, 0)


def pack(words_ref, rows_ref, extra_ref, sent_ref, *, mirrors):
    words = words_ref[...]
    sums = jnp.sum(rows_ref[...], axis=0)
    lane = lax.broadcasted_iota(jnp.int32, (1, LANES), 1)
    line = extra_ref[...]
    for m in range(mirrors):
        product = jnp.zeros((1, LANES), jnp.float32)
        for k in range(words.shape[0]):
            at = k * mirrors + m
            row = sums[at // sums.shape[1], at % sums.shape[1]][None]
            product = product + row * words[k : k + 1]
        line = jnp.where(lane == m, jnp.sum(product, axis=1, keepdims=True), line)
    high = line.astype(jnp.bfloat16).astype(jnp.float32)
    middle = (line - high).astype(jnp.bfloat16).astype(jnp.float32)
    low = line - high - middle
    rows = jnp.concatenate([words, high, middle, low, jnp.zeros_like(low)], 0)
    sent_ref[...] = jnp.broadcast_to(rows.astype(jnp.bfloat16)[None], sent_ref.shape)


def reconstruct(words_ref, cm_ref, spot_ref, sent_ref, *, rb):
    got = words_ref[...].astype(jnp.float32)
    words = got[:, :4, :].reshape(-1, LANES).astype(jnp.bfloat16)
    line = jnp.sum(got, axis=0)
    line = line[4:5] + line[5:6] + line[6:7]
    rowblk = cm_ref.shape[0] // LANES
    row = lax.broadcasted_iota(jnp.int32, (words.shape[0], LANES), 0)
    parts = []
    for i in range(rowblk):
        product = lax.dot_general(
            words,
            cm_ref[i * LANES : (i + 1) * LANES, :],
            (((1,), (1,)), ((), ())),
            preferred_element_type=jnp.float32,
        )
        chosen = jnp.where(row == spot_ref[i : i + 1, :], product, 0.0)
        parts.append(jnp.sum(chosen, axis=0, keepdims=True))
    height = spot_ref.shape[0]
    if height > rowblk:
        parts.append(jnp.zeros((height - rowblk, LANES), jnp.float32))
    parts = jnp.concatenate(parts, 0)
    source = lax.broadcasted_iota(jnp.int32, (LANES, LANES), 0)
    lane = lax.broadcasted_iota(jnp.int32, (LANES, LANES), 1)
    fold = jnp.where((source % (2 * rb)) // 2 == lane % rb, 1.0, 0.0)
    spread = jnp.dot(
        parts, fold, preferred_element_type=jnp.float32, precision=lax.Precision.HIGHEST
    )
    per = LANES // rb
    block = lax.broadcasted_iota(jnp.int32, spread.shape, 0)
    lane = lax.broadcasted_iota(jnp.int32, spread.shape, 1)
    spread = jnp.where(lane // rb == block % per, spread, 0.0)
    recon = jnp.sum(spread.reshape(height // per, per, LANES), axis=1)
    rest = sent_ref.shape[1] - recon.shape[0] - 1
    rows = jnp.concatenate([recon, line, jnp.zeros((rest, LANES), jnp.float32)], 0)
    sent_ref[...] = jnp.broadcast_to(rows[None], sent_ref.shape)


def settle(got_ref, state_ref, found_ref, slopes_ref, commands_ref, *, mirrors):
    slopes_ref[...] = found_ref[...]
    lines = state_ref.shape[0] // 3
    sums = jnp.sum(got_ref[...], axis=0)
    line = sums[lines : lines + 1]
    share = 1.0 / got_ref.shape[0]
    lane = lax.broadcasted_iota(jnp.int32, line.shape, 1)

    def entry(at):
        return jnp.sum(jnp.where(lane == at, line, 0.0), axis=1, keepdims=True)

    owner = state_ref[:lines]
    gain = state_ref[2 * lines :]
    piston = jnp.zeros(owner.shape, jnp.float32)
    for m in range(mirrors):
        total = share * entry(mirrors + m) - gain * entry(m)
        count = share * entry(2 * mirrors + m)
        piston = jnp.where(owner == float(m), total / count, piston)
    commands = state_ref[lines : 2 * lines] - gain * sums[:lines] - piston
    acts = commands_ref.shape[0]
    for i in range(lines):
        some = min(LANES, acts - i * LANES)
        commands_ref[i * LANES : i * LANES + some] = commands[i, :some]


def on_device(
    screens,
    interp_weights,
    footprint,
    illumination,
    cm_values,
    cm_columns,
    prev_commands,
    owner_map,
    dm_gain,
):
    layers, blk_dev, pixels = screens.shape
    subs, _, foot = footprint.shape
    groups, tiles = lax.axis_size("grp"), lax.axis_size("tile")
    total = blk_dev * groups * tiles
    rowblk, positions, rb, comps, cbs = cm_values.shape
    acts = rowblk * rb
    mirrors = dm_gain.shape[0]
    height = -(-acts // LANES) * LANES // rb
    lines = height * rb // LANES
    smem = pl.BlockSpec(memory_space=pltpu.SMEM)
    vmem = pl.BlockSpec(memory_space=pltpu.VMEM)
    limit = pltpu.CompilerParams(vmem_limit_bytes=24 * 2**20)
    f32 = jnp.float32

    edge = jax.ShapeDtypeStruct((layers, EDGE, pixels), screens.dtype)
    hbm = pl.BlockSpec(memory_space=pltpu.HBM)
    cm = cm_values.reshape(rowblk * positions * rb * comps, cbs)
    held = owner_map.reshape(1, acts)
    sums = 4 * mirrors

    def stay(array):
        return pltpu.with_memory_space_constraint(array, pltpu.HBM)

    outer, inner, loaded, picks, spot = pl.pallas_call(
        lambda *refs: edges(*refs, columns=tiles * subs // cbs, mirrors=mirrors),
        in_specs=[hbm] * 4,
        out_specs=[vmem] * 5,
        out_shape=[
            edge,
            edge,
            jax.ShapeDtypeStruct(cm.shape, cm.dtype),
            jax.ShapeDtypeStruct((tiles * sums, cm.shape[0]), jnp.bfloat16),
            jax.ShapeDtypeStruct((height, LANES), jnp.int32),
        ],
        scratch_shapes=[
            pltpu.VMEM((positions, rowblk), jnp.int32),
            pltpu.VMEM((1, acts), jnp.int32),
            pltpu.SemaphoreType.DMA((2 * layers + 3,)),
        ],
        compiler_params=limit,
        name="edges",
    )(stay(screens), stay(cm), stay(cm_columns.T), stay(held))
    outer = swap(outer, 1)
    inner = swap(inner, -1)

    rows, state, extra = pl.pallas_call(
        mirror_rows,
        in_specs=[smem] + [vmem] * 4,
        out_specs=[hbm, vmem, vmem],
        out_shape=(
            jax.ShapeDtypeStruct((tiles, sums // 4, 4, LANES), f32),
            jax.ShapeDtypeStruct((3 * lines, LANES), f32),
            jax.ShapeDtypeStruct((1, LANES), f32),
        ),
        scratch_shapes=[
            pltpu.VMEM((tiles, sums // 4, 4, LANES), f32),
            pltpu.SemaphoreType.DMA((2,)),
        ],
        compiler_params=limit,
        name="mirror_rows",
    )(dm_gain, held, prev_commands.reshape(1, acts), picks, loaded)
    foot_rows = jnp.transpose(footprint, (1, 2, 0))
    rows, foot_rows = lax.optimization_barrier((rows, foot_rows))
    rows = lax.all_to_all(rows, "tile", 0, 0)

    picked = pl.pallas_call(
        lambda *refs: pick_own(*refs, total=total),
        in_specs=[vmem] * 3,
        out_shape=jax.ShapeDtypeStruct((layers, subs, foot * pixels), screens.dtype),
        compiler_params=limit,
        name="pick_own",
    )(foot_rows, screens, inner)
    slopes, words = pl.pallas_call(
        lambda *refs: sense_rest(*refs, total=total, blocks=blk_dev),
        in_specs=[vmem] * 6,
        out_shape=(
            jax.ShapeDtypeStruct((2, subs), f32),
            jax.ShapeDtypeStruct((2 * subs // LANES, LANES), f32),
        ),
        compiler_params=limit,
        name="sense_rest",
    )(
        foot_rows, outer, interp_weights, picked, illumination, transform_table(SIDE)
    )
    packed = pl.pallas_call(
        lambda *refs: pack(*refs, mirrors=mirrors),
        in_specs=[vmem] * 3,
        out_shape=jax.ShapeDtypeStruct((tiles, 8, LANES), jnp.bfloat16),
        compiler_params=limit,
        name="pack",
    )(words, rows, extra)

    gathered = lax.all_to_all(packed, "tile", 0, 0)
    sent = pl.pallas_call(
        lambda *refs: reconstruct(*refs, rb=rb),
        in_specs=[vmem] * 3,
        out_shape=jax.ShapeDtypeStruct((groups, 8, LANES), f32),
        compiler_params=limit,
        name="reconstruct",
    )(gathered, cm, spot)
    got = lax.all_to_all(sent, "grp", 0, 0)
    return pl.pallas_call(
        lambda *refs: settle(*refs, mirrors=mirrors),
        in_specs=[vmem] * 3,
        out_shape=(
            jax.ShapeDtypeStruct((2, subs), f32),
            jax.ShapeDtypeStruct((acts,), f32),
        ),
        compiler_params=limit,
        name="settle",
    )(got, state, slopes)


def solution(mesh):
    in_specs = (
        P(None, ("grp", "tile"), None),
        P(),
        P(("grp", "tile"), None, None),
        P(("grp", "tile"), None),
        P("tile", "grp", None, None, None),
        P("tile", "grp"),
        P("tile"),
        P("tile"),
        P(),
    )
    out_specs = (P(None, ("grp", "tile")), P("tile"))
    return jax.shard_map(
        on_device, mesh=mesh, in_specs=in_specs, out_specs=out_specs, check_vma=False
    )
```

```python
import math

import jax
import jax.numpy as jnp
import numpy as np
from jax import lax
from jax.experimental import pallas as pl
from jax.experimental.pallas import tpu as pltpu
from jax.sharding import PartitionSpec as P


SIDE = 16
DEVICES = ("grp", "tile")
LANES = 128
EDGE = 256


def swap(block, step):
    count = lax.axis_size(DEVICES)
    route = [(i, (i + step if i % 2 else i - step) % count) for i in range(count)]
    return lax.ppermute(block, DEVICES, route)


def transform_table(side):
    index = np.arange(side * side)
    rows, cols = index // side, index % side
    turns = (rows[:, None] * rows[None, :] + cols[:, None] * cols[None, :]) % side
    angle = turns.astype(np.float32) * np.float32(2.0 * math.pi / side)
    cosine, sine = np.cos(angle), np.sin(angle)
    table = np.concatenate(
        [np.concatenate([cosine, -sine], 1), np.concatenate([sine, cosine], 1)], 0
    )
    return jnp.asarray(table.T.astype(jnp.bfloat16))


def sine_cosine(angle):
    turns = jnp.floor(angle * np.float32(2.0 / math.pi) + 0.5)
    rest = angle - turns * np.float32(1.5703125)
    rest = rest - turns * np.float32(4.837512969970703125e-4)
    rest = rest - turns * np.float32(7.54978995489188216e-8)
    sq = rest * rest
    sine = (np.float32(-1.9515295891e-4) * sq + np.float32(8.3321608736e-3)) * sq
    sine = (sine - np.float32(1.6666654611e-1)) * sq * rest + rest
    cosine = (np.float32(2.443315711809948e-5) * sq - np.float32(1.388731625493765e-3)) * sq
    cosine = (cosine + np.float32(4.166664568298827e-2)) * sq * sq - np.float32(0.5) * sq + 1.0
    quarter = turns.astype(jnp.int32)
    odd = (quarter & 1) == 1
    out_sine = jnp.where(odd, cosine, sine)
    out_cosine = jnp.where(odd, sine, cosine)
    out_sine = jnp.where((quarter & 2) == 2, -out_sine, out_sine)
    out_cosine = jnp.where(((quarter + 1) & 2) == 2, -out_cosine, out_cosine)
    return out_sine, out_cosine


def offsets_of(foot_rows, start, total):
    away = foot_rows - start
    away = jnp.where(away < -(total // 2), away + total, away)
    away = jnp.where(away >= total // 2, away - total, away)
    away = away.astype(jnp.float32)
    foot, subs = away.shape
    filled = jnp.concatenate([away, jnp.zeros((8 - foot, subs), jnp.float32)], 0)
    return filled.T.astype(jnp.int32)


def hits(column, first, count):
    column = jnp.broadcast_to(column, (column.shape[0], LANES)).astype(jnp.int16)
    lane = lax.broadcasted_iota(jnp.int16, column.shape, 1)
    one, zero = jnp.bfloat16(1), jnp.bfloat16(0)
    parts = [
        jnp.where(lane == column - jnp.int16(first + b), one, zero)
        for b in range(0, count, LANES)
    ]
    return jnp.concatenate(parts, 1)


def edges(
    screens_ref, matrix_ref, cols_hbm, owner_hbm, outer_ref, inner_ref, cm_ref, picks_ref, spot_ref,
    cols_ref, owner_ref, sems, *, columns, mirrors
):
    layers, blocks, _ = screens_ref.shape
    last = (blocks // EDGE - 1) * EDGE
    odd = lax.axis_index("tile") % 2
    outer = pl.multiple_of(odd * last, EDGE)
    inner = pl.multiple_of((1 - odd) * last, EDGE)
    copies = []
    for first, ref in ((outer, outer_ref), (inner, inner_ref)):
        for layer in range(layers):
            block = screens_ref.at[layer, pl.ds(first, EDGE)]
            copies.append(pltpu.make_async_copy(block, ref.at[layer], sems.at[len(copies)]))
    copies.append(pltpu.make_async_copy(matrix_ref, cm_ref, sems.at[len(copies)]))
    small = [
        pltpu.make_async_copy(cols_hbm, cols_ref, sems.at[len(copies)]),
        pltpu.make_async_copy(owner_hbm, owner_ref, sems.at[len(copies) + 1]),
    ]
    for copy in small + copies:
        copy.start()
    positions, rowblk = cols_ref.shape
    acts = owner_ref.shape[1]
    rb = acts // rowblk
    act = lax.broadcasted_iota(jnp.int32, (acts, LANES), 0)
    wide = lax.broadcasted_iota(jnp.int32, (acts, LANES), 1)
    over = jnp.where(act % rb == (wide % (2 * rb)) // 2, 1.0, 0.0).astype(jnp.bfloat16)
    for copy in small:
        copy.wait()
    cols = (cols_ref[...] - lax.axis_index("grp") * columns).astype(jnp.float32)
    lane = lax.broadcasted_iota(jnp.int32, (positions, LANES), 1)
    place = lax.broadcasted_iota(jnp.int32, (positions, LANES), 0)
    spread = jnp.where(lane // (2 * rb) == place, 1.0, 0.0)
    cols = lax.dot_general(
        cols, spread, (((0,), (0,)), ((), ())), preferred_element_type=jnp.float32
    ).astype(jnp.int32)
    comp = lax.broadcasted_iota(jnp.int32, cols.shape, 1) % 2
    height = spot_ref.shape[0]
    spot_ref[...] = jnp.concatenate(
        [cols * 2 + comp, jnp.full((height - rowblk, LANES), -1, jnp.int32)], 0
    )
    act = lax.broadcasted_iota(jnp.int32, (rowblk, acts), 1)
    block = lax.broadcasted_iota(jnp.int32, (rowblk, acts), 0)
    held = jnp.where(act // rb == block, owner_ref[...], 0)
    held = held.astype(jnp.float32).astype(jnp.bfloat16)
    owners = jnp.dot(held, over, preferred_element_type=jnp.float32)
    target = cols * (2 * mirrors) + comp * mirrors + owners.astype(jnp.int32)
    row = lax.broadcasted_iota(jnp.int16, (picks_ref.shape[0], LANES), 0)
    one, zero = jnp.bfloat16(1), jnp.bfloat16(0)
    for i in range(rowblk):
        named = jnp.broadcast_to(target[i : i + 1, :], row.shape).astype(jnp.int16)
        picks_ref[:, i * LANES : (i + 1) * LANES] = jnp.where(row == named, one, zero)
    for copy in copies:
        copy.wait()


def mirror_rows(
    gain_ref, owner_ref, prev_ref, picks_ref, cm_ref, sent_ref, state_ref, extra_ref, half_ref, sems
):
    tiles, threes, fours, _ = sent_ref.shape
    mirrors = gain_ref.shape[0]
    acts = owner_ref.shape[1]
    half = tiles // 2
    rows = half * threes * fours
    copies = []
    for part in range(2):
        sums = jnp.dot(
            picks_ref[part * rows : (part + 1) * rows, :],
            cm_ref[...],
            preferred_element_type=jnp.float32,
        )
        for t in range(half):
            for j in range(threes):
                at = (t * threes + j) * fours
                half_ref[part * half + t, j] = sums[at : at + fours]
        span = pl.ds(part * half, half)
        copies.append(
            pltpu.make_async_copy(half_ref.at[span], sent_ref.at[span], sems.at[part])
        )
        copies[part].start()
    owner = owner_ref[...]
    lane = lax.broadcasted_iota(jnp.int32, (1, LANES), 1)
    extra = jnp.zeros((1, LANES), jnp.float32)
    gain = jnp.zeros(owner.shape, jnp.float32)
    for m in range(mirrors):
        mine = owner == m
        gain = jnp.where(mine, gain_ref[m], gain)
        prev = jnp.sum(jnp.where(mine, prev_ref[...], 0.0), axis=1, keepdims=True)
        number = jnp.sum(jnp.where(mine, 1.0, 0.0), axis=1, keepdims=True)
        extra = jnp.where(lane == mirrors + m, prev, extra)
        extra = jnp.where(lane == 2 * mirrors + m, number, extra)
    extra_ref[...] = extra
    lines = state_ref.shape[0] // 3
    missing = lines * LANES - acts
    rows = []
    for values, fill in ((owner.astype(jnp.float32), -1.0), (prev_ref[...], 0.0), (gain, 0.0)):
        values = jnp.concatenate([values, jnp.full((1, missing), fill, jnp.float32)], 1)
        rows += [values[:, i * LANES : (i + 1) * LANES] for i in range(lines)]
    state_ref[...] = jnp.concatenate(rows, 0)
    for copy in copies:
        copy.wait()


def pick_own(foot_ref, screens_ref, inner_ref, picked_ref, *, total):
    layers, foot, _ = foot_ref.shape
    blocks, pixels = screens_ref.shape[1:]
    start = lax.axis_index(DEVICES) * blocks
    first = (1 - lax.axis_index("tile") % 2) * (blocks + EDGE) - EDGE
    for layer in range(layers):
        offsets = offsets_of(foot_ref[layer], start, total)
        for k in range(foot):
            column = offsets[:, k : k + 1]
            rows = jnp.dot(
                hits(column, 0, blocks), screens_ref[layer], preferred_element_type=jnp.float32
            )
            rows = rows + jnp.dot(
                hits(column - first, 0, EDGE),
                inner_ref[layer],
                preferred_element_type=jnp.float32,
            )
            picked_ref[layer, :, k * pixels : (k + 1) * pixels] = rows.astype(jnp.bfloat16)


def sense_rest(
    foot_ref, outer_ref, weights_ref, own_ref, illum_ref, table_ref, slopes_ref, words_ref, *,
    total, blocks
):
    layers, foot, subs = foot_ref.shape
    pixels = illum_ref.shape[1]
    start = lax.axis_index(DEVICES) * blocks
    first = (lax.axis_index("tile") % 2) * (blocks + EDGE) - EDGE
    phase = None
    for layer in range(layers):
        offsets = offsets_of(foot_ref[layer], start, total)
        for k in range(foot):
            found = hits(offsets[:, k : k + 1] - first, 0, EDGE)
            rows = jnp.dot(found, outer_ref[layer], preferred_element_type=jnp.float32)
            rows = rows.astype(jnp.bfloat16) + own_ref[layer, :, k * pixels : (k + 1) * pixels]
            part = jnp.dot(rows, weights_ref[layer, k], preferred_element_type=jnp.float32)
            phase = part if phase is None else phase + part
    phase = phase.T
    illum = illum_ref[...].T
    sine, cosine = sine_cosine(phase)
    field = jnp.concatenate([illum * cosine, illum * sine], 0).astype(jnp.bfloat16)
    spectrum = jnp.dot(table_ref[...], field, preferred_element_type=jnp.float32)
    real_part = spectrum[:pixels]
    imag_part = spectrum[pixels:]
    intensity = real_part * real_part + imag_part * imag_part
    row = lax.broadcasted_iota(jnp.int32, intensity.shape, 0)
    cv = row % SIDE
    cu = row // SIDE
    cv = (cv - SIDE * (cv >= SIDE // 2).astype(jnp.int32)).astype(jnp.float32)
    cu = (cu - SIDE * (cu >= SIDE // 2).astype(jnp.int32)).astype(jnp.float32)
    whole = jnp.sum(intensity, axis=0, keepdims=True)
    slope_x = jnp.sum(intensity * cv, axis=0, keepdims=True) / whole
    slope_y = jnp.sum(intensity * cu, axis=0, keepdims=True) / whole
    slopes = jnp.concatenate([slope_x, slope_y], 0)
    slopes_ref[...] = slopes
    words = slopes.astype(jnp.bfloat16).astype(jnp.float32)
    words = [words[:, h * LANES : (h + 1) * LANES] for h in range(subs // LANES)]
    words_ref[...] = jnp.concatenate(words, 0)


def pack(words_ref, rows_ref, extra_ref, sent_ref, *, mirrors):
    words = words_ref[...]
    sums = jnp.sum(rows_ref[...], axis=0)
    lane = lax.broadcasted_iota(jnp.int32, (1, LANES), 1)
    line = extra_ref[...]
    for m in range(mirrors):
        product = jnp.zeros((1, LANES), jnp.float32)
        for k in range(words.shape[0]):
            at = k * mirrors + m
            row = sums[at // sums.shape[1], at % sums.shape[1]][None]
            product = product + row * words[k : k + 1]
        line = jnp.where(lane == m, jnp.sum(product, axis=1, keepdims=True), line)
    high = line.astype(jnp.bfloat16).astype(jnp.float32)
    middle = (line - high).astype(jnp.bfloat16).astype(jnp.float32)
    low = line - high - middle
    rows = jnp.concatenate([words, high, middle, low, jnp.zeros_like(low)], 0)
    sent_ref[...] = jnp.broadcast_to(rows.astype(jnp.bfloat16)[None], sent_ref.shape)


def reconstruct(words_ref, cm_ref, spot_ref, sent_ref, *, rb):
    got = words_ref[...].astype(jnp.float32)
    words = got[:, :4, :].reshape(-1, LANES).astype(jnp.bfloat16)
    line = jnp.sum(got, axis=0)
    line = line[4:5] + line[5:6] + line[6:7]
    rowblk = cm_ref.shape[0] // LANES
    row = lax.broadcasted_iota(jnp.int32, (words.shape[0], LANES), 0)
    parts = []
    step = math.gcd(rowblk, 4)
    for first in range(0, rowblk, step):
        product = lax.dot_general(
            words,
            cm_ref[first * LANES : (first + step) * LANES, :],
            (((1,), (1,)), ((), ())),
            preferred_element_type=jnp.float32,
        )
        for i in range(step):
            spot = spot_ref[first + i : first + i + 1, :]
            chosen = jnp.where(row == spot, product[:, i * LANES : (i + 1) * LANES], 0.0)
            parts.append(jnp.sum(chosen, axis=0, keepdims=True))
    height = spot_ref.shape[0]
    if height > rowblk:
        parts.append(jnp.zeros((height - rowblk, LANES), jnp.float32))
    parts = jnp.concatenate(parts, 0)
    source = lax.broadcasted_iota(jnp.int32, (LANES, LANES), 0)
    lane = lax.broadcasted_iota(jnp.int32, (LANES, LANES), 1)
    fold = jnp.where((source % (2 * rb)) // 2 == lane % rb, 1.0, 0.0)
    spread = jnp.dot(
        parts, fold, preferred_element_type=jnp.float32, precision=lax.Precision.HIGHEST
    )
    per = LANES // rb
    block = lax.broadcasted_iota(jnp.int32, spread.shape, 0)
    lane = lax.broadcasted_iota(jnp.int32, spread.shape, 1)
    spread = jnp.where(lane // rb == block % per, spread, 0.0)
    recon = jnp.sum(spread.reshape(height // per, per, LANES), axis=1)
    rest = sent_ref.shape[1] - recon.shape[0] - 1
    rows = jnp.concatenate([recon, line, jnp.zeros((rest, LANES), jnp.float32)], 0)
    sent_ref[...] = jnp.broadcast_to(rows[None], sent_ref.shape)


def settle(got_ref, state_ref, found_ref, slopes_ref, commands_ref, *, mirrors):
    slopes_ref[...] = found_ref[...]
    lines = state_ref.shape[0] // 3
    sums = jnp.sum(got_ref[...], axis=0)
    line = sums[lines : lines + 1]
    share = 1.0 / got_ref.shape[0]
    lane = lax.broadcasted_iota(jnp.int32, line.shape, 1)

    def entry(at):
        return jnp.sum(jnp.where(lane == at, line, 0.0), axis=1, keepdims=True)

    owner = state_ref[:lines]
    gain = state_ref[2 * lines :]
    piston = jnp.zeros(owner.shape, jnp.float32)
    for m in range(mirrors):
        total = share * entry(mirrors + m) - gain * entry(m)
        count = share * entry(2 * mirrors + m)
        piston = jnp.where(owner == float(m), total / count, piston)
    commands = state_ref[lines : 2 * lines] - gain * sums[:lines] - piston
    acts = commands_ref.shape[0]
    for i in range(lines):
        some = min(LANES, acts - i * LANES)
        commands_ref[i * LANES : i * LANES + some] = commands[i, :some]


def on_device(
    screens,
    interp_weights,
    footprint,
    illumination,
    cm_values,
    cm_columns,
    prev_commands,
    owner_map,
    dm_gain,
):
    layers, blk_dev, pixels = screens.shape
    subs, _, foot = footprint.shape
    groups, tiles = lax.axis_size("grp"), lax.axis_size("tile")
    total = blk_dev * groups * tiles
    rowblk, positions, rb, comps, cbs = cm_values.shape
    acts = rowblk * rb
    mirrors = dm_gain.shape[0]
    height = -(-acts // LANES) * LANES // rb
    lines = height * rb // LANES
    smem = pl.BlockSpec(memory_space=pltpu.SMEM)
    vmem = pl.BlockSpec(memory_space=pltpu.VMEM)
    limit = pltpu.CompilerParams(vmem_limit_bytes=24 * 2**20)
    tight = pltpu.CompilerParams(vmem_limit_bytes=24 * 2**20)
    f32 = jnp.float32

    edge = jax.ShapeDtypeStruct((layers, EDGE, pixels), screens.dtype)
    hbm = pl.BlockSpec(memory_space=pltpu.HBM)
    cm = cm_values.reshape(rowblk * positions * rb * comps, cbs)
    held = owner_map.reshape(1, acts)
    sums = 4 * mirrors

    def stay(array):
        return pltpu.with_memory_space_constraint(array, pltpu.HBM)

    outer, inner, loaded, picks, spot = pl.pallas_call(
        lambda *refs: edges(*refs, columns=tiles * subs // cbs, mirrors=mirrors),
        in_specs=[hbm] * 4,
        out_specs=[vmem] * 5,
        out_shape=[
            edge,
            edge,
            jax.ShapeDtypeStruct(cm.shape, cm.dtype),
            jax.ShapeDtypeStruct((tiles * sums, cm.shape[0]), jnp.bfloat16),
            jax.ShapeDtypeStruct((height, LANES), jnp.int32),
        ],
        scratch_shapes=[
            pltpu.VMEM((positions, rowblk), jnp.int32),
            pltpu.VMEM((1, acts), jnp.int32),
            pltpu.SemaphoreType.DMA((2 * layers + 3,)),
        ],
        compiler_params=limit,
        name="edges",
    )(stay(screens), stay(cm), stay(cm_columns.T), stay(held))
    outer = swap(outer, 1)
    inner = swap(inner, -1)

    rows, state, extra = pl.pallas_call(
        mirror_rows,
        in_specs=[smem] + [vmem] * 4,
        out_specs=[hbm, vmem, vmem],
        out_shape=(
            jax.ShapeDtypeStruct((tiles, sums // 4, 4, LANES), f32),
            jax.ShapeDtypeStruct((3 * lines, LANES), f32),
            jax.ShapeDtypeStruct((1, LANES), f32),
        ),
        scratch_shapes=[
            pltpu.VMEM((tiles, sums // 4, 4, LANES), f32),
            pltpu.SemaphoreType.DMA((2,)),
        ],
        compiler_params=limit,
        name="mirror_rows",
    )(dm_gain, held, prev_commands.reshape(1, acts), picks, loaded)
    foot_rows = jnp.transpose(footprint, (1, 2, 0))
    rows, foot_rows = lax.optimization_barrier((rows, foot_rows))
    rows = lax.all_to_all(rows, "tile", 0, 0)

    picked = pl.pallas_call(
        lambda *refs: pick_own(*refs, total=total),
        in_specs=[vmem] * 3,
        out_shape=jax.ShapeDtypeStruct((layers, subs, foot * pixels), screens.dtype),
        compiler_params=tight,
        name="pick_own",
    )(foot_rows, screens, inner)
    slopes, words = pl.pallas_call(
        lambda *refs: sense_rest(*refs, total=total, blocks=blk_dev),
        in_specs=[vmem] * 6,
        out_shape=(
            jax.ShapeDtypeStruct((2, subs), f32),
            jax.ShapeDtypeStruct((2 * subs // LANES, LANES), f32),
        ),
        compiler_params=limit,
        name="sense_rest",
    )(
        foot_rows, outer, interp_weights, picked, illumination, transform_table(SIDE)
    )
    packed = pl.pallas_call(
        lambda *refs: pack(*refs, mirrors=mirrors),
        in_specs=[vmem] * 3,
        out_shape=jax.ShapeDtypeStruct((tiles, 8, LANES), jnp.bfloat16),
        compiler_params=limit,
        name="pack",
    )(words, rows, extra)

    gathered = lax.all_to_all(packed, "tile", 0, 0)
    sent = pl.pallas_call(
        lambda *refs: reconstruct(*refs, rb=rb),
        in_specs=[vmem] * 3,
        out_shape=jax.ShapeDtypeStruct((groups, 8, LANES), f32),
        compiler_params=limit,
        name="reconstruct",
    )(gathered, cm, spot)
    got = lax.all_to_all(sent, "grp", 0, 0)
    return pl.pallas_call(
        lambda *refs: settle(*refs, mirrors=mirrors),
        in_specs=[vmem] * 3,
        out_shape=(
            jax.ShapeDtypeStruct((2, subs), f32),
            jax.ShapeDtypeStruct((acts,), f32),
        ),
        compiler_params=limit,
        name="settle",
    )(got, state, slopes)


def solution(mesh):
    in_specs = (
        P(None, ("grp", "tile"), None),
        P(),
        P(("grp", "tile"), None, None),
        P(("grp", "tile"), None),
        P("tile", "grp", None, None, None),
        P("tile", "grp"),
        P("tile"),
        P("tile"),
        P(),
    )
    out_specs = (P(None, ("grp", "tile")), P("tile"))
    return jax.shard_map(
        on_device, mesh=mesh, in_specs=in_specs, out_specs=out_specs, check_vma=False
    )
```

```python
import math

import jax
import jax.numpy as jnp
import numpy as np
from jax import lax
from jax.experimental import pallas as pl
from jax.experimental.pallas import tpu as pltpu
from jax.sharding import PartitionSpec as P


SIDE = 16
DEVICES = ("grp", "tile")
LANES = 128
EDGE = 256


def swap(block, step):
    count = lax.axis_size(DEVICES)
    route = [(i, (i + step if i % 2 else i - step) % count) for i in range(count)]
    return lax.ppermute(block, DEVICES, route)


def transform_table(side):
    index = np.arange(side * side)
    rows, cols = index // side, index % side
    turns = (rows[:, None] * rows[None, :] + cols[:, None] * cols[None, :]) % side
    angle = turns.astype(np.float32) * np.float32(2.0 * math.pi / side)
    cosine, sine = np.cos(angle), np.sin(angle)
    table = np.concatenate(
        [np.concatenate([cosine, -sine], 1), np.concatenate([sine, cosine], 1)], 0
    )
    return jnp.asarray(table.T.astype(jnp.bfloat16))


def sine_cosine(angle):
    turns = jnp.floor(angle * np.float32(2.0 / math.pi) + 0.5)
    rest = angle - turns * np.float32(1.5703125)
    rest = rest - turns * np.float32(4.837512969970703125e-4)
    rest = rest - turns * np.float32(7.54978995489188216e-8)
    sq = rest * rest
    sine = (np.float32(-1.9515295891e-4) * sq + np.float32(8.3321608736e-3)) * sq
    sine = (sine - np.float32(1.6666654611e-1)) * sq * rest + rest
    cosine = (np.float32(2.443315711809948e-5) * sq - np.float32(1.388731625493765e-3)) * sq
    cosine = (cosine + np.float32(4.166664568298827e-2)) * sq * sq - np.float32(0.5) * sq + 1.0
    quarter = turns.astype(jnp.int32)
    odd = (quarter & 1) == 1
    out_sine = jnp.where(odd, cosine, sine)
    out_cosine = jnp.where(odd, sine, cosine)
    out_sine = jnp.where((quarter & 2) == 2, -out_sine, out_sine)
    out_cosine = jnp.where(((quarter + 1) & 2) == 2, -out_cosine, out_cosine)
    return out_sine, out_cosine


def offsets_of(foot_rows, start, total):
    away = foot_rows - start
    away = jnp.where(away < -(total // 2), away + total, away)
    away = jnp.where(away >= total // 2, away - total, away)
    away = away.astype(jnp.float32)
    foot, subs = away.shape
    filled = jnp.concatenate([away, jnp.zeros((8 - foot, subs), jnp.float32)], 0)
    return filled.T.astype(jnp.int32)


def hits(column, first, count):
    column = jnp.broadcast_to(column, (column.shape[0], LANES)).astype(jnp.int16)
    lane = lax.broadcasted_iota(jnp.int16, column.shape, 1)
    one, zero = jnp.bfloat16(1), jnp.bfloat16(0)
    parts = [
        jnp.where(lane == column - jnp.int16(first + b), one, zero)
        for b in range(0, count, LANES)
    ]
    return jnp.concatenate(parts, 1)


def edges(
    screens_ref, matrix_ref, cols_hbm, owner_hbm, outer_ref, inner_ref, cm_ref, picks_ref, spot_ref,
    cols_ref, owner_ref, sems, *, columns, mirrors
):
    layers, blocks, _ = screens_ref.shape
    last = (blocks // EDGE - 1) * EDGE
    odd = lax.axis_index("tile") % 2
    outer = pl.multiple_of(odd * last, EDGE)
    inner = pl.multiple_of((1 - odd) * last, EDGE)
    copies = []
    for first, ref in ((outer, outer_ref), (inner, inner_ref)):
        for layer in range(layers):
            block = screens_ref.at[layer, pl.ds(first, EDGE)]
            copies.append(pltpu.make_async_copy(block, ref.at[layer], sems.at[len(copies)]))
    copies.append(pltpu.make_async_copy(matrix_ref, cm_ref, sems.at[len(copies)]))
    small = [
        pltpu.make_async_copy(cols_hbm, cols_ref, sems.at[len(copies)]),
        pltpu.make_async_copy(owner_hbm, owner_ref, sems.at[len(copies) + 1]),
    ]
    for copy in small + copies:
        copy.start()
    positions, rowblk = cols_ref.shape
    acts = owner_ref.shape[1]
    rb = acts // rowblk
    act = lax.broadcasted_iota(jnp.int32, (acts, LANES), 0)
    wide = lax.broadcasted_iota(jnp.int32, (acts, LANES), 1)
    over = jnp.where(act % rb == (wide % (2 * rb)) // 2, 1.0, 0.0).astype(jnp.bfloat16)
    for copy in small:
        copy.wait()
    cols = (cols_ref[...] - lax.axis_index("grp") * columns).astype(jnp.float32)
    lane = lax.broadcasted_iota(jnp.int32, (positions, LANES), 1)
    place = lax.broadcasted_iota(jnp.int32, (positions, LANES), 0)
    spread = jnp.where(lane // (2 * rb) == place, 1.0, 0.0)
    cols = lax.dot_general(
        cols, spread, (((0,), (0,)), ((), ())), preferred_element_type=jnp.float32
    ).astype(jnp.int32)
    comp = lax.broadcasted_iota(jnp.int32, cols.shape, 1) % 2
    height = spot_ref.shape[0]
    spot_ref[...] = jnp.concatenate(
        [cols * 2 + comp, jnp.full((height - rowblk, LANES), -1, jnp.int32)], 0
    )
    act = lax.broadcasted_iota(jnp.int32, (rowblk, acts), 1)
    block = lax.broadcasted_iota(jnp.int32, (rowblk, acts), 0)
    held = jnp.where(act // rb == block, owner_ref[...], 0)
    held = held.astype(jnp.float32).astype(jnp.bfloat16)
    owners = jnp.dot(held, over, preferred_element_type=jnp.float32)
    target = cols * (2 * mirrors) + comp * mirrors + owners.astype(jnp.int32)
    row = lax.broadcasted_iota(jnp.int16, (picks_ref.shape[0], LANES), 0)
    one, zero = jnp.bfloat16(1), jnp.bfloat16(0)
    for i in range(rowblk):
        named = jnp.broadcast_to(target[i : i + 1, :], row.shape).astype(jnp.int16)
        picks_ref[:, i * LANES : (i + 1) * LANES] = jnp.where(row == named, one, zero)
    for copy in copies:
        copy.wait()


def mirror_rows(
    gain_ref, owner_ref, prev_ref, picks_ref, cm_ref, sent_ref, state_ref, extra_ref, half_ref, sems
):
    tiles, threes, fours, _ = sent_ref.shape
    mirrors = gain_ref.shape[0]
    acts = owner_ref.shape[1]
    half = tiles // 2
    rows = half * threes * fours
    copies = []
    for part in range(2):
        sums = jnp.dot(
            picks_ref[part * rows : (part + 1) * rows, :],
            cm_ref[...],
            preferred_element_type=jnp.float32,
        )
        for t in range(half):
            for j in range(threes):
                at = (t * threes + j) * fours
                half_ref[part * half + t, j] = sums[at : at + fours]
        span = pl.ds(part * half, half)
        copies.append(
            pltpu.make_async_copy(half_ref.at[span], sent_ref.at[span], sems.at[part])
        )
        copies[part].start()
    owner = owner_ref[...]
    lane = lax.broadcasted_iota(jnp.int32, (1, LANES), 1)
    extra = jnp.zeros((1, LANES), jnp.float32)
    gain = jnp.zeros(owner.shape, jnp.float32)
    for m in range(mirrors):
        mine = owner == m
        gain = jnp.where(mine, gain_ref[m], gain)
        prev = jnp.sum(jnp.where(mine, prev_ref[...], 0.0), axis=1, keepdims=True)
        number = jnp.sum(jnp.where(mine, 1.0, 0.0), axis=1, keepdims=True)
        extra = jnp.where(lane == mirrors + m, prev, extra)
        extra = jnp.where(lane == 2 * mirrors + m, number, extra)
    extra_ref[...] = extra
    lines = state_ref.shape[0] // 3
    missing = lines * LANES - acts
    rows = []
    for values, fill in ((owner.astype(jnp.float32), -1.0), (prev_ref[...], 0.0), (gain, 0.0)):
        values = jnp.concatenate([values, jnp.full((1, missing), fill, jnp.float32)], 1)
        rows += [values[:, i * LANES : (i + 1) * LANES] for i in range(lines)]
    state_ref[...] = jnp.concatenate(rows, 0)
    for copy in copies:
        copy.wait()


def pick_own(foot_ref, screens_ref, inner_ref, picked_ref, named_ref, *, total):
    layers, foot, _ = foot_ref.shape
    blocks, pixels = screens_ref.shape[1:]
    start = lax.axis_index(DEVICES) * blocks
    odd = lax.axis_index("tile") % 2
    first = (1 - odd) * (blocks + EDGE) - EDGE
    other = odd * (blocks + EDGE) - EDGE
    for layer in range(layers):
        offsets = offsets_of(foot_ref[layer], start, total)
        for k in range(foot):
            column = offsets[:, k : k + 1]
            rows = jnp.dot(
                hits(column, 0, blocks), screens_ref[layer], preferred_element_type=jnp.float32
            )
            rows = rows + jnp.dot(
                hits(column - first, 0, EDGE),
                inner_ref[layer],
                preferred_element_type=jnp.float32,
            )
            picked_ref[layer, :, k * pixels : (k + 1) * pixels] = rows.astype(jnp.bfloat16)
            named_ref[layer, :, k * EDGE : (k + 1) * EDGE] = hits(column - other, 0, EDGE)


def sense_rest(
    named_ref, outer_ref, weights_ref, own_ref, illum_ref, table_ref, slopes_ref, words_ref
):
    layers, foot = weights_ref.shape[:2]
    subs, pixels = illum_ref.shape
    phase = None
    for layer in range(layers):
        for k in range(foot):
            found = named_ref[layer, :, k * EDGE : (k + 1) * EDGE]
            rows = jnp.dot(found, outer_ref[layer], preferred_element_type=jnp.float32)
            rows = rows.astype(jnp.bfloat16) + own_ref[layer, :, k * pixels : (k + 1) * pixels]
            part = jnp.dot(rows, weights_ref[layer, k], preferred_element_type=jnp.float32)
            phase = part if phase is None else phase + part
    phase = phase.T
    illum = illum_ref[...].T
    sine, cosine = sine_cosine(phase)
    field = jnp.concatenate([illum * cosine, illum * sine], 0).astype(jnp.bfloat16)
    spectrum = jnp.dot(table_ref[...], field, preferred_element_type=jnp.float32)
    real_part = spectrum[:pixels]
    imag_part = spectrum[pixels:]
    intensity = real_part * real_part + imag_part * imag_part
    row = lax.broadcasted_iota(jnp.int32, intensity.shape, 0)
    cv = row % SIDE
    cu = row // SIDE
    cv = (cv - SIDE * (cv >= SIDE // 2).astype(jnp.int32)).astype(jnp.float32)
    cu = (cu - SIDE * (cu >= SIDE // 2).astype(jnp.int32)).astype(jnp.float32)
    whole = jnp.sum(intensity, axis=0, keepdims=True)
    slope_x = jnp.sum(intensity * cv, axis=0, keepdims=True) / whole
    slope_y = jnp.sum(intensity * cu, axis=0, keepdims=True) / whole
    slopes = jnp.concatenate([slope_x, slope_y], 0)
    slopes_ref[...] = slopes
    words = slopes.astype(jnp.bfloat16).astype(jnp.float32)
    words = [words[:, h * LANES : (h + 1) * LANES] for h in range(subs // LANES)]
    words_ref[...] = jnp.concatenate(words, 0)


def pack(words_ref, rows_ref, extra_ref, sent_ref, *, mirrors):
    words = words_ref[...]
    sums = jnp.sum(rows_ref[...], axis=0)
    lane = lax.broadcasted_iota(jnp.int32, (1, LANES), 1)
    line = extra_ref[...]
    for m in range(mirrors):
        product = jnp.zeros((1, LANES), jnp.float32)
        for k in range(words.shape[0]):
            at = k * mirrors + m
            row = sums[at // sums.shape[1], at % sums.shape[1]][None]
            product = product + row * words[k : k + 1]
        line = jnp.where(lane == m, jnp.sum(product, axis=1, keepdims=True), line)
    high = line.astype(jnp.bfloat16).astype(jnp.float32)
    middle = (line - high).astype(jnp.bfloat16).astype(jnp.float32)
    low = line - high - middle
    rows = jnp.concatenate([words, high, middle, low, jnp.zeros_like(low)], 0)
    sent_ref[...] = jnp.broadcast_to(rows.astype(jnp.bfloat16)[None], sent_ref.shape)


def reconstruct(words_ref, cm_ref, spot_ref, sent_ref, *, rb):
    got = words_ref[...].astype(jnp.float32)
    words = got[:, :4, :].reshape(-1, LANES).astype(jnp.bfloat16)
    line = jnp.sum(got, axis=0)
    line = line[4:5] + line[5:6] + line[6:7]
    rowblk = cm_ref.shape[0] // LANES
    row = lax.broadcasted_iota(jnp.int32, (words.shape[0], LANES), 0)
    parts = []
    step = math.gcd(rowblk, 4)
    for first in range(0, rowblk, step):
        product = lax.dot_general(
            words,
            cm_ref[first * LANES : (first + step) * LANES, :],
            (((1,), (1,)), ((), ())),
            preferred_element_type=jnp.float32,
        )
        for i in range(step):
            spot = spot_ref[first + i : first + i + 1, :]
            chosen = jnp.where(row == spot, product[:, i * LANES : (i + 1) * LANES], 0.0)
            parts.append(jnp.sum(chosen, axis=0, keepdims=True))
    height = spot_ref.shape[0]
    if height > rowblk:
        parts.append(jnp.zeros((height - rowblk, LANES), jnp.float32))
    parts = jnp.concatenate(parts, 0)
    source = lax.broadcasted_iota(jnp.int32, (LANES, LANES), 0)
    lane = lax.broadcasted_iota(jnp.int32, (LANES, LANES), 1)
    fold = jnp.where((source % (2 * rb)) // 2 == lane % rb, 1.0, 0.0)
    spread = jnp.dot(
        parts, fold, preferred_element_type=jnp.float32, precision=lax.Precision.HIGHEST
    )
    per = LANES // rb
    block = lax.broadcasted_iota(jnp.int32, spread.shape, 0)
    lane = lax.broadcasted_iota(jnp.int32, spread.shape, 1)
    spread = jnp.where(lane // rb == block % per, spread, 0.0)
    recon = jnp.sum(spread.reshape(height // per, per, LANES), axis=1)
    rest = sent_ref.shape[0] - recon.shape[0] - 1
    sent_ref[...] = jnp.concatenate([recon, line, jnp.zeros((rest, LANES), jnp.float32)], 0)


def settle(*refs, mirrors):
    *got_refs, state_ref, found_ref, slopes_ref, commands_ref = refs
    slopes_ref[...] = found_ref[...]
    lines = state_ref.shape[0] // 3
    sums = got_refs[0][...]
    for got_ref in got_refs[1:]:
        sums = sums + got_ref[...]
    line = sums[lines : lines + 1]
    share = 1.0 / len(got_refs)
    lane = lax.broadcasted_iota(jnp.int32, line.shape, 1)

    def entry(at):
        return jnp.sum(jnp.where(lane == at, line, 0.0), axis=1, keepdims=True)

    owner = state_ref[:lines]
    gain = state_ref[2 * lines :]
    piston = jnp.zeros(owner.shape, jnp.float32)
    for m in range(mirrors):
        total = share * entry(mirrors + m) - gain * entry(m)
        count = share * entry(2 * mirrors + m)
        piston = jnp.where(owner == float(m), total / count, piston)
    commands = state_ref[lines : 2 * lines] - gain * sums[:lines] - piston
    acts = commands_ref.shape[0]
    for i in range(lines):
        some = min(LANES, acts - i * LANES)
        commands_ref[i * LANES : i * LANES + some] = commands[i, :some]


def on_device(
    screens,
    interp_weights,
    footprint,
    illumination,
    cm_values,
    cm_columns,
    prev_commands,
    owner_map,
    dm_gain,
):
    layers, blk_dev, pixels = screens.shape
    subs, _, foot = footprint.shape
    groups, tiles = lax.axis_size("grp"), lax.axis_size("tile")
    total = blk_dev * groups * tiles
    rowblk, positions, rb, comps, cbs = cm_values.shape
    acts = rowblk * rb
    mirrors = dm_gain.shape[0]
    height = -(-acts // LANES) * LANES // rb
    lines = height * rb // LANES
    smem = pl.BlockSpec(memory_space=pltpu.SMEM)
    vmem = pl.BlockSpec(memory_space=pltpu.VMEM)
    limit = pltpu.CompilerParams(vmem_limit_bytes=24 * 2**20)
    tight = pltpu.CompilerParams(vmem_limit_bytes=24 * 2**20)
    f32 = jnp.float32

    edge = jax.ShapeDtypeStruct((layers, EDGE, pixels), screens.dtype)
    hbm = pl.BlockSpec(memory_space=pltpu.HBM)
    cm = cm_values.reshape(rowblk * positions * rb * comps, cbs)
    held = owner_map.reshape(1, acts)
    sums = 4 * mirrors

    def stay(array):
        return pltpu.with_memory_space_constraint(array, pltpu.HBM)

    outer, inner, loaded, picks, spot = pl.pallas_call(
        lambda *refs: edges(*refs, columns=tiles * subs // cbs, mirrors=mirrors),
        in_specs=[hbm] * 4,
        out_specs=[vmem] * 5,
        out_shape=[
            edge,
            edge,
            jax.ShapeDtypeStruct(cm.shape, cm.dtype),
            jax.ShapeDtypeStruct((tiles * sums, cm.shape[0]), jnp.bfloat16),
            jax.ShapeDtypeStruct((height, LANES), jnp.int32),
        ],
        scratch_shapes=[
            pltpu.VMEM((positions, rowblk), jnp.int32),
            pltpu.VMEM((1, acts), jnp.int32),
            pltpu.SemaphoreType.DMA((2 * layers + 3,)),
        ],
        compiler_params=limit,
        name="edges",
    )(stay(screens), stay(cm), stay(cm_columns.T), stay(held))
    outer = swap(outer, 1)
    inner = swap(inner, -1)

    rows, state, extra = pl.pallas_call(
        mirror_rows,
        in_specs=[smem] + [vmem] * 4,
        out_specs=[hbm, vmem, vmem],
        out_shape=(
            jax.ShapeDtypeStruct((tiles, sums // 4, 4, LANES), f32),
            jax.ShapeDtypeStruct((3 * lines, LANES), f32),
            jax.ShapeDtypeStruct((1, LANES), f32),
        ),
        scratch_shapes=[
            pltpu.VMEM((tiles, sums // 4, 4, LANES), f32),
            pltpu.SemaphoreType.DMA((2,)),
        ],
        compiler_params=tight,
        name="mirror_rows",
    )(dm_gain, held, prev_commands.reshape(1, acts), picks, loaded)
    foot_rows = jnp.transpose(footprint, (1, 2, 0))
    rows, foot_rows = lax.optimization_barrier((rows, foot_rows))
    rows = lax.all_to_all(rows, "tile", 0, 0)

    picked, named = pl.pallas_call(
        lambda *refs: pick_own(*refs, total=total),
        in_specs=[vmem] * 3,
        out_shape=(
            jax.ShapeDtypeStruct((layers, subs, foot * pixels), screens.dtype),
            jax.ShapeDtypeStruct((layers, subs, foot * EDGE), jnp.bfloat16),
        ),
        compiler_params=tight,
        name="pick_own",
    )(foot_rows, screens, inner)
    slopes, words = pl.pallas_call(
        sense_rest,
        in_specs=[vmem] * 6,
        out_shape=(
            jax.ShapeDtypeStruct((2, subs), f32),
            jax.ShapeDtypeStruct((2 * subs // LANES, LANES), f32),
        ),
        compiler_params=limit,
        name="sense_rest",
    )(
        named, outer, interp_weights, picked, illumination, transform_table(SIDE)
    )
    packed = pl.pallas_call(
        lambda *refs: pack(*refs, mirrors=mirrors),
        in_specs=[vmem] * 3,
        out_shape=jax.ShapeDtypeStruct((tiles, 8, LANES), jnp.bfloat16),
        compiler_params=limit,
        name="pack",
    )(words, rows, extra)

    gathered = lax.all_to_all(packed, "tile", 0, 0)
    sent = pl.pallas_call(
        lambda *refs: reconstruct(*refs, rb=rb),
        in_specs=[vmem] * 3,
        out_shape=jax.ShapeDtypeStruct((8, LANES), f32),
        compiler_params=limit,
        name="reconstruct",
    )(gathered, cm, spot)
    got = [sent]
    for far in range(1, groups):
        route = [(g, (g + far) % groups) for g in range(groups)]
        got.append(lax.ppermute(sent, "grp", route))
    return pl.pallas_call(
        lambda *refs: settle(*refs, mirrors=mirrors),
        in_specs=[vmem] * (groups + 2),
        out_shape=(
            jax.ShapeDtypeStruct((2, subs), f32),
            jax.ShapeDtypeStruct((acts,), f32),
        ),
        compiler_params=limit,
        name="settle",
    )(*got, state, slopes)


def solution(mesh):
    in_specs = (
        P(None, ("grp", "tile"), None),
        P(),
        P(("grp", "tile"), None, None),
        P(("grp", "tile"), None),
        P("tile", "grp", None, None, None),
        P("tile", "grp"),
        P("tile"),
        P("tile"),
        P(),
    )
    out_specs = (P(None, ("grp", "tile")), P("tile"))
    return jax.shard_map(
        on_device, mesh=mesh, in_specs=in_specs, out_specs=out_specs, check_vma=False
    )
```

```python
import math

import jax
import jax.numpy as jnp
import numpy as np
from jax import lax
from jax.experimental import pallas as pl
from jax.experimental.pallas import tpu as pltpu
from jax.sharding import PartitionSpec as P


SIDE = 16
DEVICES = ("grp", "tile")
LANES = 128
EDGE = 256


def swap(block, step):
    count = lax.axis_size(DEVICES)
    route = [(i, (i + step if i % 2 else i - step) % count) for i in range(count)]
    return lax.ppermute(block, DEVICES, route)


def transform_table(side):
    index = np.arange(side * side)
    rows, cols = index // side, index % side
    turns = (rows[:, None] * rows[None, :] + cols[:, None] * cols[None, :]) % side
    angle = turns.astype(np.float32) * np.float32(2.0 * math.pi / side)
    cosine, sine = np.cos(angle), np.sin(angle)
    table = np.concatenate(
        [np.concatenate([cosine, -sine], 1), np.concatenate([sine, cosine], 1)], 0
    )
    return jnp.asarray(table.T.astype(jnp.bfloat16))


def sine_cosine(angle):
    turns = jnp.floor(angle * np.float32(2.0 / math.pi) + 0.5)
    rest = angle - turns * np.float32(1.5703125)
    rest = rest - turns * np.float32(4.837512969970703125e-4)
    rest = rest - turns * np.float32(7.54978995489188216e-8)
    sq = rest * rest
    sine = (np.float32(-1.9515295891e-4) * sq + np.float32(8.3321608736e-3)) * sq
    sine = (sine - np.float32(1.6666654611e-1)) * sq * rest + rest
    cosine = (np.float32(2.443315711809948e-5) * sq - np.float32(1.388731625493765e-3)) * sq
    cosine = (cosine + np.float32(4.166664568298827e-2)) * sq * sq - np.float32(0.5) * sq + 1.0
    quarter = turns.astype(jnp.int32)
    odd = (quarter & 1) == 1
    out_sine = jnp.where(odd, cosine, sine)
    out_cosine = jnp.where(odd, sine, cosine)
    out_sine = jnp.where((quarter & 2) == 2, -out_sine, out_sine)
    out_cosine = jnp.where(((quarter + 1) & 2) == 2, -out_cosine, out_cosine)
    return out_sine, out_cosine


def offsets_of(foot_rows, start, total):
    away = foot_rows - start
    away = jnp.where(away < -(total // 2), away + total, away)
    away = jnp.where(away >= total // 2, away - total, away)
    away = away.astype(jnp.float32)
    foot, subs = away.shape
    filled = jnp.concatenate([away, jnp.zeros((8 - foot, subs), jnp.float32)], 0)
    return filled.T.astype(jnp.int32)


def hits(column, first, count):
    column = jnp.broadcast_to(column, (column.shape[0], LANES)).astype(jnp.int16)
    lane = lax.broadcasted_iota(jnp.int16, column.shape, 1)
    one, zero = jnp.bfloat16(1), jnp.bfloat16(0)
    parts = [
        jnp.where(lane == column - jnp.int16(first + b), one, zero)
        for b in range(0, count, LANES)
    ]
    return jnp.concatenate(parts, 1)


def edges(
    screens_ref, matrix_ref, cols_hbm, owner_hbm, outer_ref, inner_ref, cm_ref, picks_ref, spot_ref,
    cols_ref, owner_ref, sems, *, columns, mirrors
):
    layers, blocks, _ = screens_ref.shape
    last = (blocks // EDGE - 1) * EDGE
    odd = lax.axis_index("tile") % 2
    outer = pl.multiple_of(odd * last, EDGE)
    inner = pl.multiple_of((1 - odd) * last, EDGE)
    copies = []
    for first, ref in ((outer, outer_ref), (inner, inner_ref)):
        for layer in range(layers):
            block = screens_ref.at[layer, pl.ds(first, EDGE)]
            copies.append(pltpu.make_async_copy(block, ref.at[layer], sems.at[len(copies)]))
    copies.append(pltpu.make_async_copy(matrix_ref, cm_ref, sems.at[len(copies)]))
    small = [
        pltpu.make_async_copy(cols_hbm, cols_ref, sems.at[len(copies)]),
        pltpu.make_async_copy(owner_hbm, owner_ref, sems.at[len(copies) + 1]),
    ]
    for copy in small + copies:
        copy.start()
    positions, rowblk = cols_ref.shape
    acts = owner_ref.shape[1]
    rb = acts // rowblk
    act = lax.broadcasted_iota(jnp.int32, (acts, LANES), 0)
    wide = lax.broadcasted_iota(jnp.int32, (acts, LANES), 1)
    over = jnp.where(act % rb == (wide % (2 * rb)) // 2, 1.0, 0.0).astype(jnp.bfloat16)
    for copy in small:
        copy.wait()
    cols = (cols_ref[...] - lax.axis_index("grp") * columns).astype(jnp.float32)
    lane = lax.broadcasted_iota(jnp.int32, (positions, LANES), 1)
    place = lax.broadcasted_iota(jnp.int32, (positions, LANES), 0)
    spread = jnp.where(lane // (2 * rb) == place, 1.0, 0.0)
    cols = lax.dot_general(
        cols, spread, (((0,), (0,)), ((), ())), preferred_element_type=jnp.float32
    ).astype(jnp.int32)
    comp = lax.broadcasted_iota(jnp.int32, cols.shape, 1) % 2
    height = spot_ref.shape[0]
    spot_ref[...] = jnp.concatenate(
        [cols * 2 + comp, jnp.full((height - rowblk, LANES), -1, jnp.int32)], 0
    )
    act = lax.broadcasted_iota(jnp.int32, (rowblk, acts), 1)
    block = lax.broadcasted_iota(jnp.int32, (rowblk, acts), 0)
    held = jnp.where(act // rb == block, owner_ref[...], 0)
    held = held.astype(jnp.float32).astype(jnp.bfloat16)
    owners = jnp.dot(held, over, preferred_element_type=jnp.float32)
    target = cols * (2 * mirrors) + comp * mirrors + owners.astype(jnp.int32)
    row = lax.broadcasted_iota(jnp.int16, (picks_ref.shape[0], LANES), 0)
    one, zero = jnp.bfloat16(1), jnp.bfloat16(0)
    for i in range(rowblk):
        named = jnp.broadcast_to(target[i : i + 1, :], row.shape).astype(jnp.int16)
        picks_ref[:, i * LANES : (i + 1) * LANES] = jnp.where(row == named, one, zero)
    for copy in copies:
        copy.wait()


def mirror_rows(
    gain_ref, owner_ref, prev_ref, picks_ref, cm_ref, sent_ref, state_ref, extra_ref, half_ref, sems
):
    tiles, threes, fours, _ = sent_ref.shape
    mirrors = gain_ref.shape[0]
    acts = owner_ref.shape[1]
    half = tiles // 2
    rows = half * threes * fours
    copies = []
    for part in range(2):
        sums = jnp.dot(
            picks_ref[part * rows : (part + 1) * rows, :],
            cm_ref[...],
            preferred_element_type=jnp.float32,
        )
        for t in range(half):
            for j in range(threes):
                at = (t * threes + j) * fours
                half_ref[part * half + t, j] = sums[at : at + fours]
        span = pl.ds(part * half, half)
        copies.append(
            pltpu.make_async_copy(half_ref.at[span], sent_ref.at[span], sems.at[part])
        )
        copies[part].start()
    owner = owner_ref[...]
    lane = lax.broadcasted_iota(jnp.int32, (1, LANES), 1)
    extra = jnp.zeros((1, LANES), jnp.float32)
    gain = jnp.zeros(owner.shape, jnp.float32)
    for m in range(mirrors):
        mine = owner == m
        gain = jnp.where(mine, gain_ref[m], gain)
        prev = jnp.sum(jnp.where(mine, prev_ref[...], 0.0), axis=1, keepdims=True)
        number = jnp.sum(jnp.where(mine, 1.0, 0.0), axis=1, keepdims=True)
        extra = jnp.where(lane == mirrors + m, prev, extra)
        extra = jnp.where(lane == 2 * mirrors + m, number, extra)
    extra_ref[...] = extra
    lines = state_ref.shape[0] // 3
    missing = lines * LANES - acts
    rows = []
    for values, fill in ((owner.astype(jnp.float32), -1.0), (prev_ref[...], 0.0), (gain, 0.0)):
        values = jnp.concatenate([values, jnp.full((1, missing), fill, jnp.float32)], 1)
        rows += [values[:, i * LANES : (i + 1) * LANES] for i in range(lines)]
    state_ref[...] = jnp.concatenate(rows, 0)
    for copy in copies:
        copy.wait()


def pick_own(foot_ref, screens_ref, inner_ref, picked_ref, *, total):
    layers, foot, _ = foot_ref.shape
    blocks, pixels = screens_ref.shape[1:]
    start = lax.axis_index(DEVICES) * blocks
    first = (1 - lax.axis_index("tile") % 2) * (blocks + EDGE) - EDGE
    for layer in range(layers):
        offsets = offsets_of(foot_ref[layer], start, total)
        for k in range(foot):
            column = offsets[:, k : k + 1]
            rows = jnp.dot(
                hits(column, 0, blocks), screens_ref[layer], preferred_element_type=jnp.float32
            )
            rows = rows + jnp.dot(
                hits(column - first, 0, EDGE),
                inner_ref[layer],
                preferred_element_type=jnp.float32,
            )
            picked_ref[layer, :, k * pixels : (k + 1) * pixels] = rows.astype(jnp.bfloat16)


def sense_rest(
    foot_ref, outer_ref, weights_ref, own_ref, illum_ref, table_ref, slopes_ref, words_ref, *,
    total, blocks
):
    layers, foot, subs = foot_ref.shape
    pixels = illum_ref.shape[1]
    start = lax.axis_index(DEVICES) * blocks
    first = (lax.axis_index("tile") % 2) * (blocks + EDGE) - EDGE
    phase = None
    for layer in range(layers):
        offsets = offsets_of(foot_ref[layer], start, total)
        for k in range(foot):
            found = hits(offsets[:, k : k + 1] - first, 0, EDGE)
            rows = jnp.dot(found, outer_ref[layer], preferred_element_type=jnp.float32)
            rows = rows.astype(jnp.bfloat16) + own_ref[layer, :, k * pixels : (k + 1) * pixels]
            part = jnp.dot(rows, weights_ref[layer, k], preferred_element_type=jnp.float32)
            phase = part if phase is None else phase + part
    phase = phase.T
    illum = illum_ref[...].T
    sine, cosine = sine_cosine(phase)
    field = jnp.concatenate([illum * cosine, illum * sine], 0).astype(jnp.bfloat16)
    spectrum = jnp.dot(table_ref[...], field, preferred_element_type=jnp.float32)
    real_part = spectrum[:pixels]
    imag_part = spectrum[pixels:]
    intensity = real_part * real_part + imag_part * imag_part
    row = lax.broadcasted_iota(jnp.int32, intensity.shape, 0)
    cv = row % SIDE
    cu = row // SIDE
    cv = (cv - SIDE * (cv >= SIDE // 2).astype(jnp.int32)).astype(jnp.float32)
    cu = (cu - SIDE * (cu >= SIDE // 2).astype(jnp.int32)).astype(jnp.float32)
    whole = jnp.sum(intensity, axis=0, keepdims=True)
    slope_x = jnp.sum(intensity * cv, axis=0, keepdims=True) / whole
    slope_y = jnp.sum(intensity * cu, axis=0, keepdims=True) / whole
    slopes = jnp.concatenate([slope_x, slope_y], 0)
    slopes_ref[...] = slopes
    words = slopes.astype(jnp.bfloat16).astype(jnp.float32)
    words = [words[:, h * LANES : (h + 1) * LANES] for h in range(subs // LANES)]
    words_ref[...] = jnp.concatenate(words, 0)


def pack(words_ref, rows_ref, extra_ref, sent_ref, *, mirrors):
    words = words_ref[...]
    sums = jnp.sum(rows_ref[...], axis=0)
    lane = lax.broadcasted_iota(jnp.int32, (1, LANES), 1)
    line = extra_ref[...]
    for m in range(mirrors):
        product = jnp.zeros((1, LANES), jnp.float32)
        for k in range(words.shape[0]):
            at = k * mirrors + m
            row = sums[at // sums.shape[1], at % sums.shape[1]][None]
            product = product + row * words[k : k + 1]
        line = jnp.where(lane == m, jnp.sum(product, axis=1, keepdims=True), line)
    high = line.astype(jnp.bfloat16).astype(jnp.float32)
    middle = (line - high).astype(jnp.bfloat16).astype(jnp.float32)
    low = line - high - middle
    rows = jnp.concatenate([words, high, middle, low, jnp.zeros_like(low)], 0)
    sent_ref[...] = jnp.broadcast_to(rows.astype(jnp.bfloat16)[None], sent_ref.shape)


def reconstruct(words_ref, cm_ref, spot_ref, sent_ref, *, rb):
    got = words_ref[...].astype(jnp.float32)
    words = got[:, :4, :].reshape(-1, LANES).astype(jnp.bfloat16)
    line = jnp.sum(got, axis=0)
    line = line[4:5] + line[5:6] + line[6:7]
    rowblk = cm_ref.shape[0] // LANES
    row = lax.broadcasted_iota(jnp.int32, (words.shape[0], LANES), 0)
    parts = []
    step = math.gcd(rowblk, 4)
    for first in range(0, rowblk, step):
        product = lax.dot_general(
            words,
            cm_ref[first * LANES : (first + step) * LANES, :],
            (((1,), (1,)), ((), ())),
            preferred_element_type=jnp.float32,
        )
        for i in range(step):
            spot = spot_ref[first + i : first + i + 1, :]
            chosen = jnp.where(row == spot, product[:, i * LANES : (i + 1) * LANES], 0.0)
            parts.append(jnp.sum(chosen, axis=0, keepdims=True))
    height = spot_ref.shape[0]
    if height > rowblk:
        parts.append(jnp.zeros((height - rowblk, LANES), jnp.float32))
    parts = jnp.concatenate(parts, 0)
    source = lax.broadcasted_iota(jnp.int32, (LANES, LANES), 0)
    lane = lax.broadcasted_iota(jnp.int32, (LANES, LANES), 1)
    fold = jnp.where((source % (2 * rb)) // 2 == lane % rb, 1.0, 0.0)
    spread = jnp.dot(
        parts, fold, preferred_element_type=jnp.float32, precision=lax.Precision.HIGHEST
    )
    per = LANES // rb
    block = lax.broadcasted_iota(jnp.int32, spread.shape, 0)
    lane = lax.broadcasted_iota(jnp.int32, spread.shape, 1)
    spread = jnp.where(lane // rb == block % per, spread, 0.0)
    recon = jnp.sum(spread.reshape(height // per, per, LANES), axis=1)
    rest = sent_ref.shape[0] - recon.shape[0] - 1
    sent_ref[...] = jnp.concatenate([recon, line, jnp.zeros((rest, LANES), jnp.float32)], 0)


def settle(*refs, mirrors):
    *got_refs, state_ref, found_ref, slopes_ref, commands_ref = refs
    slopes_ref[...] = found_ref[...]
    lines = state_ref.shape[0] // 3
    sums = got_refs[0][...]
    for got_ref in got_refs[1:]:
        sums = sums + got_ref[...]
    line = sums[lines : lines + 1]
    share = 1.0 / len(got_refs)
    lane = lax.broadcasted_iota(jnp.int32, line.shape, 1)

    def entry(at):
        return jnp.sum(jnp.where(lane == at, line, 0.0), axis=1, keepdims=True)

    owner = state_ref[:lines]
    gain = state_ref[2 * lines :]
    piston = jnp.zeros(owner.shape, jnp.float32)
    for m in range(mirrors):
        total = share * entry(mirrors + m) - gain * entry(m)
        count = share * entry(2 * mirrors + m)
        piston = jnp.where(owner == float(m), total / count, piston)
    commands = state_ref[lines : 2 * lines] - gain * sums[:lines] - piston
    acts = commands_ref.shape[0]
    for i in range(lines):
        some = min(LANES, acts - i * LANES)
        commands_ref[i * LANES : i * LANES + some] = commands[i, :some]


def on_device(
    screens,
    interp_weights,
    footprint,
    illumination,
    cm_values,
    cm_columns,
    prev_commands,
    owner_map,
    dm_gain,
):
    layers, blk_dev, pixels = screens.shape
    subs, _, foot = footprint.shape
    groups, tiles = lax.axis_size("grp"), lax.axis_size("tile")
    total = blk_dev * groups * tiles
    rowblk, positions, rb, comps, cbs = cm_values.shape
    acts = rowblk * rb
    mirrors = dm_gain.shape[0]
    height = -(-acts // LANES) * LANES // rb
    lines = height * rb // LANES
    smem = pl.BlockSpec(memory_space=pltpu.SMEM)
    vmem = pl.BlockSpec(memory_space=pltpu.VMEM)
    limit = pltpu.CompilerParams(vmem_limit_bytes=24 * 2**20)
    tight = pltpu.CompilerParams(vmem_limit_bytes=24 * 2**20)
    f32 = jnp.float32

    edge = jax.ShapeDtypeStruct((layers, EDGE, pixels), screens.dtype)
    hbm = pl.BlockSpec(memory_space=pltpu.HBM)
    cm = cm_values.reshape(rowblk * positions * rb * comps, cbs)
    held = owner_map.reshape(1, acts)
    sums = 4 * mirrors

    def stay(array):
        return pltpu.with_memory_space_constraint(array, pltpu.HBM)

    outer, inner, loaded, picks, spot = pl.pallas_call(
        lambda *refs: edges(*refs, columns=tiles * subs // cbs, mirrors=mirrors),
        in_specs=[hbm] * 4,
        out_specs=[vmem] * 5,
        out_shape=[
            edge,
            edge,
            jax.ShapeDtypeStruct(cm.shape, cm.dtype),
            jax.ShapeDtypeStruct((tiles * sums, cm.shape[0]), jnp.bfloat16),
            jax.ShapeDtypeStruct((height, LANES), jnp.int32),
        ],
        scratch_shapes=[
            pltpu.VMEM((positions, rowblk), jnp.int32),
            pltpu.VMEM((1, acts), jnp.int32),
            pltpu.SemaphoreType.DMA((2 * layers + 3,)),
        ],
        compiler_params=limit,
        name="edges",
    )(stay(screens), stay(cm), stay(cm_columns.T), stay(held))
    outer = swap(outer, 1)
    inner = swap(inner, -1)

    rows, state, extra = pl.pallas_call(
        mirror_rows,
        in_specs=[smem] + [vmem] * 4,
        out_specs=[hbm, vmem, vmem],
        out_shape=(
            jax.ShapeDtypeStruct((tiles, sums // 4, 4, LANES), f32),
            jax.ShapeDtypeStruct((3 * lines, LANES), f32),
            jax.ShapeDtypeStruct((1, LANES), f32),
        ),
        scratch_shapes=[
            pltpu.VMEM((tiles, sums // 4, 4, LANES), f32),
            pltpu.SemaphoreType.DMA((2,)),
        ],
        compiler_params=tight,
        name="mirror_rows",
    )(dm_gain, held, prev_commands.reshape(1, acts), picks, loaded)
    foot_rows = jnp.transpose(footprint, (1, 2, 0))
    rows, foot_rows = lax.optimization_barrier((rows, foot_rows))
    rows = lax.all_to_all(rows, "tile", 0, 0)

    picked = pl.pallas_call(
        lambda *refs: pick_own(*refs, total=total),
        in_specs=[vmem] * 3,
        out_shape=jax.ShapeDtypeStruct((layers, subs, foot * pixels), screens.dtype),
        compiler_params=tight,
        name="pick_own",
    )(foot_rows, screens, inner)
    slopes, words = pl.pallas_call(
        lambda *refs: sense_rest(*refs, total=total, blocks=blk_dev),
        in_specs=[vmem] * 6,
        out_shape=(
            jax.ShapeDtypeStruct((2, subs), f32),
            jax.ShapeDtypeStruct((2 * subs // LANES, LANES), f32),
        ),
        compiler_params=limit,
        name="sense_rest",
    )(
        foot_rows, outer, interp_weights, picked, illumination, transform_table(SIDE)
    )
    packed = pl.pallas_call(
        lambda *refs: pack(*refs, mirrors=mirrors),
        in_specs=[vmem] * 3,
        out_shape=jax.ShapeDtypeStruct((tiles, 8, LANES), jnp.bfloat16),
        compiler_params=limit,
        name="pack",
    )(words, rows, extra)

    gathered = lax.all_to_all(packed, "tile", 0, 0)
    sent = pl.pallas_call(
        lambda *refs: reconstruct(*refs, rb=rb),
        in_specs=[vmem] * 3,
        out_shape=jax.ShapeDtypeStruct((8, LANES), f32),
        compiler_params=limit,
        name="reconstruct",
    )(gathered, cm, spot)
    got = [sent]
    for far in range(1, groups):
        route = [(g, (g + far) % groups) for g in range(groups)]
        got.append(lax.ppermute(sent, "grp", route))
    return pl.pallas_call(
        lambda *refs: settle(*refs, mirrors=mirrors),
        in_specs=[vmem] * (groups + 2),
        out_shape=(
            jax.ShapeDtypeStruct((2, subs), f32),
            jax.ShapeDtypeStruct((acts,), f32),
        ),
        compiler_params=limit,
        name="settle",
    )(*got, state, slopes)


def solution(mesh):
    in_specs = (
        P(None, ("grp", "tile"), None),
        P(),
        P(("grp", "tile"), None, None),
        P(("grp", "tile"), None),
        P("tile", "grp", None, None, None),
        P("tile", "grp"),
        P("tile"),
        P("tile"),
        P(),
    )
    out_specs = (P(None, ("grp", "tile")), P("tile"))
    return jax.shard_map(
        on_device, mesh=mesh, in_specs=in_specs, out_specs=out_specs, check_vma=False
    )
```

```python
import math

import jax
import jax.numpy as jnp
import numpy as np
from jax import lax
from jax.experimental import pallas as pl
from jax.experimental.pallas import tpu as pltpu
from jax.sharding import PartitionSpec as P


SIDE = 16
DEVICES = ("grp", "tile")
LANES = 128
EDGE = 256


def swap(block, step):
    count = lax.axis_size(DEVICES)
    route = [(i, (i + step if i % 2 else i - step) % count) for i in range(count)]
    return lax.ppermute(block, DEVICES, route)


def transform_table(side):
    index = np.arange(side * side)
    rows, cols = index // side, index % side
    turns = (rows[:, None] * rows[None, :] + cols[:, None] * cols[None, :]) % side
    angle = turns.astype(np.float32) * np.float32(2.0 * math.pi / side)
    cosine, sine = np.cos(angle), np.sin(angle)
    table = np.concatenate(
        [np.concatenate([cosine, -sine], 1), np.concatenate([sine, cosine], 1)], 0
    )
    return jnp.asarray(table.T.astype(jnp.bfloat16))


def sine_cosine(angle):
    turns = jnp.floor(angle * np.float32(2.0 / math.pi) + 0.5)
    rest = angle - turns * np.float32(1.5703125)
    rest = rest - turns * np.float32(4.837512969970703125e-4)
    rest = rest - turns * np.float32(7.54978995489188216e-8)
    sq = rest * rest
    sine = (np.float32(-1.9515295891e-4) * sq + np.float32(8.3321608736e-3)) * sq
    sine = (sine - np.float32(1.6666654611e-1)) * sq * rest + rest
    cosine = (np.float32(2.443315711809948e-5) * sq - np.float32(1.388731625493765e-3)) * sq
    cosine = (cosine + np.float32(4.166664568298827e-2)) * sq * sq - np.float32(0.5) * sq + 1.0
    quarter = turns.astype(jnp.int32)
    odd = (quarter & 1) == 1
    out_sine = jnp.where(odd, cosine, sine)
    out_cosine = jnp.where(odd, sine, cosine)
    out_sine = jnp.where((quarter & 2) == 2, -out_sine, out_sine)
    out_cosine = jnp.where(((quarter + 1) & 2) == 2, -out_cosine, out_cosine)
    return out_sine, out_cosine


def offsets_of(foot_rows, start, total):
    away = foot_rows - start
    away = jnp.where(away < -(total // 2), away + total, away)
    away = jnp.where(away >= total // 2, away - total, away)
    away = away.astype(jnp.float32)
    foot, subs = away.shape
    filled = jnp.concatenate([away, jnp.zeros((8 - foot, subs), jnp.float32)], 0)
    return filled.T.astype(jnp.int32)


def hits(column, first, count):
    column = jnp.broadcast_to(column, (column.shape[0], LANES)).astype(jnp.int16)
    lane = lax.broadcasted_iota(jnp.int16, column.shape, 1)
    one, zero = jnp.bfloat16(1), jnp.bfloat16(0)
    parts = [
        jnp.where(lane == column - jnp.int16(first + b), one, zero)
        for b in range(0, count, LANES)
    ]
    return jnp.concatenate(parts, 1)


def edges(
    screens_ref, matrix_ref, cols_hbm, owner_hbm, outer_ref, inner_ref, cm_ref, picks_ref, spot_ref,
    cols_ref, owner_ref, sems, *, columns, mirrors
):
    layers, blocks, _ = screens_ref.shape
    last = (blocks // EDGE - 1) * EDGE
    odd = lax.axis_index("tile") % 2
    outer = pl.multiple_of(odd * last, EDGE)
    inner = pl.multiple_of((1 - odd) * last, EDGE)
    copies = []
    for first, ref in ((outer, outer_ref), (inner, inner_ref)):
        for layer in range(layers):
            block = screens_ref.at[layer, pl.ds(first, EDGE)]
            copies.append(pltpu.make_async_copy(block, ref.at[layer], sems.at[len(copies)]))
    copies.append(pltpu.make_async_copy(matrix_ref, cm_ref, sems.at[len(copies)]))
    small = [
        pltpu.make_async_copy(cols_hbm, cols_ref, sems.at[len(copies)]),
        pltpu.make_async_copy(owner_hbm, owner_ref, sems.at[len(copies) + 1]),
    ]
    for copy in small + copies:
        copy.start()
    positions, rowblk = cols_ref.shape
    acts = owner_ref.shape[1]
    rb = acts // rowblk
    act = lax.broadcasted_iota(jnp.int32, (acts, LANES), 0)
    wide = lax.broadcasted_iota(jnp.int32, (acts, LANES), 1)
    over = jnp.where(act % rb == (wide % (2 * rb)) // 2, 1.0, 0.0).astype(jnp.bfloat16)
    for copy in small:
        copy.wait()
    cols = (cols_ref[...] - lax.axis_index("grp") * columns).astype(jnp.float32)
    lane = lax.broadcasted_iota(jnp.int32, (positions, LANES), 1)
    place = lax.broadcasted_iota(jnp.int32, (positions, LANES), 0)
    spread = jnp.where(lane // (2 * rb) == place, 1.0, 0.0)
    cols = lax.dot_general(
        cols, spread, (((0,), (0,)), ((), ())), preferred_element_type=jnp.float32
    ).astype(jnp.int32)
    comp = lax.broadcasted_iota(jnp.int32, cols.shape, 1) % 2
    height = spot_ref.shape[0]
    spot_ref[...] = jnp.concatenate(
        [cols * 2 + comp, jnp.full((height - rowblk, LANES), -1, jnp.int32)], 0
    )
    act = lax.broadcasted_iota(jnp.int32, (rowblk, acts), 1)
    block = lax.broadcasted_iota(jnp.int32, (rowblk, acts), 0)
    held = jnp.where(act // rb == block, owner_ref[...], 0)
    held = held.astype(jnp.float32).astype(jnp.bfloat16)
    owners = jnp.dot(held, over, preferred_element_type=jnp.float32)
    target = cols * (2 * mirrors) + comp * mirrors + owners.astype(jnp.int32)
    row = lax.broadcasted_iota(jnp.int16, (picks_ref.shape[0], LANES), 0)
    one, zero = jnp.bfloat16(1), jnp.bfloat16(0)
    for i in range(rowblk):
        named = jnp.broadcast_to(target[i : i + 1, :], row.shape).astype(jnp.int16)
        picks_ref[:, i * LANES : (i + 1) * LANES] = jnp.where(row == named, one, zero)
    for copy in copies:
        copy.wait()


def mirror_rows(
    gain_ref, owner_ref, prev_ref, picks_ref, cm_ref, sent_ref, state_ref, extra_ref, half_ref, sems
):
    tiles, threes, fours, _ = sent_ref.shape
    mirrors = gain_ref.shape[0]
    acts = owner_ref.shape[1]
    half = tiles // 2
    rows = half * threes * fours
    copies = []
    for part in range(2):
        sums = jnp.dot(
            picks_ref[part * rows : (part + 1) * rows, :],
            cm_ref[...],
            preferred_element_type=jnp.float32,
        )
        for t in range(half):
            for j in range(threes):
                at = (t * threes + j) * fours
                half_ref[part * half + t, j] = sums[at : at + fours]
        span = pl.ds(part * half, half)
        copies.append(
            pltpu.make_async_copy(half_ref.at[span], sent_ref.at[span], sems.at[part])
        )
        copies[part].start()
    owner = owner_ref[...]
    lane = lax.broadcasted_iota(jnp.int32, (1, LANES), 1)
    extra = jnp.zeros((1, LANES), jnp.float32)
    gain = jnp.zeros(owner.shape, jnp.float32)
    for m in range(mirrors):
        mine = owner == m
        gain = jnp.where(mine, gain_ref[m], gain)
        prev = jnp.sum(jnp.where(mine, prev_ref[...], 0.0), axis=1, keepdims=True)
        number = jnp.sum(jnp.where(mine, 1.0, 0.0), axis=1, keepdims=True)
        extra = jnp.where(lane == mirrors + m, prev, extra)
        extra = jnp.where(lane == 2 * mirrors + m, number, extra)
    extra_ref[...] = extra
    lines = state_ref.shape[0] // 3
    missing = lines * LANES - acts
    rows = []
    for values, fill in ((owner.astype(jnp.float32), -1.0), (prev_ref[...], 0.0), (gain, 0.0)):
        values = jnp.concatenate([values, jnp.full((1, missing), fill, jnp.float32)], 1)
        rows += [values[:, i * LANES : (i + 1) * LANES] for i in range(lines)]
    state_ref[...] = jnp.concatenate(rows, 0)
    for copy in copies:
        copy.wait()


def pick_own(foot_ref, screens_ref, inner_ref, picked_ref, *, total):
    layers, foot, _ = foot_ref.shape
    blocks, pixels = screens_ref.shape[1:]
    start = lax.axis_index(DEVICES) * blocks
    first = (1 - lax.axis_index("tile") % 2) * (blocks + EDGE) - EDGE
    for layer in range(layers):
        offsets = offsets_of(foot_ref[layer], start, total)
        for k in range(foot):
            column = offsets[:, k : k + 1]
            rows = jnp.dot(
                hits(column, 0, blocks), screens_ref[layer], preferred_element_type=jnp.float32
            )
            rows = rows + jnp.dot(
                hits(column - first, 0, EDGE),
                inner_ref[layer],
                preferred_element_type=jnp.float32,
            )
            picked_ref[layer, :, k * pixels : (k + 1) * pixels] = rows.astype(jnp.bfloat16)


def sense_rest(
    foot_ref, outer_ref, weights_ref, own_ref, illum_ref, table_ref, slopes_ref, words_ref, *,
    total, blocks
):
    layers, foot, subs = foot_ref.shape
    pixels = illum_ref.shape[1]
    start = lax.axis_index(DEVICES) * blocks
    first = (lax.axis_index("tile") % 2) * (blocks + EDGE) - EDGE
    phase = None
    for layer in range(layers):
        offsets = offsets_of(foot_ref[layer], start, total)
        for k in range(foot):
            found = hits(offsets[:, k : k + 1] - first, 0, EDGE)
            rows = jnp.dot(found, outer_ref[layer], preferred_element_type=jnp.float32)
            rows = rows.astype(jnp.bfloat16) + own_ref[layer, :, k * pixels : (k + 1) * pixels]
            part = jnp.dot(rows, weights_ref[layer, k], preferred_element_type=jnp.float32)
            phase = part if phase is None else phase + part
    phase = phase.T
    illum = illum_ref[...].T
    sine, cosine = sine_cosine(phase)
    field = jnp.concatenate([illum * cosine, illum * sine], 0).astype(jnp.bfloat16)
    spectrum = jnp.dot(table_ref[...], field, preferred_element_type=jnp.float32)
    real_part = spectrum[:pixels]
    imag_part = spectrum[pixels:]
    intensity = real_part * real_part + imag_part * imag_part
    row = lax.broadcasted_iota(jnp.int32, intensity.shape, 0)
    cv = row % SIDE
    cu = row // SIDE
    cv = (cv - SIDE * (cv >= SIDE // 2).astype(jnp.int32)).astype(jnp.float32)
    cu = (cu - SIDE * (cu >= SIDE // 2).astype(jnp.int32)).astype(jnp.float32)
    whole = jnp.sum(intensity, axis=0, keepdims=True)
    slope_x = jnp.sum(intensity * cv, axis=0, keepdims=True) / whole
    slope_y = jnp.sum(intensity * cu, axis=0, keepdims=True) / whole
    slopes = jnp.concatenate([slope_x, slope_y], 0)
    slopes_ref[...] = slopes
    words = slopes.astype(jnp.bfloat16).astype(jnp.float32)
    words = [words[:, h * LANES : (h + 1) * LANES] for h in range(subs // LANES)]
    words_ref[...] = jnp.concatenate(words, 0)


def pack(words_ref, rows_ref, extra_ref, sent_ref, *, mirrors):
    words = words_ref[...]
    sums = jnp.sum(rows_ref[...], axis=0)
    lane = lax.broadcasted_iota(jnp.int32, (1, LANES), 1)
    line = extra_ref[...]
    for m in range(mirrors):
        product = jnp.zeros((1, LANES), jnp.float32)
        for k in range(words.shape[0]):
            at = k * mirrors + m
            row = sums[at // sums.shape[1], at % sums.shape[1]][None]
            product = product + row * words[k : k + 1]
        line = jnp.where(lane == m, jnp.sum(product, axis=1, keepdims=True), line)
    high = line.astype(jnp.bfloat16).astype(jnp.float32)
    middle = (line - high).astype(jnp.bfloat16).astype(jnp.float32)
    low = line - high - middle
    rows = jnp.concatenate([words, high, middle, low, jnp.zeros_like(low)], 0)
    sent_ref[...] = jnp.broadcast_to(rows.astype(jnp.bfloat16)[None], sent_ref.shape)


def reconstruct(words_ref, cm_ref, spot_ref, sent_ref, *, rb):
    got = words_ref[...].astype(jnp.float32)
    words = got[:, :4, :].reshape(-1, LANES).astype(jnp.bfloat16)
    line = jnp.sum(got, axis=0)
    line = line[4:5] + line[5:6] + line[6:7]
    rowblk = cm_ref.shape[0] // LANES
    row = lax.broadcasted_iota(jnp.int32, (words.shape[0], LANES), 0)
    parts = []
    step = math.gcd(rowblk, 4)
    for first in range(0, rowblk, step):
        product = lax.dot_general(
            words,
            cm_ref[first * LANES : (first + step) * LANES, :],
            (((1,), (1,)), ((), ())),
            preferred_element_type=jnp.float32,
        )
        for i in range(step):
            spot = spot_ref[first + i : first + i + 1, :]
            chosen = jnp.where(row == spot, product[:, i * LANES : (i + 1) * LANES], 0.0)
            parts.append(jnp.sum(chosen, axis=0, keepdims=True))
    height = spot_ref.shape[0]
    if height > rowblk:
        parts.append(jnp.zeros((height - rowblk, LANES), jnp.float32))
    parts = jnp.concatenate(parts, 0)
    source = lax.broadcasted_iota(jnp.int32, (LANES, LANES), 0)
    lane = lax.broadcasted_iota(jnp.int32, (LANES, LANES), 1)
    fold = jnp.where((source % (2 * rb)) // 2 == lane % rb, 1.0, 0.0)
    spread = jnp.dot(
        parts, fold, preferred_element_type=jnp.float32, precision=lax.Precision.HIGHEST
    )
    per = LANES // rb
    block = lax.broadcasted_iota(jnp.int32, spread.shape, 0)
    lane = lax.broadcasted_iota(jnp.int32, spread.shape, 1)
    spread = jnp.where(lane // rb == block % per, spread, 0.0)
    recon = jnp.sum(spread.reshape(height // per, per, LANES), axis=1)
    rest = sent_ref.shape[0] - recon.shape[0] - 1
    sent_ref[...] = jnp.concatenate([recon, line, jnp.zeros((rest, LANES), jnp.float32)], 0)


def settle(*refs, mirrors):
    *got_refs, state_ref, found_ref, slopes_ref, commands_ref = refs
    slopes_ref[...] = found_ref[...]
    lines = state_ref.shape[0] // 3
    sums = got_refs[0][...]
    for got_ref in got_refs[1:]:
        sums = sums + got_ref[...]
    line = sums[lines : lines + 1]
    share = 1.0 / len(got_refs)
    lane = lax.broadcasted_iota(jnp.int32, line.shape, 1)

    def entry(at):
        return jnp.sum(jnp.where(lane == at, line, 0.0), axis=1, keepdims=True)

    owner = state_ref[:lines]
    gain = state_ref[2 * lines :]
    piston = jnp.zeros(owner.shape, jnp.float32)
    for m in range(mirrors):
        total = share * entry(mirrors + m) - gain * entry(m)
        count = share * entry(2 * mirrors + m)
        piston = jnp.where(owner == float(m), total / count, piston)
    commands = state_ref[lines : 2 * lines] - gain * sums[:lines] - piston
    acts = commands_ref.shape[0]
    for i in range(lines):
        some = min(LANES, acts - i * LANES)
        commands_ref[i * LANES : i * LANES + some] = commands[i, :some]


def on_device(
    screens,
    interp_weights,
    footprint,
    illumination,
    cm_values,
    cm_columns,
    prev_commands,
    owner_map,
    dm_gain,
):
    layers, blk_dev, pixels = screens.shape
    subs, _, foot = footprint.shape
    groups, tiles = lax.axis_size("grp"), lax.axis_size("tile")
    total = blk_dev * groups * tiles
    rowblk, positions, rb, comps, cbs = cm_values.shape
    acts = rowblk * rb
    mirrors = dm_gain.shape[0]
    height = -(-acts // LANES) * LANES // rb
    lines = height * rb // LANES
    smem = pl.BlockSpec(memory_space=pltpu.SMEM)
    vmem = pl.BlockSpec(memory_space=pltpu.VMEM)
    limit = pltpu.CompilerParams(vmem_limit_bytes=24 * 2**20)
    tight = pltpu.CompilerParams(vmem_limit_bytes=24 * 2**20)
    f32 = jnp.float32

    edge = jax.ShapeDtypeStruct((layers, EDGE, pixels), screens.dtype)
    hbm = pl.BlockSpec(memory_space=pltpu.HBM)
    cm = cm_values.reshape(rowblk * positions * rb * comps, cbs)
    held = owner_map.reshape(1, acts)
    sums = 4 * mirrors

    def stay(array):
        return pltpu.with_memory_space_constraint(array, pltpu.HBM)

    outer, inner, loaded, picks, spot = pl.pallas_call(
        lambda *refs: edges(*refs, columns=tiles * subs // cbs, mirrors=mirrors),
        in_specs=[hbm] * 4,
        out_specs=[vmem] * 5,
        out_shape=[
            edge,
            edge,
            jax.ShapeDtypeStruct(cm.shape, cm.dtype),
            jax.ShapeDtypeStruct((tiles * sums, cm.shape[0]), jnp.bfloat16),
            jax.ShapeDtypeStruct((height, LANES), jnp.int32),
        ],
        scratch_shapes=[
            pltpu.VMEM((positions, rowblk), jnp.int32),
            pltpu.VMEM((1, acts), jnp.int32),
            pltpu.SemaphoreType.DMA((2 * layers + 3,)),
        ],
        compiler_params=tight,
        name="edges",
    )(stay(screens), stay(cm), stay(cm_columns.T), stay(held))
    outer = swap(outer, 1)
    inner = swap(inner, -1)

    rows, state, extra = pl.pallas_call(
        mirror_rows,
        in_specs=[smem] + [vmem] * 4,
        out_specs=[hbm, vmem, vmem],
        out_shape=(
            jax.ShapeDtypeStruct((tiles, sums // 4, 4, LANES), f32),
            jax.ShapeDtypeStruct((3 * lines, LANES), f32),
            jax.ShapeDtypeStruct((1, LANES), f32),
        ),
        scratch_shapes=[
            pltpu.VMEM((tiles, sums // 4, 4, LANES), f32),
            pltpu.SemaphoreType.DMA((2,)),
        ],
        compiler_params=tight,
        name="mirror_rows",
    )(dm_gain, held, prev_commands.reshape(1, acts), picks, loaded)
    foot_rows = jnp.transpose(footprint, (1, 2, 0))
    rows, foot_rows = lax.optimization_barrier((rows, foot_rows))
    rows = lax.all_to_all(rows, "tile", 0, 0)

    picked = pl.pallas_call(
        lambda *refs: pick_own(*refs, total=total),
        in_specs=[vmem] * 3,
        out_shape=jax.ShapeDtypeStruct((layers, subs, foot * pixels), screens.dtype),
        compiler_params=tight,
        name="pick_own",
    )(foot_rows, screens, inner)
    slopes, words = pl.pallas_call(
        lambda *refs: sense_rest(*refs, total=total, blocks=blk_dev),
        in_specs=[vmem] * 6,
        out_shape=(
            jax.ShapeDtypeStruct((2, subs), f32),
            jax.ShapeDtypeStruct((2 * subs // LANES, LANES), f32),
        ),
        compiler_params=tight,
        name="sense_rest",
    )(
        foot_rows, outer, interp_weights, picked, illumination, transform_table(SIDE)
    )
    packed = pl.pallas_call(
        lambda *refs: pack(*refs, mirrors=mirrors),
        in_specs=[vmem] * 3,
        out_shape=jax.ShapeDtypeStruct((tiles, 8, LANES), jnp.bfloat16),
        compiler_params=tight,
        name="pack",
    )(words, rows, extra)

    gathered = lax.all_to_all(packed, "tile", 0, 0)
    sent = pl.pallas_call(
        lambda *refs: reconstruct(*refs, rb=rb),
        in_specs=[vmem] * 3,
        out_shape=jax.ShapeDtypeStruct((8, LANES), f32),
        compiler_params=tight,
        name="reconstruct",
    )(gathered, cm, spot)
    got = [sent]
    for far in range(1, groups):
        route = [(g, (g + far) % groups) for g in range(groups)]
        got.append(lax.ppermute(sent, "grp", route))
    return pl.pallas_call(
        lambda *refs: settle(*refs, mirrors=mirrors),
        in_specs=[vmem] * (groups + 2),
        out_shape=(
            jax.ShapeDtypeStruct((2, subs), f32),
            jax.ShapeDtypeStruct((acts,), f32),
        ),
        compiler_params=tight,
        name="settle",
    )(*got, state, slopes)


def solution(mesh):
    in_specs = (
        P(None, ("grp", "tile"), None),
        P(),
        P(("grp", "tile"), None, None),
        P(("grp", "tile"), None),
        P("tile", "grp", None, None, None),
        P("tile", "grp"),
        P("tile"),
        P("tile"),
        P(),
    )
    out_specs = (P(None, ("grp", "tile")), P("tile"))
    return jax.shard_map(
        on_device, mesh=mesh, in_specs=in_specs, out_specs=out_specs, check_vma=False
    )
```
